256 devices in a mesh: space: 8 (over x, core), dir: 32 (over z, y).
Axes of the slice: x: 4, y: 4, z: 8, core: 2. Of those that a mesh axis runs over, the one named last changes fastest.
Arguments:
- phonon_heat_density: float32 [128, 40, 16, 4, 256], P('dir', None, 'space'), may hold values from 0.01 to 20, as said below
- directions: float32 [3, 128], replicated, may hold values from -1 to 1, as said below
- quad_weight: float32 [128], replicated, may hold values from 0 to 1, as said below
- mirror: int32 [3, 128], replicated, may hold values from 0 to 127, as said below
- band_courant: float32 [40], replicated, may hold values from 0.3 to 1.9
- relax_rate: float32 [40], replicated, may hold values from 0.05 to 0.95
- mode_heat_magnitude: float32 [40], replicated, may hold values from 0.5 to 2
- mode_pulsation: float32 [40], replicated, may hold values from 0.3 to 2.5
- wall_blocks: int32 [8, 16], P('space'), may hold values from 0 to 15, as said below
- wall_count: int32 [8], P('space'), may hold values from 0 to 16, as said below
- wall_facet: int32 [8, 16, 128], P('space'), may hold values from 0 to 6, as said below
Outputs:
- energy_out: float32 [128, 40, 16, 4, 256], P('dir', None, 'space')
- pseudo_kelvin_field: float32 [16, 4, 256], P('space')
The draws below stay inside these ranges and needn't reach their ends.
Inputs may be any that keep to these rules, and one draw needn't show every extreme that they name: Unit vectors with no zero component; negating any one component of a direction gives another of the directions. `quad_weight`: Positive, summing to 1, equal for directions that differ only in the signs of components. mirror[a, d] is the direction whose vector is that of d with component a negated. `phonon_heat_density`: Positive. `wall_blocks`: the entries of each row are distinct blocks of the tile; the first wall_count[t] of them are its wall blocks. `wall_count`: tiles t and t + 4 hold at most 16 wall blocks together; some pair holds exactly that, with one of its tiles at 16. `wall_facet`: 0 marks a cell that is no wall, and every cell of slots from wall_count[t] on; f from 1 to 6 names the facet normal along axis (f - 1) // 2, positive for odd f and negative for even f.
All inputs are finite; a program needn't handle non-finite values.
Results may differ from the reference program's by a relative error of at most 0.0003.
Values sent between devices are 32-bit elements; how exact they have to be, the bound alone decides.
No kernel may reach another device: no remote copies, remote signals or barrier semaphores. Data moves between devices by JAX's collectives and lax.ppermute only.
A program may use at most 64 MiB of HBM per device.

```python
import math
import jax
import jax.numpy as jnp
from jax import lax

BANDS = 40
DIRS = 128
NBASE = 16
MESH_DEEP_COUNT = 256
LAYER_HIGH_COUNT = 4
STEPS = 2
NEWTON = 4
BLOCK = 128
WPAIR = 8
WMAX = 16
TILES = 8
MESH_WIDE_COUNT = 16
TILE_BLOCKS = 16


def direction_set(key):
    base_key = jax.random.fold_in(key, 101)
    first_key, second_key, third_key = jax.random.split(base_key, 3)
    cosine = jax.random.uniform(first_key, (NBASE,), jnp.float32, 0.15, 0.95)
    azimuth = jax.random.uniform(second_key, (NBASE,), jnp.float32, 0.15, 1.42)
    radial = jnp.sqrt(1.0 - cosine * cosine)
    base_vectors = jnp.stack([radial * jnp.cos(azimuth), radial * jnp.sin(azimuth), cosine])
    base_weight = jnp.exp(jax.random.uniform(third_key, (NBASE,), jnp.float32, jnp.log(0.3), jnp.log(3.0)))
    ordering = jax.random.permutation(jax.random.fold_in(key, 102), DIRS).astype(jnp.int32)
    octant = ordering // NBASE
    member = ordering % NBASE
    return (base_vectors, base_weight, ordering, octant, member)


def octant_bit(octant, axis_num):
    return octant // 2 ** axis_num % 2


def draw_directions(key, part):
    base_vectors, base_weight, ordering, octant, member = direction_set(key)
    rows = []
    for axis_num in range(3):
        signs = (1 - 2 * octant_bit(octant, axis_num)).astype(jnp.float32)
        rows.append(signs * base_vectors[axis_num][member])
    return jnp.stack(rows).astype(jnp.float32)


def draw_quad_weight(key, part):
    base_vectors, base_weight, ordering, octant, member = direction_set(key)
    return (base_weight[member] / (8.0 * jnp.sum(base_weight))).astype(jnp.float32)


def draw_mirror(key, part):
    base_vectors, base_weight, ordering, octant, member = direction_set(key)
    inverse = jnp.argsort(ordering).astype(jnp.int32)
    rows = []
    for axis_num in range(3):
        flipped = octant + (1 - 2 * octant_bit(octant, axis_num)) * 2 ** axis_num
        rows.append(inverse[flipped * NBASE + member])
    return jnp.stack(rows).astype(jnp.int32)


def draw_phonon_heat_density(key, part):
    cell_key, entry_key = jax.random.split(jax.random.fold_in(key, 1), 2)
    full_shape = (DIRS, BANDS, MESH_WIDE_COUNT, LAYER_HIGH_COUNT, MESH_DEEP_COUNT)
    scale = jnp.exp(jax.random.uniform(cell_key, (MESH_WIDE_COUNT, LAYER_HIGH_COUNT, MESH_DEEP_COUNT), jnp.float32, jnp.log(0.2), jnp.log(5.0)))
    factor = jnp.exp(jax.random.uniform(entry_key, full_shape, jnp.float32, jnp.log(0.2), jnp.log(2.0)))
    return (factor * scale[None, None]).astype(jnp.float32)


def wall_layout(key):
    layout_key = jax.random.fold_in(key, 201)
    block_key, count_key, facet_key = jax.random.split(layout_key, 3)
    tile_keys = jax.random.split(block_key, TILES)

    def pick_blocks(one_key):
        return jax.random.permutation(one_key, TILE_BLOCKS)[:WMAX]
    blocks = jax.vmap(pick_blocks)(tile_keys).astype(jnp.int32)
    half_tiles = TILES // 2
    large_key, small_key, force_key, flip_key = jax.random.split(count_key, 4)
    larger = jax.random.randint(large_key, (half_tiles,), WPAIR, WMAX + 1)
    forced = jax.random.randint(force_key, (), 0, half_tiles)
    larger = jnp.where(jnp.arange(half_tiles) == forced, WMAX, larger)
    smaller = jax.random.randint(small_key, (half_tiles,), 0, WMAX - larger + 1)
    flips = jax.random.randint(flip_key, (half_tiles,), 0, 2)
    first_half = jnp.where(flips == 1, larger, smaller)
    second_half = jnp.where(flips == 1, smaller, larger)
    counts = jnp.concatenate([first_half, second_half]).astype(jnp.int32)
    facets = jax.random.randint(facet_key, (TILES, WMAX, BLOCK), 0, 7)
    slot_ids = jnp.arange(WMAX, dtype=jnp.int32)
    facets = jnp.where(slot_ids[None, :, None] < counts[:, None, None], facets, 0).astype(jnp.int32)
    return (blocks, counts, facets)


def draw_wall_blocks(key, part):
    return wall_layout(key)[0]


def draw_wall_count(key, part):
    return wall_layout(key)[1]


def draw_wall_facet(key, part):
    return wall_layout(key)[2]


def setup_inputs(seed: int = 0) -> dict:
    arg_keys = jax.random.split(jax.random.key(seed), 12)
    return {
        "phonon_heat_density": draw_phonon_heat_density(jax.random.fold_in(arg_keys[11], 71), 0),
        "directions": draw_directions(jax.random.fold_in(arg_keys[11], 71), 0),
        "quad_weight": draw_quad_weight(jax.random.fold_in(arg_keys[11], 71), 0),
        "mirror": draw_mirror(jax.random.fold_in(arg_keys[11], 71), 0),
        "band_courant": jnp.clip(jax.random.uniform(arg_keys[4], (BANDS,), jnp.float32, 0.3, 1.9), 0.3, 1.9),
        "relax_rate": jnp.clip(jnp.exp(jax.random.uniform(arg_keys[5], (BANDS,), jnp.float32, math.log(0.05), math.log(0.95))), 0.05, 0.95),
        "mode_heat_magnitude": jnp.clip(jnp.exp(jax.random.uniform(arg_keys[6], (BANDS,), jnp.float32, math.log(0.5), math.log(2.0))), 0.5, 2.0),
        "mode_pulsation": jnp.clip(jnp.exp(jax.random.uniform(arg_keys[7], (BANDS,), jnp.float32, math.log(0.3), math.log(2.5))), 0.3, 2.5),
        "wall_blocks": draw_wall_blocks(jax.random.fold_in(arg_keys[11], 71), 0),
        "wall_count": draw_wall_count(jax.random.fold_in(arg_keys[11], 71), 0),
        "wall_facet": draw_wall_facet(jax.random.fold_in(arg_keys[11], 71), 0),
    }


def beam_coeffs(courant):
    abs_speed = jnp.abs(courant)
    centre = 1.0 - 1.5 * abs_speed + 0.5 * abs_speed * abs_speed
    near_weight = 2.0 * abs_speed - abs_speed * abs_speed
    far_weight = 0.5 * abs_speed * abs_speed - 0.5 * abs_speed
    forward = courant > 0
    return (centre, jnp.where(forward, near_weight, 0.0), jnp.where(forward, far_weight, 0.0),
            jnp.where(forward, 0.0, near_weight), jnp.where(forward, 0.0, far_weight))


def combine(coeffs, centre_field, back_one, back_two, fore_one, fore_two):
    return (coeffs[0] * centre_field + coeffs[1] * back_one + coeffs[2] * back_two
            + coeffs[3] * fore_one + coeffs[4] * fore_two)


def roll_sweep(field_in, coeffs, axis_num):
    return combine(coeffs, field_in, jnp.roll(field_in, 1, axis_num), jnp.roll(field_in, 2, axis_num),
                   jnp.roll(field_in, -1, axis_num), jnp.roll(field_in, -2, axis_num))


def root_finder_guess(injection_contribution, collision_speed_factor, mode_pulsation):
    pseudo_kelvin_field = jnp.ones_like(injection_contribution)
    for newton_turn in range(NEWTON):
        dimensionless_pulsation = mode_pulsation[:, None] / pseudo_kelvin_field[None, :]
        heat_surplus = jnp.expm1(dimensionless_pulsation)
        mismatch_error = jnp.sum(collision_speed_factor[:, None] / heat_surplus, axis=0) - injection_contribution
        gradient_guess = jnp.sum(collision_speed_factor[:, None] * dimensionless_pulsation * jnp.exp(dimensionless_pulsation) / (heat_surplus * heat_surplus), axis=0) / pseudo_kelvin_field
        pseudo_kelvin_field = jnp.clip(pseudo_kelvin_field - mismatch_error / gradient_guess, 0.5 * pseudo_kelvin_field, 2.0 * pseudo_kelvin_field)
    return pseudo_kelvin_field


def reflect_walls(phonon_heat_density, directions, mirror, wall_blocks, wall_count, wall_facet):
    grid_view = phonon_heat_density.reshape(DIRS, BANDS, TILES, TILE_BLOCKS, BLOCK)
    tile_ids = jnp.arange(TILES, dtype=jnp.int32)[:, None]
    walls = grid_view[:, :, tile_ids, wall_blocks]
    slot_ids = jnp.arange(WMAX, dtype=jnp.int32)
    facets = jnp.where(slot_ids[None, :, None] < wall_count[:, None, None], wall_facet, 0)
    result = walls
    for axis_num in range(3):
        mirrored = walls[mirror[axis_num]]
        component = directions[axis_num][:, None, None, None, None]
        chosen = (((facets == 2 * axis_num + 1)[None, None] & (component > 0))
                  | ((facets == 2 * axis_num + 2)[None, None] & (component < 0)))
        result = jnp.where(chosen, mirrored, result)
    grid_view = grid_view.at[:, :, tile_ids, wall_blocks].set(result)
    return grid_view.reshape(phonon_heat_density.shape)


def reference(phonon_heat_density, directions, quad_weight, mirror, band_courant, relax_rate, mode_heat_magnitude, mode_pulsation, wall_blocks, wall_count, wall_facet):
    def move_one(pair):
        field_in, unit_vec = pair
        moved = roll_sweep(field_in, beam_coeffs((unit_vec[0] * band_courant)[:, None, None, None]), 1)
        moved = roll_sweep(moved, beam_coeffs((unit_vec[1] * band_courant)[:, None, None, None]), 3)
        moved = roll_sweep(moved, beam_coeffs((unit_vec[2] * band_courant)[:, None, None, None]), 2)
        return moved

    weights = (quad_weight[:, None] * relax_rate[None, :]).reshape(-1)
    collision_speed_factor = relax_rate * mode_heat_magnitude
    pseudo_kelvin_field = jnp.ones((MESH_WIDE_COUNT * LAYER_HIGH_COUNT * MESH_DEEP_COUNT,), jnp.float32)
    for step_num in range(STEPS):
        phonon_heat_density = reflect_walls(phonon_heat_density, directions, mirror, wall_blocks, wall_count, wall_facet)
        phonon_heat_density = lax.map(move_one, (phonon_heat_density, directions.T))
        injection_contribution = jnp.tensordot(weights, phonon_heat_density.reshape(DIRS * BANDS, MESH_WIDE_COUNT * LAYER_HIGH_COUNT * MESH_DEEP_COUNT), axes=1, precision=lax.Precision.HIGHEST)
        pseudo_kelvin_field = root_finder_guess(injection_contribution, collision_speed_factor, mode_pulsation)
        bose_einstein_heat = mode_heat_magnitude[:, None] / jnp.expm1(mode_pulsation[:, None] / pseudo_kelvin_field[None, :])
        phonon_heat_density = phonon_heat_density + relax_rate[None, :, None, None, None] * (bose_einstein_heat.reshape(1, BANDS, MESH_WIDE_COUNT, LAYER_HIGH_COUNT, MESH_DEEP_COUNT) - phonon_heat_density)
    return phonon_heat_density, pseudo_kelvin_field.reshape(MESH_WIDE_COUNT, LAYER_HIGH_COUNT, MESH_DEEP_COUNT)
```

```python
import functools

import jax
import jax.numpy as jnp
from jax import lax
from jax.experimental import pallas as pl
from jax.experimental.pallas import tpu as pltpu
from jax.sharding import PartitionSpec as P

NEWTON = 4
BANDS = 40
OCTS = 5
DIRS = 128
SRC = 32
OWN = 4
YC = 8
XZ = 8
ROW = BANDS * XZ
BLKS = 20
MSG = BLKS * OWN
MSG_OUT = MSG + 8
HI = lax.Precision.HIGHEST
NT = (((1,), (1,)), ((), ()))


def nt_dot(a, b):
    return lax.dot_general(a, b, NT, precision=HI, preferred_element_type=jnp.float32)


def nn_dot(a, b):
    return jnp.dot(a, b, precision=HI, preferred_element_type=jnp.float32)


def lanes(rows):
    return lax.broadcasted_iota(jnp.int32, (rows, DIRS), 1)


def tables_kernel(
    dirs_ref, weight_ref, mirror_ref, bands_ref, own_ref, blocks_ref, count_ref, facet_ref,
    spread_ref, coef_ref, srcw_ref, cols_ref, fac_ref, tmp, tmp2, slots,
):
    eye = (lax.broadcasted_iota(jnp.int32, (DIRS, DIRS), 0) == lanes(DIRS)).astype(jnp.float32)
    dirs = dirs_ref[...]
    tmp[...] = jnp.zeros_like(tmp)
    tmp[0:3, :] = (dirs < 0).astype(jnp.float32)
    tmp[3:6, :] = mirror_ref[...].astype(jnp.float32)
    cols = nt_dot(eye, tmp[...])
    lane_f = lanes(DIRS).astype(jnp.float32)
    rep = eye
    for axis in range(3):
        image = (cols[:, 3 + axis : 4 + axis] == lane_f).astype(jnp.float32)
        rep = jnp.where(cols[:, axis : axis + 1] > 0.5, nn_dot(rep, image), rep)
    negs = cols[:, 0:1] + cols[:, 1:2] + cols[:, 2:3]
    positive = jnp.broadcast_to((negs < 0.5).astype(jnp.float32), (DIRS, DIRS))
    below = (lax.broadcasted_iota(jnp.int32, (DIRS, DIRS), 0) > lanes(DIRS)).astype(jnp.float32)
    rank = nn_dot(rep, nn_dot(below, positive))
    place = 64.0 * cols[:, 0:1] + 32.0 * cols[:, 1:2] + 16.0 * cols[:, 2:3] + rank
    tmp2[...] = (place == lane_f).astype(jnp.float32)
    for own in range(OWN):
        spread_ref[own * SRC : (own + 1) * SRC, :] = tmp2[pl.ds(own, SRC, stride=OWN), :]
    tmp[0:3, :] = jnp.abs(dirs)
    tmp[3:4, :] = weight_ref[...]
    placed = nn_dot(tmp[...], tmp2[...])
    eye_b = (
        lax.broadcasted_iota(jnp.int32, (BANDS, BANDS), 0)
        == lax.broadcasted_iota(jnp.int32, (BANDS, BANDS), 1)
    ).astype(jnp.float32)
    per_band = nt_dot(eye_b, bands_ref[...])
    cols_ref[...] = per_band
    courant = per_band[:, 0:1]
    for axis in range(3):
        s = courant * placed[axis : axis + 1, :]
        at = axis * 3 * BANDS
        coef_ref[at : at + BANDS, :] = 1.0 - 1.5 * s + 0.5 * s * s
        coef_ref[at + BANDS : at + 2 * BANDS, :] = 2.0 * s - s * s
        coef_ref[at + 2 * BANDS : at + 3 * BANDS, :] = 0.5 * s * s - 0.5 * s
    srcw_ref[...] = per_band[:, 1:2] * placed[3:4, :]

    own = own_ref[0]
    half = own // 16
    offset = (own % 16) * YC
    for block in range(16):
        slots[block] = -1
    for k in range(16):
        @pl.when(k < count_ref[0])
        def _():
            slots[blocks_ref[0, k]] = k
    for xz in range(XZ):
        slot = slots[(xz // 4) * 8 + (xz % 4) * 2 + half]
        for y in range(YC):
            found = facet_ref[0, jnp.maximum(slot, 0), offset + y]
            fac_ref[xz * YC + y] = jnp.where(slot >= 0, found, 0)


def pack_kernel(x_ref, s_ref):
    for own in range(OWN):
        for half in range(2):
            pieces = []
            for xz in range(XZ):
                start = (own * BANDS * 2 + xz // 4) * 8 + half * 4 + xz % 4
                pieces.append(x_ref[pl.ds(start, BANDS, stride=16), :])
            rows = jnp.concatenate(pieces, axis=0)
            for part in range(2):
                t = rows[part * 128 : (part + 1) * 128].T
                for jj in range(16):
                    at = ((half * 16 + jj) * BLKS + part * YC) * OWN + own
                    s_ref[pl.ds(at, YC, stride=OWN), :] = t[jj * YC : (jj + 1) * YC]
            rest = rows[256:320]
            t = jnp.concatenate([rest, pltpu.roll(rest, 124, 1)], axis=0).T
            for jj in range(16):
                at = ((half * 16 + jj) * BLKS + 16) * OWN + own
                s_ref[pl.ds(at, 4, stride=OWN), :] = t[jj * YC : jj * YC + 4]


def block_rows(blk):
    if blk < 16:
        return [((blk % 8) * ROW + (blk // 8) * 128, 128)]
    y = blk - 16
    return [(y * ROW + 256, 64), ((y + 4) * ROW + 256, 64)]


def reflected(e, facet, lane):
    axis = lax.shift_right_logical(facet - 1, 1)
    odd = facet & 1
    bit = jnp.where(facet > 0, lax.shift_right_logical(64, jnp.maximum(axis, 0)), 0)
    want = jnp.where(facet > 0, jnp.where(odd == 1, 0, bit), 1)
    shift = jnp.where(odd == 1, 128 - bit, bit) & 127
    return jnp.where((lane & bit) == want, pltpu.roll(e, shift, 1), e)


def store_faces(y, z, e0, e1, low, a_ref, b_ref):
    at = (y * 4 + z) * BANDS
    r1 = pltpu.roll(e1, 64, 1)
    a_ref[pl.ds(at, BANDS), :] = jnp.where(low, e0, r1)
    b_ref[pl.ds(at, BANDS), :] = jnp.where(low, r1, e0)


def spread_kernel(r_ref, spread_ref, fac_ref, e_ref, a_ref, b_ref, f_ref):
    spread = spread_ref[...]
    for blk in range(BLKS):
        x = jnp.concatenate(
            [r_ref[pl.ds(blk * OWN + own, SRC, stride=MSG), :] for own in range(OWN)], axis=0
        )
        out = nn_dot(x.T, spread)
        done = 0
        for at, rows in block_rows(blk):
            f_ref[at : at + rows, :] = out[done : done + rows]
            done += rows
    lane = lanes(BANDS)
    low = lane < 64

    def one_y(y, carry):
        for z in range(4):
            cells = []
            for x in range(2):
                at = pl.multiple_of(y * ROW + (x * 4 + z) * BANDS, 8)
                e = reflected(f_ref[pl.ds(at, BANDS), :], fac_ref[(x * 4 + z) * YC + y], lane)
                e_ref[pl.ds(at, BANDS), :] = e
                cells.append(e)
            store_faces(y, z, cells[0], cells[1], low, a_ref, b_ref)
        return carry

    lax.fori_loop(0, YC, one_y, 0)


def sweep_x_kernel(e_ref, ml_ref, mr_ref, coef_ref, ax_ref, ya_ref, yb_ref):
    lane = lanes(BANDS)
    low = lane < 64
    pos = (lane & 32) == 0
    c0 = coef_ref[0:BANDS, :]
    c1 = coef_ref[BANDS : 2 * BANDS, :]
    c2 = coef_ref[2 * BANDS : 3 * BANDS, :]

    def one_y(y, carry):
        for z in range(4):
            at0 = pl.multiple_of(y * ROW + z * BANDS, 8)
            at1 = pl.multiple_of(y * ROW + (4 + z) * BANDS, 8)
            face = pl.multiple_of((y * 4 + z) * BANDS, 8)
            e0 = e_ref[pl.ds(at0, BANDS), :]
            e1 = e_ref[pl.ds(at1, BANDS), :]
            ml = ml_ref[pl.ds(face, BANDS), :]
            mr = mr_ref[pl.ds(face, BANDS), :]
            g0 = jnp.where(low, ml, mr)
            g1 = pltpu.roll(jnp.where(low, mr, ml), 64, 1)
            ax_ref[pl.ds(at0, BANDS), :] = c0 * e0 + c1 * jnp.where(low, g1, e1) + c2 * g0
            ax_ref[pl.ds(at1, BANDS), :] = c0 * e1 + c1 * jnp.where(low, e0, g0) + c2 * g1
        return carry

    lax.fori_loop(0, YC, one_y, 0)
    for xz in range(XZ):
        at = xz * BANDS
        row = lambda y: ax_ref[y * ROW + at : y * ROW + at + BANDS, :]
        ya_ref[at : at + BANDS, :] = jnp.where(pos, row(6), pltpu.roll(row(7), 32, 1))
        yb_ref[at : at + BANDS, :] = jnp.where(pos, pltpu.roll(row(1), 96, 1), row(0))


def expm1(q):
    small = q * (1.0 + q * (1 / 2) * (1.0 + q * (1 / 3) * (1.0 + q * (1 / 4) * (
        1.0 + q * (1 / 5) * (1.0 + q * (1 / 6))))))
    return jnp.where(q < 0.25, small, jnp.exp(q) - 1.0)


def moved_and_heat(ax_ref, ml_ref, mr_ref, coef_ref, srcw_ref, cols_ref, mv_ref, acc_ref):
    lane = lanes(8)
    pos_y = (lane & 32) == 0
    pos_z = (lane & 16) == 0
    acc_ref[...] = jnp.zeros_like(acc_ref)

    def one_octet(octet, carry):
        base = octet * 8

        def coef(k):
            return coef_ref[pl.ds(pl.multiple_of(base + k * BANDS, 8), 8), :]

        y0, y1, y2, z0, z1, z2 = (coef(k) for k in range(3, 9))
        weight = srcw_ref[pl.ds(pl.multiple_of(base, 8), 8), :]
        for x in range(2):
            ays = []
            for z in range(4):
                at = (x * 4 + z) * BANDS
                ml = ml_ref[pl.ds(pl.multiple_of(base + at, 8), 8), :]
                mr = mr_ref[pl.ds(pl.multiple_of(base + at, 8), 8), :]
                h0 = jnp.where(pos_y, ml, mr)
                h1 = jnp.where(pos_y, pltpu.roll(ml, 96, 1), pltpu.roll(mr, 32, 1))
                own = [
                    ax_ref[pl.ds(pl.multiple_of(base + y * ROW + at, 8), 8), :] for y in range(YC)
                ]
                ext = [h0, h1] + own + [h0, h1]
                ays.append([
                    y0 * ext[y + 2]
                    + y1 * jnp.where(pos_y, ext[y + 1], ext[y + 3])
                    + y2 * jnp.where(pos_y, ext[y], ext[y + 4])
                    for y in range(YC)
                ])
            for z in range(4):
                for y in range(YC):
                    near = jnp.where(pos_z, ays[(z + 3) % 4][y], ays[(z + 1) % 4][y])
                    mv = z0 * ays[z][y] + z1 * near + z2 * ays[(z + 2) % 4][y]
                    xz = x * 4 + z
                    mv_ref[pl.ds(pl.multiple_of(base + y * ROW + xz * BANDS, 8), 8), :] = mv
                    cell = (xz * YC + y) * 8
                    acc_ref[cell : cell + 8, :] += weight * mv
        return carry

    lax.fori_loop(0, OCTS, one_octet, 0)
    per_cell = acc_ref[...].reshape(64, 8, DIRS).sum(axis=1)
    source = nt_dot(jnp.ones((8, DIRS), jnp.float32), per_cell)[0:1, :]
    relax = cols_ref[:, 1:2]
    heat = cols_ref[:, 2:3]
    pulse = cols_ref[:, 3:4]
    speed = relax * heat
    temp = jnp.ones((1, 64), jnp.float32)
    for _ in range(NEWTON):
        q = pulse / temp
        surplus = expm1(q)
        mismatch = jnp.sum(speed / surplus, axis=0, keepdims=True) - source
        slope = jnp.sum(
            speed * q * jnp.exp(q) / (surplus * surplus), axis=0, keepdims=True
        ) / temp
        temp = jnp.clip(temp - mismatch / slope, 0.5 * temp, 2.0 * temp)
    return temp, relax * (heat / expm1(pulse / temp))


def step_kernel(
    ax_ref, ml_ref, mr_ref, coef_ref, srcw_ref, cols_ref, fac_ref,
    e_ref, a_ref, b_ref, mv_ref, acc_ref,
):
    _, eq = moved_and_heat(ax_ref, ml_ref, mr_ref, coef_ref, srcw_ref, cols_ref, mv_ref, acc_ref)
    keep = 1.0 - cols_ref[:, 1:2]
    lane = lanes(BANDS)
    low = lane < 64
    for y in range(YC):
        for z in range(4):
            cells = []
            for x in range(2):
                xz = x * 4 + z
                cell = xz * YC + y
                at = y * ROW + xz * BANDS
                e = keep * mv_ref[at : at + BANDS, :] + eq[:, cell : cell + 1]
                e = reflected(e, fac_ref[cell], lane)
                e_ref[at : at + BANDS, :] = e
                cells.append(e)
            store_faces(y, z, cells[0], cells[1], low, a_ref, b_ref)


def last_kernel(
    ax_ref, ml_ref, mr_ref, coef_ref, srcw_ref, cols_ref, spread_ref, own_ref,
    s_ref, mv_ref, acc_ref,
):
    temp, eq = moved_and_heat(
        ax_ref, ml_ref, mr_ref, coef_ref, srcw_ref, cols_ref, mv_ref, acc_ref
    )
    keep = 1.0 - cols_ref[:, 1:2]
    for y in range(YC):
        for xz in range(XZ):
            cell = xz * YC + y
            at = y * ROW + xz * BANDS
            mv_ref[at : at + BANDS, :] = (
                keep * mv_ref[at : at + BANDS, :] + eq[:, cell : cell + 1]
            )
    spread = spread_ref[...]
    for blk in range(BLKS):
        rows = jnp.concatenate([mv_ref[at : at + n, :] for at, n in block_rows(blk)], axis=0)
        out = nt_dot(spread, rows)
        for own in range(OWN):
            s_ref[pl.ds(blk * OWN + own, SRC, stride=MSG_OUT), :] = out[own * SRC : (own + 1) * SRC]
    offset = (own_ref[0] % 16) * YC
    lane = lanes(8)
    sub = lax.broadcasted_iota(jnp.int32, (8, DIRS), 0)
    wide = jnp.broadcast_to(
        jnp.concatenate([temp, jnp.zeros((1, 64), jnp.float32)], axis=1), (8, DIRS)
    )
    tile = jnp.zeros((8, DIRS), jnp.float32)
    for xz in range(XZ):
        turned = pltpu.roll(wide, (offset + (DIRS - xz * YC)) & 127, 1)
        tile = jnp.where(sub == xz, turned, tile)
    tile = jnp.where((lane >= offset) & (lane < offset + YC), tile, 0.0)
    for i in range(SRC):
        s_ref[i * MSG_OUT + MSG : (i + 1) * MSG_OUT, :] = tile


def unpack_kernel(r_ref, x_ref, t_ref):
    lane = lanes(64)
    for half in range(2):
        total = r_ref[half * 16 * MSG_OUT + MSG : (half * 16 + 1) * MSG_OUT, :]
        for jj in range(1, 16):
            at = (half * 16 + jj) * MSG_OUT
            total = total + r_ref[at + MSG : at + MSG_OUT, :]
        t_ref[:, half * 128 : (half + 1) * 128] = total
    for own in range(OWN):
        for half in range(2):
            base = half * 16 * MSG_OUT
            parts = []
            for part in range(2):
                rows = jnp.concatenate(
                    [
                        r_ref[pl.ds(base + jj * MSG_OUT + part * YC * OWN + own, YC, stride=OWN), :]
                        for jj in range(16)
                    ],
                    axis=0,
                )
                parts.append(rows.T)
            rows = []
            for jj in range(16):
                four = r_ref[pl.ds(base + jj * MSG_OUT + 16 * OWN + own, 4, stride=OWN), :]
                rows += [four, four]
            t = jnp.concatenate(rows, axis=0).T
            parts.append(jnp.where((lane & 4) == 0, t[:64], t[64:]))
            full = jnp.concatenate(parts, axis=0)
            for xz in range(XZ):
                start = (own * BANDS * 2 + xz // 4) * 8 + half * 4 + xz % 4
                x_ref[pl.ds(start, BANDS, stride=16), :] = full[xz * BANDS : (xz + 1) * BANDS]


def f32(*shape):
    return jax.ShapeDtypeStruct(shape, jnp.float32)


VMEM = pl.BlockSpec(memory_space=pltpu.VMEM)
SMEM = pl.BlockSpec(memory_space=pltpu.SMEM)


def call(kernel, in_specs, out_shape, scratch=(), out_specs=None, name=None):
    return pl.pallas_call(
        kernel,
        in_specs=in_specs,
        out_specs=out_specs or jax.tree.map(lambda _: VMEM, out_shape),
        out_shape=out_shape,
        scratch_shapes=list(scratch),
        name=name,
    )


def both_ways(up, down, axis):
    count = lax.axis_size(axis)
    right = [(i, (i + 1) % count) for i in range(count)]
    left = [(j, i) for i, j in right]
    return lax.ppermute(up, axis, right), lax.ppermute(down, axis, left)


def on_device(
    phonon_heat_density,
    directions,
    quad_weight,
    mirror,
    band_courant,
    relax_rate,
    mode_heat_magnitude,
    mode_pulsation,
    wall_blocks,
    wall_count,
    wall_facet,
):
    own = lax.axis_index("dir").astype(jnp.int32).reshape(1)
    bands = jnp.stack([band_courant, relax_rate, mode_heat_magnitude, mode_pulsation])
    bands = jnp.concatenate([bands, jnp.zeros_like(bands)])
    x2 = phonon_heat_density.reshape(OWN, BANDS, 2, 4, 2, 128)
    x2 = x2.transpose(0, 1, 2, 4, 3, 5).reshape(2560, 128)
    packed = call(pack_kernel, [VMEM], f32(2560, 128), name="pack")(x2)
    spread, coef, srcw, cols, fac = call(
        tables_kernel,
        [VMEM] * 4 + [SMEM] * 4,
        (f32(128, 128), f32(360, 128), f32(40, 128), f32(40, 8),
         jax.ShapeDtypeStruct((64,), jnp.int32)),
        [pltpu.VMEM((8, 128), jnp.float32), pltpu.VMEM((128, 128), jnp.float32),
         pltpu.SMEM((16,), jnp.int32)],
        (VMEM, VMEM, VMEM, VMEM, SMEM),
        name="tables",
    )(directions, quad_weight.reshape(1, 128), mirror, bands, own, wall_blocks, wall_count,
      wall_facet)
    met = lax.all_to_all(packed, "dir", 0, 0, tiled=True)
    faces = f32(1280, 128)
    field = f32(2560, 128)
    edge = f32(320, 128)
    e, a, b = call(
        spread_kernel, [VMEM, VMEM, SMEM], (field, faces, faces),
        [pltpu.VMEM((2560, 128), jnp.float32)], name="spread",
    )(met, spread, fac)
    work = [pltpu.VMEM((2560, 128), jnp.float32), pltpu.VMEM((512, 128), jnp.float32)]
    for step in range(2):
        ml, mr = both_ways(a, b, "space")
        ax, ya, yb = call(sweep_x_kernel, [VMEM] * 4, (field, edge, edge), name="sweep_x")(
            e, ml, mr, coef
        )
        ml, mr = both_ways(ya, yb, "dir")
        if step == 0:
            e, a, b = call(
                step_kernel, [VMEM] * 6 + [SMEM], (field, faces, faces), work, name="step"
            )(ax, ml, mr, coef, srcw, cols, fac)
        else:
            out = call(
                last_kernel, [VMEM] * 7 + [SMEM], f32(SRC * MSG_OUT, 128), work[:2], name="last"
            )(ax, ml, mr, coef, srcw, cols, spread, own)
    back = lax.all_to_all(out, "dir", 0, 0, tiled=True)
    x2, temp = call(unpack_kernel, [VMEM], (field, f32(8, 256)), name="unpack")(back)
    energy = x2.reshape(OWN, BANDS, 2, 2, 4, 128).transpose(0, 1, 2, 4, 3, 5)
    return energy.reshape(phonon_heat_density.shape), temp.reshape(2, 4, 256)


def solution(mesh):
    in_specs = (
        P("dir", None, "space", None, None),
        P(),
        P(),
        P(),
        P(),
        P(),
        P(),
        P(),
        P("space", None),
        P("space"),
        P("space", None, None),
    )
    out_specs = (P("dir", None, "space", None, None), P("space", None, None))
    return jax.shard_map(
        on_device, mesh=mesh, in_specs=in_specs, out_specs=out_specs, check_vma=False
    )
```

```python
import functools

import jax
import jax.numpy as jnp
from jax import lax
from jax.experimental import pallas as pl
from jax.experimental.pallas import tpu as pltpu
from jax.sharding import PartitionSpec as P

NEWTON = 4
BANDS = 40
OCTS = 5
DIRS = 128
SRC = 32
OWN = 4
YC = 8
XZ = 8
ROW = BANDS * XZ
BLKS = 20
MSG = BLKS * OWN
MSG_OUT = MSG + 8
HI = lax.Precision.HIGHEST
NT = (((1,), (1,)), ((), ()))


def nt_dot(a, b):
    return lax.dot_general(a, b, NT, precision=HI, preferred_element_type=jnp.float32)


def nn_dot(a, b):
    return jnp.dot(a, b, precision=HI, preferred_element_type=jnp.float32)


def lanes(rows):
    return lax.broadcasted_iota(jnp.int32, (rows, DIRS), 1)


def tables_kernel(
    dirs_ref, weight_ref, mirror_ref, bands_ref, own_ref, blocks_ref, count_ref, facet_ref,
    spread_ref, coef_ref, srcw_ref, cols_ref, fac_ref, tmp, tmp2, slots,
):
    eye = (lax.broadcasted_iota(jnp.int32, (DIRS, DIRS), 0) == lanes(DIRS)).astype(jnp.float32)
    dirs = dirs_ref[...]
    tmp[...] = jnp.zeros_like(tmp)
    tmp[0:3, :] = (dirs < 0).astype(jnp.float32)
    tmp[3:6, :] = mirror_ref[...].astype(jnp.float32)
    cols = nt_dot(eye, tmp[...])
    lane_f = lanes(DIRS).astype(jnp.float32)
    rep = eye
    for axis in range(3):
        image = (cols[:, 3 + axis : 4 + axis] == lane_f).astype(jnp.float32)
        rep = jnp.where(cols[:, axis : axis + 1] > 0.5, nn_dot(rep, image), rep)
    negs = cols[:, 0:1] + cols[:, 1:2] + cols[:, 2:3]
    positive = jnp.broadcast_to((negs < 0.5).astype(jnp.float32), (DIRS, DIRS))
    below = (lax.broadcasted_iota(jnp.int32, (DIRS, DIRS), 0) > lanes(DIRS)).astype(jnp.float32)
    rank = nn_dot(rep, nn_dot(below, positive))
    place = 64.0 * cols[:, 0:1] + 32.0 * cols[:, 1:2] + 16.0 * cols[:, 2:3] + rank
    tmp2[...] = (place == lane_f).astype(jnp.float32)
    for own in range(OWN):
        spread_ref[own * SRC : (own + 1) * SRC, :] = tmp2[pl.ds(own, SRC, stride=OWN), :]
    tmp[0:3, :] = jnp.abs(dirs)
    tmp[3:4, :] = weight_ref[...]
    placed = nn_dot(tmp[...], tmp2[...])
    eye_b = (
        lax.broadcasted_iota(jnp.int32, (BANDS, BANDS), 0)
        == lax.broadcasted_iota(jnp.int32, (BANDS, BANDS), 1)
    ).astype(jnp.float32)
    per_band = nt_dot(eye_b, bands_ref[...])
    cols_ref[...] = per_band
    courant = per_band[:, 0:1]
    for axis in range(3):
        s = courant * placed[axis : axis + 1, :]
        at = axis * 3 * BANDS
        coef_ref[at : at + BANDS, :] = 1.0 - 1.5 * s + 0.5 * s * s
        coef_ref[at + BANDS : at + 2 * BANDS, :] = 2.0 * s - s * s
        coef_ref[at + 2 * BANDS : at + 3 * BANDS, :] = 0.5 * s * s - 0.5 * s
    srcw_ref[...] = per_band[:, 1:2] * placed[3:4, :]

    own = own_ref[0]
    half = own // 16
    offset = (own % 16) * YC
    for block in range(16):
        slots[block] = -1
    for k in range(16):
        @pl.when(k < count_ref[0])
        def _():
            slots[blocks_ref[0, k]] = k
    for xz in range(XZ):
        slot = slots[(xz // 4) * 8 + (xz % 4) * 2 + half]
        for y in range(YC):
            found = facet_ref[0, jnp.maximum(slot, 0), offset + y]
            fac_ref[xz * YC + y] = jnp.where(slot >= 0, found, 0)


def pack_kernel(x_hbm, s_hbm, x_ref, s_ref, sems):
    ins = [
        pltpu.make_async_copy(
            x_hbm.at[pl.ds(own * 640, 640)], x_ref.at[pl.ds(own * 640, 640)], sems.at[own]
        )
        for own in range(OWN)
    ]
    outs = [
        pltpu.make_async_copy(
            s_ref.at[pl.ds(half * 1280, 1280)], s_hbm.at[pl.ds(half * 1280, 1280)],
            sems.at[OWN + half],
        )
        for half in range(2)
    ]
    for copy in ins:
        copy.start()
    for half in range(2):
        for own in range(OWN):
            if half == 0:
                ins[own].wait()
            pieces = []
            for xz in range(XZ):
                start = (own * BANDS * 2 + xz // 4) * 8 + half * 4 + xz % 4
                pieces.append(x_ref[pl.ds(start, BANDS, stride=16), :])
            rows = jnp.concatenate(pieces, axis=0)
            for part in range(2):
                t = rows[part * 128 : (part + 1) * 128].T
                for jj in range(16):
                    at = ((half * 16 + jj) * BLKS + part * YC) * OWN + own
                    s_ref[pl.ds(at, YC, stride=OWN), :] = t[jj * YC : (jj + 1) * YC]
            rest = rows[256:320]
            t = jnp.concatenate([rest, pltpu.roll(rest, 124, 1)], axis=0).T
            for jj in range(16):
                at = ((half * 16 + jj) * BLKS + 16) * OWN + own
                s_ref[pl.ds(at, 4, stride=OWN), :] = t[jj * YC : jj * YC + 4]
        outs[half].start()
    for copy in outs:
        copy.wait()


def block_rows(blk):
    if blk < 16:
        return [((blk % 8) * ROW + (blk // 8) * 128, 128)]
    y = blk - 16
    return [(y * ROW + 256, 64), ((y + 4) * ROW + 256, 64)]


def reflected(e, facet, lane):
    axis = lax.shift_right_logical(facet - 1, 1)
    odd = facet & 1
    bit = jnp.where(facet > 0, lax.shift_right_logical(64, jnp.maximum(axis, 0)), 0)
    want = jnp.where(facet > 0, jnp.where(odd == 1, 0, bit), 1)
    shift = jnp.where(odd == 1, 128 - bit, bit) & 127
    return jnp.where((lane & bit) == want, pltpu.roll(e, shift, 1), e)


def store_faces(y, z, e0, e1, low, a_ref, b_ref):
    at = (y * 4 + z) * BANDS
    r1 = pltpu.roll(e1, 64, 1)
    a_ref[pl.ds(at, BANDS), :] = jnp.where(low, e0, r1)
    b_ref[pl.ds(at, BANDS), :] = jnp.where(low, r1, e0)


def spread_kernel(r_ref, spread_ref, fac_ref, e_ref, a_ref, b_ref, f_ref):
    spread = spread_ref[...]
    for blk in range(BLKS):
        x = jnp.concatenate(
            [r_ref[pl.ds(blk * OWN + own, SRC, stride=MSG), :] for own in range(OWN)], axis=0
        )
        out = nn_dot(x.T, spread)
        done = 0
        for at, rows in block_rows(blk):
            f_ref[at : at + rows, :] = out[done : done + rows]
            done += rows
    lane = lanes(BANDS)
    low = lane < 64

    def one_y(y, carry):
        for z in range(4):
            cells = []
            for x in range(2):
                at = pl.multiple_of(y * ROW + (x * 4 + z) * BANDS, 8)
                e = reflected(f_ref[pl.ds(at, BANDS), :], fac_ref[(x * 4 + z) * YC + y], lane)
                e_ref[pl.ds(at, BANDS), :] = e
                cells.append(e)
            store_faces(y, z, cells[0], cells[1], low, a_ref, b_ref)
        return carry

    lax.fori_loop(0, YC, one_y, 0)


def sweep_x_kernel(e_ref, ml_ref, mr_ref, coef_ref, ax_ref, ya_ref, yb_ref):
    lane = lanes(BANDS)
    low = lane < 64
    pos = (lane & 32) == 0
    c0 = coef_ref[0:BANDS, :]
    c1 = coef_ref[BANDS : 2 * BANDS, :]
    c2 = coef_ref[2 * BANDS : 3 * BANDS, :]

    def one_y(y, carry):
        for z in range(4):
            at0 = pl.multiple_of(y * ROW + z * BANDS, 8)
            at1 = pl.multiple_of(y * ROW + (4 + z) * BANDS, 8)
            face = pl.multiple_of((y * 4 + z) * BANDS, 8)
            e0 = e_ref[pl.ds(at0, BANDS), :]
            e1 = e_ref[pl.ds(at1, BANDS), :]
            ml = ml_ref[pl.ds(face, BANDS), :]
            mr = mr_ref[pl.ds(face, BANDS), :]
            g0 = jnp.where(low, ml, mr)
            g1 = pltpu.roll(jnp.where(low, mr, ml), 64, 1)
            ax_ref[pl.ds(at0, BANDS), :] = c0 * e0 + c1 * jnp.where(low, g1, e1) + c2 * g0
            ax_ref[pl.ds(at1, BANDS), :] = c0 * e1 + c1 * jnp.where(low, e0, g0) + c2 * g1
        return carry

    lax.fori_loop(0, YC, one_y, 0)
    for xz in range(XZ):
        at = xz * BANDS
        row = lambda y: ax_ref[y * ROW + at : y * ROW + at + BANDS, :]
        ya_ref[at : at + BANDS, :] = jnp.where(pos, row(6), pltpu.roll(row(7), 32, 1))
        yb_ref[at : at + BANDS, :] = jnp.where(pos, pltpu.roll(row(1), 96, 1), row(0))


def expm1(q):
    small = q * (1.0 + q * (1 / 2) * (1.0 + q * (1 / 3) * (1.0 + q * (1 / 4) * (
        1.0 + q * (1 / 5) * (1.0 + q * (1 / 6))))))
    return jnp.where(q < 0.25, small, jnp.exp(q) - 1.0)


def moved_and_heat(ax_ref, ml_ref, mr_ref, coef_ref, srcw_ref, cols_ref, mv_ref, acc_ref):
    lane = lanes(8)
    pos_y = (lane & 32) == 0
    pos_z = (lane & 16) == 0
    acc_ref[...] = jnp.zeros_like(acc_ref)

    def one_octet(octet, carry):
        base = octet * 8

        def coef(k):
            return coef_ref[pl.ds(pl.multiple_of(base + k * BANDS, 8), 8), :]

        y0, y1, y2, z0, z1, z2 = (coef(k) for k in range(3, 9))
        weight = srcw_ref[pl.ds(pl.multiple_of(base, 8), 8), :]
        for x in range(2):
            ays = []
            for z in range(4):
                at = (x * 4 + z) * BANDS
                ml = ml_ref[pl.ds(pl.multiple_of(base + at, 8), 8), :]
                mr = mr_ref[pl.ds(pl.multiple_of(base + at, 8), 8), :]
                h0 = jnp.where(pos_y, ml, mr)
                h1 = jnp.where(pos_y, pltpu.roll(ml, 96, 1), pltpu.roll(mr, 32, 1))
                own = [
                    ax_ref[pl.ds(pl.multiple_of(base + y * ROW + at, 8), 8), :] for y in range(YC)
                ]
                ext = [h0, h1] + own + [h0, h1]
                ays.append([
                    y0 * ext[y + 2]
                    + y1 * jnp.where(pos_y, ext[y + 1], ext[y + 3])
                    + y2 * jnp.where(pos_y, ext[y], ext[y + 4])
                    for y in range(YC)
                ])
            for z in range(4):
                for y in range(YC):
                    near = jnp.where(pos_z, ays[(z + 3) % 4][y], ays[(z + 1) % 4][y])
                    mv = z0 * ays[z][y] + z1 * near + z2 * ays[(z + 2) % 4][y]
                    xz = x * 4 + z
                    mv_ref[pl.ds(pl.multiple_of(base + y * ROW + xz * BANDS, 8), 8), :] = mv
                    cell = (xz * YC + y) * 8
                    acc_ref[cell : cell + 8, :] += weight * mv
        return carry

    lax.fori_loop(0, OCTS, one_octet, 0)
    per_cell = acc_ref[...].reshape(64, 8, DIRS).sum(axis=1)
    source = nt_dot(jnp.ones((8, DIRS), jnp.float32), per_cell)[0:1, :]
    relax = cols_ref[:, 1:2]
    heat = cols_ref[:, 2:3]
    pulse = cols_ref[:, 3:4]
    speed = relax * heat
    temp = jnp.ones((1, 64), jnp.float32)
    for _ in range(NEWTON):
        q = pulse / temp
        surplus = expm1(q)
        mismatch = jnp.sum(speed / surplus, axis=0, keepdims=True) - source
        slope = jnp.sum(
            speed * q * jnp.exp(q) / (surplus * surplus), axis=0, keepdims=True
        ) / temp
        temp = jnp.clip(temp - mismatch / slope, 0.5 * temp, 2.0 * temp)
    return temp, relax * (heat / expm1(pulse / temp))


def step_kernel(
    ax_ref, ml_ref, mr_ref, coef_ref, srcw_ref, cols_ref, fac_ref,
    e_ref, a_ref, b_ref, mv_ref, acc_ref,
):
    _, eq = moved_and_heat(ax_ref, ml_ref, mr_ref, coef_ref, srcw_ref, cols_ref, mv_ref, acc_ref)
    keep = 1.0 - cols_ref[:, 1:2]
    lane = lanes(BANDS)
    low = lane < 64
    for y in range(YC):
        for z in range(4):
            cells = []
            for x in range(2):
                xz = x * 4 + z
                cell = xz * YC + y
                at = y * ROW + xz * BANDS
                e = keep * mv_ref[at : at + BANDS, :] + eq[:, cell : cell + 1]
                e = reflected(e, fac_ref[cell], lane)
                e_ref[at : at + BANDS, :] = e
                cells.append(e)
            store_faces(y, z, cells[0], cells[1], low, a_ref, b_ref)


def last_kernel(
    ax_ref, ml_ref, mr_ref, coef_ref, srcw_ref, cols_ref, spread_ref, own_ref,
    s_ref, mv_ref, acc_ref,
):
    temp, eq = moved_and_heat(
        ax_ref, ml_ref, mr_ref, coef_ref, srcw_ref, cols_ref, mv_ref, acc_ref
    )
    keep = 1.0 - cols_ref[:, 1:2]
    for y in range(YC):
        for xz in range(XZ):
            cell = xz * YC + y
            at = y * ROW + xz * BANDS
            mv_ref[at : at + BANDS, :] = (
                keep * mv_ref[at : at + BANDS, :] + eq[:, cell : cell + 1]
            )
    spread = spread_ref[...]
    for blk in range(BLKS):
        rows = jnp.concatenate([mv_ref[at : at + n, :] for at, n in block_rows(blk)], axis=0)
        out = nt_dot(spread, rows)
        for own in range(OWN):
            s_ref[pl.ds(blk * OWN + own, SRC, stride=MSG_OUT), :] = out[own * SRC : (own + 1) * SRC]
    offset = (own_ref[0] % 16) * YC
    lane = lanes(8)
    sub = lax.broadcasted_iota(jnp.int32, (8, DIRS), 0)
    wide = jnp.broadcast_to(
        jnp.concatenate([temp, jnp.zeros((1, 64), jnp.float32)], axis=1), (8, DIRS)
    )
    tile = jnp.zeros((8, DIRS), jnp.float32)
    for xz in range(XZ):
        turned = pltpu.roll(wide, (offset + (DIRS - xz * YC)) & 127, 1)
        tile = jnp.where(sub == xz, turned, tile)
    tile = jnp.where((lane >= offset) & (lane < offset + YC), tile, 0.0)
    for i in range(SRC):
        s_ref[i * MSG_OUT + MSG : (i + 1) * MSG_OUT, :] = tile


def unpack_kernel(r_ref, x_hbm, t_ref, x_ref, sems):
    lane = lanes(64)
    copies = []
    for half in range(2):
        total = r_ref[half * 16 * MSG_OUT + MSG : (half * 16 + 1) * MSG_OUT, :]
        for jj in range(1, 16):
            at = (half * 16 + jj) * MSG_OUT
            total = total + r_ref[at + MSG : at + MSG_OUT, :]
        for x in range(2):
            t_ref[x, :, half * 128 : (half + 1) * 128] = total[x * 4 : (x + 1) * 4]
    for own in range(OWN):
        for half in range(2):
            base = half * 16 * MSG_OUT
            parts = []
            for part in range(2):
                rows = jnp.concatenate(
                    [
                        r_ref[pl.ds(base + jj * MSG_OUT + part * YC * OWN + own, YC, stride=OWN), :]
                        for jj in range(16)
                    ],
                    axis=0,
                )
                parts.append(rows.T)
            rows = []
            for jj in range(16):
                four = r_ref[pl.ds(base + jj * MSG_OUT + 16 * OWN + own, 4, stride=OWN), :]
                rows += [four, four]
            t = jnp.concatenate(rows, axis=0).T
            parts.append(jnp.where((lane & 4) == 0, t[:64], t[64:]))
            full = jnp.concatenate(parts, axis=0)
            for xz in range(XZ):
                start = (own * BANDS * 2 + xz // 4) * 8 + half * 4 + xz % 4
                x_ref[pl.ds(start, BANDS, stride=16), :] = full[xz * BANDS : (xz + 1) * BANDS]
        part = pl.ds(own * 640, 640)
        copies.append(pltpu.make_async_copy(x_ref.at[part], x_hbm.at[part], sems.at[own]))
        copies[own].start()
    for copy in copies:
        copy.wait()


def f32(*shape):
    return pltpu.VMEM(shape, jnp.float32)


VMEM = pl.BlockSpec(memory_space=pltpu.VMEM)
SMEM = pl.BlockSpec(memory_space=pltpu.SMEM)
ANY = pl.BlockSpec(memory_space=pltpu.HBM)


def call(kernel, in_specs, out_shape, scratch=(), out_specs=None, name=None):
    def run(*args):
        args = [
            a if s is SMEM else pltpu.with_memory_space_constraint(a, s.memory_space)
            for a, s in zip(args, in_specs)
        ]
        return inner(*args)

    inner = pl.pallas_call(
        kernel,
        in_specs=in_specs,
        out_specs=out_specs or (tuple(VMEM for _ in out_shape) if isinstance(out_shape, tuple) else VMEM),
        out_shape=out_shape,
        scratch_shapes=list(scratch),
        compiler_params=pltpu.CompilerParams(vmem_limit_bytes=24 << 20),
        name=name,
    )
    return run


def both_ways(up, down, axis):
    count = lax.axis_size(axis)
    right = [(i, (i + 1) % count) for i in range(count)]
    left = [(j, i) for i, j in right]
    return lax.ppermute(up, axis, right), lax.ppermute(down, axis, left)


def on_device(
    phonon_heat_density,
    directions,
    quad_weight,
    mirror,
    band_courant,
    relax_rate,
    mode_heat_magnitude,
    mode_pulsation,
    wall_blocks,
    wall_count,
    wall_facet,
):
    own = lax.axis_index("dir").astype(jnp.int32).reshape(1)
    bands = jnp.stack([band_courant, relax_rate, mode_heat_magnitude, mode_pulsation])
    bands = jnp.concatenate([bands, jnp.zeros_like(bands)])
    x2 = phonon_heat_density.reshape(OWN, BANDS, 2, 4, 2, 128)
    x2 = x2.transpose(0, 1, 2, 4, 3, 5).reshape(2560, 128)
    staging = [pltpu.VMEM((2560, 128), jnp.float32), pltpu.SemaphoreType.DMA((OWN,))]
    packed = call(
        pack_kernel, [ANY], jax.ShapeDtypeStruct((2560, 128), jnp.float32),
        [pltpu.VMEM((2560, 128), jnp.float32)] * 2 + [pltpu.SemaphoreType.DMA((OWN + 2,))], ANY,
        name="pack",
    )(x2)
    spread, coef, srcw, cols, fac = call(
        tables_kernel,
        [VMEM] * 4 + [SMEM] * 4,
        (f32(128, 128), f32(360, 128), f32(40, 128), f32(40, 8),
         jax.ShapeDtypeStruct((64,), jnp.int32)),
        [pltpu.VMEM((8, 128), jnp.float32), pltpu.VMEM((128, 128), jnp.float32),
         pltpu.SMEM((16,), jnp.int32)],
        (VMEM, VMEM, VMEM, VMEM, SMEM),
        name="tables",
    )(directions, quad_weight.reshape(1, 128), mirror, bands, own, wall_blocks, wall_count,
      wall_facet)
    met = lax.all_to_all(packed, "dir", 0, 0, tiled=True)
    faces = f32(1280, 128)
    field = f32(2560, 128)
    edge = f32(320, 128)
    e, a, b = call(
        spread_kernel, [VMEM, VMEM, SMEM], (field, faces, faces),
        [pltpu.VMEM((2560, 128), jnp.float32)], name="spread",
    )(met, spread, fac)
    work = [pltpu.VMEM((2560, 128), jnp.float32), pltpu.VMEM((512, 128), jnp.float32)]
    for step in range(2):
        ml, mr = both_ways(a, b, "space")
        ax, ya, yb = call(sweep_x_kernel, [VMEM] * 4, (field, edge, edge), name="sweep_x")(
            e, ml, mr, coef
        )
        ml, mr = both_ways(ya, yb, "dir")
        if step == 0:
            e, a, b = call(
                step_kernel, [VMEM] * 6 + [SMEM], (field, faces, faces), work, name="step"
            )(ax, ml, mr, coef, srcw, cols, fac)
        else:
            out = call(
                last_kernel, [VMEM] * 7 + [SMEM], f32(SRC * MSG_OUT, 128), work[:2], name="last"
            )(ax, ml, mr, coef, srcw, cols, spread, own)
    back = lax.all_to_all(out, "dir", 0, 0, tiled=True)
    x2, temp = call(
        unpack_kernel,
        [VMEM],
        (jax.ShapeDtypeStruct((2560, 128), jnp.float32),
         jax.ShapeDtypeStruct((2, 4, 256), jnp.float32)),
        staging,
        (ANY, VMEM),
        name="unpack",
    )(back)
    energy = x2.reshape(OWN, BANDS, 2, 2, 4, 128).transpose(0, 1, 2, 4, 3, 5)
    return energy.reshape(phonon_heat_density.shape), temp


def solution(mesh):
    in_specs = (
        P("dir", None, "space", None, None),
        P(),
        P(),
        P(),
        P(),
        P(),
        P(),
        P(),
        P("space", None),
        P("space"),
        P("space", None, None),
    )
    out_specs = (P("dir", None, "space", None, None), P("space", None, None))
    return jax.shard_map(
        on_device, mesh=mesh, in_specs=in_specs, out_specs=out_specs, check_vma=False
    )
```

```python
import functools

import jax
import jax.numpy as jnp
from jax import lax
from jax.experimental import pallas as pl
from jax.experimental.pallas import tpu as pltpu
from jax.sharding import PartitionSpec as P

NEWTON = 4
BANDS = 40
OCTS = 5
DIRS = 128
SRC = 32
OWN = 4
YC = 8
XZ = 8
ROW = BANDS * XZ
BLKS = 20
MSG = BLKS * OWN
HI = lax.Precision.HIGHEST
NT = (((1,), (1,)), ((), ()))


def nt_dot(a, b):
    return lax.dot_general(a, b, NT, precision=HI, preferred_element_type=jnp.float32)


def nn_dot(a, b):
    return jnp.dot(a, b, precision=HI, preferred_element_type=jnp.float32)


def lanes(rows):
    return lax.broadcasted_iota(jnp.int32, (rows, DIRS), 1)


def tables_kernel(
    dirs_ref, weight_ref, mirror_ref, bands_ref, own_ref, blocks_ref, count_ref, facet_ref,
    spread_ref, coef_ref, srcw_ref, cols_ref, fac_ref, tmp, tmp2, slots,
):
    eye = (lax.broadcasted_iota(jnp.int32, (DIRS, DIRS), 0) == lanes(DIRS)).astype(jnp.float32)
    dirs = dirs_ref[...]
    tmp[...] = jnp.zeros_like(tmp)
    tmp[0:3, :] = (dirs < 0).astype(jnp.float32)
    tmp[3:6, :] = mirror_ref[...].astype(jnp.float32)
    cols = nt_dot(eye, tmp[...])
    lane_f = lanes(DIRS).astype(jnp.float32)
    rep = eye
    for axis in range(3):
        image = (cols[:, 3 + axis : 4 + axis] == lane_f).astype(jnp.float32)
        rep = jnp.where(cols[:, axis : axis + 1] > 0.5, nn_dot(rep, image), rep)
    negs = cols[:, 0:1] + cols[:, 1:2] + cols[:, 2:3]
    positive = jnp.broadcast_to((negs < 0.5).astype(jnp.float32), (DIRS, DIRS))
    below = (lax.broadcasted_iota(jnp.int32, (DIRS, DIRS), 0) > lanes(DIRS)).astype(jnp.float32)
    rank = nn_dot(rep, nn_dot(below, positive))
    place = 64.0 * cols[:, 0:1] + 32.0 * cols[:, 1:2] + 16.0 * cols[:, 2:3] + rank
    tmp2[...] = (place == lane_f).astype(jnp.float32)
    for own in range(OWN):
        spread_ref[own * SRC : (own + 1) * SRC, :] = tmp2[pl.ds(own, SRC, stride=OWN), :]
    tmp[0:3, :] = jnp.abs(dirs)
    tmp[3:4, :] = weight_ref[...]
    placed = nn_dot(tmp[...], tmp2[...])
    eye_b = (
        lax.broadcasted_iota(jnp.int32, (BANDS, BANDS), 0)
        == lax.broadcasted_iota(jnp.int32, (BANDS, BANDS), 1)
    ).astype(jnp.float32)
    per_band = nt_dot(eye_b, bands_ref[...])
    cols_ref[...] = per_band
    courant = per_band[:, 0:1]
    for axis in range(3):
        s = courant * placed[axis : axis + 1, :]
        at = axis * 3 * BANDS
        coef_ref[at : at + BANDS, :] = 1.0 - 1.5 * s + 0.5 * s * s
        coef_ref[at + BANDS : at + 2 * BANDS, :] = 2.0 * s - s * s
        coef_ref[at + 2 * BANDS : at + 3 * BANDS, :] = 0.5 * s * s - 0.5 * s
    srcw_ref[...] = per_band[:, 1:2] * placed[3:4, :]

    own = own_ref[0]
    half = own // 16
    offset = (own % 16) * YC
    for block in range(16):
        slots[block] = -1
    for k in range(16):
        @pl.when(k < count_ref[0])
        def _():
            slots[blocks_ref[0, k]] = k
    for xz in range(XZ):
        slot = slots[(xz // 4) * 8 + (xz % 4) * 2 + half]
        for y in range(YC):
            found = facet_ref[0, jnp.maximum(slot, 0), offset + y]
            fac_ref[xz * YC + y] = jnp.where(slot >= 0, found, 0)


def pack_kernel(x_hbm, s_hbm, x_ref, s_ref, sems):
    ins = [
        pltpu.make_async_copy(
            x_hbm.at[pl.ds(own * 640, 640)], x_ref.at[pl.ds(own * 640, 640)], sems.at[own]
        )
        for own in range(OWN)
    ]
    outs = [
        pltpu.make_async_copy(
            s_ref.at[pl.ds(half * 1280, 1280)], s_hbm.at[pl.ds(half * 1280, 1280)],
            sems.at[OWN + half],
        )
        for half in range(2)
    ]
    for copy in ins:
        copy.start()
    for half in range(2):
        for own in range(OWN):
            if half == 0:
                ins[own].wait()
            pieces = []
            for xz in range(XZ):
                start = (own * BANDS * 2 + xz // 4) * 8 + half * 4 + xz % 4
                pieces.append(x_ref[pl.ds(start, BANDS, stride=16), :])
            rows = jnp.concatenate(pieces, axis=0)
            for part in range(2):
                t = rows[part * 128 : (part + 1) * 128].T
                for jj in range(16):
                    at = ((half * 16 + jj) * BLKS + part * YC) * OWN + own
                    s_ref[pl.ds(at, YC, stride=OWN), :] = t[jj * YC : (jj + 1) * YC]
            rest = rows[256:320]
            t = jnp.concatenate([rest, pltpu.roll(rest, 124, 1)], axis=0).T
            for jj in range(16):
                at = ((half * 16 + jj) * BLKS + 16) * OWN + own
                s_ref[pl.ds(at, 4, stride=OWN), :] = t[jj * YC : jj * YC + 4]
        outs[half].start()
    for copy in outs:
        copy.wait()


def block_rows(blk):
    if blk < 16:
        return [((blk % 8) * ROW + (blk // 8) * 128, 128)]
    y = blk - 16
    return [(y * ROW + 256, 64), ((y + 4) * ROW + 256, 64)]


def reflected(e, facet, lane):
    axis = lax.shift_right_logical(facet - 1, 1)
    odd = facet & 1
    bit = jnp.where(facet > 0, lax.shift_right_logical(64, jnp.maximum(axis, 0)), 0)
    want = jnp.where(facet > 0, jnp.where(odd == 1, 0, bit), 1)
    shift = jnp.where(odd == 1, 128 - bit, bit) & 127
    return jnp.where((lane & bit) == want, pltpu.roll(e, shift, 1), e)


def store_edges(e_ref, ya_ref, yb_ref):
    pos = (lanes(BANDS) & 32) == 0
    for xz in range(XZ):
        at = xz * BANDS
        row = lambda y: e_ref[y * ROW + at : y * ROW + at + BANDS, :]
        ya_ref[at : at + BANDS, :] = jnp.where(pos, row(6), pltpu.roll(row(7), 32, 1))
        yb_ref[at : at + BANDS, :] = jnp.where(pos, pltpu.roll(row(1), 96, 1), row(0))


def store_faces(at, e0, e1, low, a_ref, b_ref):
    r1 = pltpu.roll(e1, 64, 1)
    a_ref[pl.ds(at, BANDS), :] = jnp.where(low, e0, r1)
    b_ref[pl.ds(at, BANDS), :] = jnp.where(low, r1, e0)


def spread_kernel(r_ref, spread_ref, fac_ref, e_ref, ya_ref, yb_ref, f_ref):
    spread = spread_ref[...]
    for blk in range(BLKS):
        x = jnp.concatenate(
            [r_ref[pl.ds(blk * OWN + own, SRC, stride=MSG), :] for own in range(OWN)], axis=0
        )
        out = nn_dot(x.T, spread)
        done = 0
        for at, rows in block_rows(blk):
            f_ref[at : at + rows, :] = out[done : done + rows]
            done += rows
    lane = lanes(BANDS)

    def one_y(y, carry):
        for xz in range(XZ):
            at = pl.multiple_of(y * ROW + xz * BANDS, 8)
            e_ref[pl.ds(at, BANDS), :] = reflected(
                f_ref[pl.ds(at, BANDS), :], fac_ref[xz * YC + y], lane
            )
        return carry

    lax.fori_loop(0, YC, one_y, 0)
    store_edges(e_ref, ya_ref, yb_ref)


def inner_kernel(e_ref, coef_ref, ay_ref, a_ref, b_ref):
    lane = lanes(BANDS)
    low = lane < 64
    pos = (lane & 32) == 0
    y0, y1, y2 = (coef_ref[k * BANDS : (k + 1) * BANDS, :] for k in range(3, 6))

    def one_row(k, carry):
        for z in range(4):
            swept = []
            for x in range(2):
                at = (x * 4 + z) * BANDS
                far, near, here = (
                    e_ref[pl.ds(pl.multiple_of((k + j) * ROW + at, 8), BANDS), :] for j in range(3)
                )
                ay = y0 * jnp.where(pos, here, far) + y1 * near + y2 * jnp.where(pos, far, here)
                ay_ref[pl.ds(pl.multiple_of(k * ROW + at, 8), BANDS), :] = ay
                swept.append(ay)
            at = pl.multiple_of((k * 4 + z) * BANDS, 8)
            store_faces(at, swept[0], swept[1], low, a_ref, b_ref)
        return carry

    lax.fori_loop(0, YC - 2, one_row, 0)


def outer_kernel(e_ref, ml_ref, mr_ref, coef_ref, ay_ref, a_ref, b_ref):
    lane = lanes(BANDS)
    low = lane < 64
    pos = (lane & 32) == 0
    y0, y1, y2 = (coef_ref[k * BANDS : (k + 1) * BANDS, :] for k in range(3, 6))
    for z in range(4):
        swept = []
        for x in range(2):
            at = (x * 4 + z) * BANDS
            row = lambda y: e_ref[y * ROW + at : y * ROW + at + BANDS, :]
            ml = ml_ref[at : at + BANDS, :]
            mr = mr_ref[at : at + BANDS, :]
            h0 = jnp.where(pos, ml, mr)
            h1 = jnp.where(pos, pltpu.roll(ml, 96, 1), pltpu.roll(mr, 32, 1))
            e0, e7 = row(0), row(7)
            ay0 = y0 * jnp.where(pos, e0, row(6)) + y1 * jnp.where(pos, h1, e7) + y2 * h0
            ay1 = y0 * jnp.where(pos, row(1), e7) + y1 * jnp.where(pos, e0, h0) + y2 * h1
            ay_ref[at : at + BANDS, :] = ay0
            ay_ref[ROW + at : ROW + at + BANDS, :] = ay1
            swept.append((ay0, ay1))
        for k in range(2):
            store_faces((k * 4 + z) * BANDS, swept[0][k], swept[1][k], low, a_ref, b_ref)


def expm1(q):
    small = q * (1.0 + q * (1 / 2) * (1.0 + q * (1 / 3) * (1.0 + q * (1 / 4) * (
        1.0 + q * (1 / 5) * (1.0 + q * (1 / 6))))))
    return jnp.where(q < 0.25, small, jnp.exp(q) - 1.0)


def moved_and_heat(
    inner, outer, coef_ref, srcw_ref, cols_ref, mv_ref, acc_ref
):
    lane = lanes(8)
    low = lane < 64
    pos_z = (lane & 16) == 0
    acc_ref[...] = jnp.zeros_like(acc_ref)

    def one_octet(octet, carry):
        base = octet * 8

        def load(ref, at):
            return ref[pl.ds(pl.multiple_of(base + at, 8), 8), :]

        x0, x1, x2, z0, z1, z2 = (load(coef_ref, k * BANDS) for k in (0, 1, 2, 6, 7, 8))
        weight = load(srcw_ref, 0)
        for k in range(YC):
            (ay_ref, ml_ref, mr_ref), row = (outer, k) if k < 2 else (inner, k - 2)
            swept = [[], []]
            for z in range(4):
                e0 = load(ay_ref, row * ROW + z * BANDS)
                e1 = load(ay_ref, row * ROW + (4 + z) * BANDS)
                ml = load(ml_ref, (row * 4 + z) * BANDS)
                mr = load(mr_ref, (row * 4 + z) * BANDS)
                g0 = jnp.where(low, ml, mr)
                g1 = pltpu.roll(jnp.where(low, mr, ml), 64, 1)
                swept[0].append(x0 * e0 + x1 * jnp.where(low, g1, e1) + x2 * g0)
                swept[1].append(x0 * e1 + x1 * jnp.where(low, e0, g0) + x2 * g1)
            for x in range(2):
                ax = swept[x]
                for z in range(4):
                    near = jnp.where(pos_z, ax[(z + 3) % 4], ax[(z + 1) % 4])
                    mv = z0 * ax[z] + z1 * near + z2 * ax[(z + 2) % 4]
                    xz = x * 4 + z
                    mv_ref[pl.ds(pl.multiple_of(base + k * ROW + xz * BANDS, 8), 8), :] = mv
                    cell = (xz * YC + k) * 8
                    acc_ref[cell : cell + 8, :] += weight * mv
        return carry

    lax.fori_loop(0, OCTS, one_octet, 0)
    skewed = acc_ref[...].reshape(64, 8, DIRS).sum(axis=1)
    turned = jnp.concatenate(
        [pltpu.roll(skewed[xz * YC : (xz + 1) * YC], 6, 0) for xz in range(XZ)], axis=0
    )
    per_cell = jnp.where((lanes(64) & 32) == 0, skewed, turned)
    source = nt_dot(jnp.ones((8, DIRS), jnp.float32), per_cell)[0:1, :]
    relax = cols_ref[:, 1:2]
    heat = cols_ref[:, 2:3]
    pulse = cols_ref[:, 3:4]
    speed = relax * heat
    temp = jnp.ones((1, 64), jnp.float32)
    for _ in range(NEWTON):
        q = pulse / temp
        surplus = expm1(q)
        mismatch = jnp.sum(speed / surplus, axis=0, keepdims=True) - source
        slope = jnp.sum(
            speed * q * jnp.exp(q) / (surplus * surplus), axis=0, keepdims=True
        ) / temp
        temp = jnp.clip(temp - mismatch / slope, 0.5 * temp, 2.0 * temp)
    return temp, relax * (heat / expm1(pulse / temp))


def relaxed(mv_ref, keep, eq, y, xz, pos):
    here, turned = (
        mv_ref[k * ROW + xz * BANDS : k * ROW + (xz + 1) * BANDS, :] for k in (y, (y + 2) % YC)
    )
    cell = xz * YC + y
    return keep * jnp.where(pos, here, turned) + eq[:, cell : cell + 1]


def step_kernel(
    ayi_ref, mli_ref, mri_ref, ayo_ref, mlo_ref, mro_ref, coef_ref, srcw_ref, cols_ref, fac_ref,
    e_ref, ya_ref, yb_ref, mv_ref, acc_ref,
):
    _, eq = moved_and_heat(
        (ayi_ref, mli_ref, mri_ref), (ayo_ref, mlo_ref, mro_ref), coef_ref, srcw_ref, cols_ref,
        mv_ref, acc_ref,
    )
    keep = 1.0 - cols_ref[:, 1:2]
    lane = lanes(BANDS)
    pos = (lane & 32) == 0
    for y in range(YC):
        for xz in range(XZ):
            e = relaxed(mv_ref, keep, eq, y, xz, pos)
            at = y * ROW + xz * BANDS
            e_ref[at : at + BANDS, :] = reflected(e, fac_ref[xz * YC + y], lane)
    store_edges(e_ref, ya_ref, yb_ref)


def last_kernel(
    ayi_ref, mli_ref, mri_ref, ayo_ref, mlo_ref, mro_ref, coef_ref, srcw_ref, cols_ref, spread_ref,
    own_ref, s_hbm, t_ref, mv_ref, acc_ref, e_ref, s_ref, sems,
):
    temp, eq = moved_and_heat(
        (ayi_ref, mli_ref, mri_ref), (ayo_ref, mlo_ref, mro_ref), coef_ref, srcw_ref, cols_ref,
        mv_ref, acc_ref,
    )
    offset = (own_ref[0] % 16) * YC
    lane = lanes(8)
    sub = lax.broadcasted_iota(jnp.int32, (8, DIRS), 0)
    wide = jnp.broadcast_to(
        jnp.concatenate([temp, jnp.zeros((1, 64), jnp.float32)], axis=1), (8, DIRS)
    )
    tile = jnp.zeros((8, DIRS), jnp.float32)
    for xz in range(XZ):
        turned = pltpu.roll(wide, (offset + (DIRS - xz * YC)) & 127, 1)
        tile = jnp.where(sub == xz, turned, tile)
    tile = jnp.where((lane >= offset) & (lane < offset + YC), tile, 0.0)
    half = own_ref[0] // 16
    for h in range(2):
        t_ref[h * 8 : (h + 1) * 8, :] = jnp.where(half == h, tile, 0.0)
    keep = 1.0 - cols_ref[:, 1:2]
    pos = (lanes(BANDS) & 32) == 0
    for y in range(YC):
        for xz in range(XZ):
            at = y * ROW + xz * BANDS
            e_ref[at : at + BANDS, :] = relaxed(mv_ref, keep, eq, y, xz, pos)
    spread = spread_ref[...]
    rows_ref = s_ref.reshape(SRC * MSG, DIRS)
    copies = []
    for blk in range(BLKS):
        rows = jnp.concatenate([e_ref[at : at + n, :] for at, n in block_rows(blk)], axis=0)
        out = nt_dot(spread, rows)
        for own in range(OWN):
            rows_ref[pl.ds(blk * OWN + own, SRC, stride=MSG), :] = out[own * SRC : (own + 1) * SRC]
        if blk % 10 == 9:
            part = pl.ds(blk // 10 * 40, 40)
            copies.append(
                pltpu.make_async_copy(
                    s_ref.at[:, part, :], s_hbm.at[:, part, :], sems.at[blk // 10]
                )
            )
            copies[-1].start()
    for copy in copies:
        copy.wait()


def unpack_kernel(r_ref, tiles_ref, x_hbm, t_ref, x_ref, sems):
    lane = lanes(64)
    copies = []
    for half in range(2):
        total = tiles_ref[half * 8 : (half + 1) * 8, :]
        for x in range(2):
            t_ref[x, :, half * 128 : (half + 1) * 128] = total[x * 4 : (x + 1) * 4]
    for own in range(OWN):
        for half in range(2):
            base = half * 16 * MSG
            parts = []
            for part in range(2):
                rows = jnp.concatenate(
                    [
                        r_ref[pl.ds(base + jj * MSG + part * YC * OWN + own, YC, stride=OWN), :]
                        for jj in range(16)
                    ],
                    axis=0,
                )
                parts.append(rows.T)
            rows = []
            for jj in range(16):
                four = r_ref[pl.ds(base + jj * MSG + 16 * OWN + own, 4, stride=OWN), :]
                rows += [four, four]
            t = jnp.concatenate(rows, axis=0).T
            parts.append(jnp.where((lane & 4) == 0, t[:64], t[64:]))
            full = jnp.concatenate(parts, axis=0)
            for xz in range(XZ):
                start = (own * BANDS * 2 + xz // 4) * 8 + half * 4 + xz % 4
                x_ref[pl.ds(start, BANDS, stride=16), :] = full[xz * BANDS : (xz + 1) * BANDS]
        part = pl.ds(own * 640, 640)
        copies.append(pltpu.make_async_copy(x_ref.at[part], x_hbm.at[part], sems.at[own]))
        copies[own].start()
    for copy in copies:
        copy.wait()


def f32(*shape):
    return pltpu.VMEM(shape, jnp.float32)


VMEM = pl.BlockSpec(memory_space=pltpu.VMEM)
SMEM = pl.BlockSpec(memory_space=pltpu.SMEM)
ANY = pl.BlockSpec(memory_space=pltpu.HBM)


def call(kernel, in_specs, out_shape, scratch=(), out_specs=None, name=None):
    def run(*args):
        args = [
            a if s is SMEM else pltpu.with_memory_space_constraint(a, s.memory_space)
            for a, s in zip(args, in_specs)
        ]
        return inner(*args)

    inner = pl.pallas_call(
        kernel,
        in_specs=in_specs,
        out_specs=out_specs or (tuple(VMEM for _ in out_shape) if isinstance(out_shape, tuple) else VMEM),
        out_shape=out_shape,
        scratch_shapes=list(scratch),
        compiler_params=pltpu.CompilerParams(vmem_limit_bytes=24 << 20),
        name=name,
    )
    return run


def both_ways(up, down, axis):
    count = lax.axis_size(axis)
    right = [(i, (i + 1) % count) for i in range(count)]
    left = [(j, i) for i, j in right]
    return lax.ppermute(up, axis, right), lax.ppermute(down, axis, left)


def on_device(
    phonon_heat_density,
    directions,
    quad_weight,
    mirror,
    band_courant,
    relax_rate,
    mode_heat_magnitude,
    mode_pulsation,
    wall_blocks,
    wall_count,
    wall_facet,
):
    own = lax.axis_index("dir").astype(jnp.int32).reshape(1)
    bands = jnp.stack([band_courant, relax_rate, mode_heat_magnitude, mode_pulsation])
    bands = jnp.concatenate([bands, jnp.zeros_like(bands)])
    x2 = phonon_heat_density.reshape(OWN, BANDS, 2, 4, 2, 128)
    x2 = x2.transpose(0, 1, 2, 4, 3, 5).reshape(2560, 128)
    staging = [pltpu.VMEM((2560, 128), jnp.float32), pltpu.SemaphoreType.DMA((OWN,))]
    packed = call(
        pack_kernel, [ANY], jax.ShapeDtypeStruct((2560, 128), jnp.float32),
        [pltpu.VMEM((2560, 128), jnp.float32)] * 2 + [pltpu.SemaphoreType.DMA((OWN + 2,))], ANY,
        name="pack",
    )(x2)
    spread, coef, srcw, cols, fac = call(
        tables_kernel,
        [VMEM] * 4 + [SMEM] * 4,
        (f32(128, 128), f32(360, 128), f32(40, 128), f32(40, 8),
         jax.ShapeDtypeStruct((64,), jnp.int32)),
        [pltpu.VMEM((8, 128), jnp.float32), pltpu.VMEM((128, 128), jnp.float32),
         pltpu.SMEM((16,), jnp.int32)],
        (VMEM, VMEM, VMEM, VMEM, SMEM),
        name="tables",
    )(directions, quad_weight.reshape(1, 128), mirror, bands, own, wall_blocks, wall_count,
      wall_facet)
    met = lax.all_to_all(packed, "dir", 0, 0, tiled=True)
    field = f32(2560, 128)
    edge = f32(320, 128)
    e, ya, yb = call(
        spread_kernel, [VMEM, VMEM, SMEM], (field, edge, edge),
        [pltpu.VMEM((2560, 128), jnp.float32)], name="spread",
    )(met, spread, fac)
    work = [pltpu.VMEM((2560, 128), jnp.float32), pltpu.VMEM((512, 128), jnp.float32)]
    for step in range(2):
        yl, yr = both_ways(ya, yb, "dir")
        ayi, a, b = call(
            inner_kernel, [VMEM] * 2, (f32(1920, 128), f32(960, 128), f32(960, 128)), name="inner"
        )(e, coef)
        mli, mri = both_ways(a, b, "space")
        ayo, a, b = call(outer_kernel, [VMEM] * 4, (f32(640, 128), edge, edge), name="outer")(
            e, yl, yr, coef
        )
        mlo, mro = both_ways(a, b, "space")
        swept = (ayi, mli, mri, ayo, mlo, mro, coef, srcw, cols)
        if step == 0:
            e, ya, yb = call(
                step_kernel, [VMEM] * 9 + [SMEM], (field, edge, edge), work, name="step"
            )(*swept, fac)
        else:
            out, tiles = call(
                last_kernel,
                [VMEM] * 10 + [SMEM],
                (jax.ShapeDtypeStruct((SRC, MSG, 128), jnp.float32), f32(16, 128)),
                work + [pltpu.VMEM((2560, 128), jnp.float32), pltpu.VMEM((SRC, MSG, 128), jnp.float32),
                        pltpu.SemaphoreType.DMA((2,))],
                (ANY, VMEM),
                name="last",
            )(*swept, spread, own)
    back = lax.all_to_all(out, "dir", 0, 0, tiled=True).reshape(2560, 128)
    for k in (1, 2, 4, 8, 16):
        tiles = tiles + lax.ppermute(tiles, "dir", [(i, i ^ k) for i in range(SRC)])
    x2, temp = call(
        unpack_kernel,
        [VMEM, VMEM],
        (jax.ShapeDtypeStruct((2560, 128), jnp.float32),
         jax.ShapeDtypeStruct((2, 4, 256), jnp.float32)),
        staging,
        (ANY, VMEM),
        name="unpack",
    )(back, tiles)
    energy = x2.reshape(OWN, BANDS, 2, 2, 4, 128).transpose(0, 1, 2, 4, 3, 5)
    return energy.reshape(phonon_heat_density.shape), temp


def solution(mesh):
    in_specs = (
        P("dir", None, "space", None, None),
        P(),
        P(),
        P(),
        P(),
        P(),
        P(),
        P(),
        P("space", None),
        P("space"),
        P("space", None, None),
    )
    out_specs = (P("dir", None, "space", None, None), P("space", None, None))
    return jax.shard_map(
        on_device, mesh=mesh, in_specs=in_specs, out_specs=out_specs, check_vma=False
    )
```

```python
import jax
import jax.numpy as jnp
from jax import lax
from jax.experimental import pallas as pl
from jax.experimental.pallas import tpu as pltpu
from jax.sharding import PartitionSpec as P

NEWTON = 4
BANDS = 40
OCTS = 5
DIRS = 128
SRC = 32
OWN = 4
YC = 8
XZ = 8
TILE = XZ * 8
ROW = OCTS * TILE
FACE = ROW // 2
MSG = 81
SENT = SRC * MSG
HI = lax.Precision.HIGHEST
NT = (((1,), (1,)), ((), ()))


def nt_dot(a, b):
    return lax.dot_general(a, b, NT, precision=HI, preferred_element_type=jnp.float32)


def nn_dot(a, b):
    return jnp.dot(a, b, precision=HI, preferred_element_type=jnp.float32)


def lanes(rows):
    return lax.broadcasted_iota(jnp.int32, (rows, DIRS), 1)


def taken(x, index):
    return jnp.take_along_axis(x, index, axis=1)


def tiled(x, count):
    return jnp.concatenate([x] * count, axis=0)


def tables_kernel(
    dirs_ref, weight_ref, mirror_ref, bands_ref, own_ref, blocks_ref, count_ref, facet_ref,
    coef_ref, srcw_ref, cols_ref, first_ref, image_ref, back_ref, tmp, tmp2, spread_ref, slots,
):
    eye = (lax.broadcasted_iota(jnp.int32, (DIRS, DIRS), 0) == lanes(DIRS)).astype(jnp.float32)
    dirs = dirs_ref[...]
    tmp[...] = jnp.zeros_like(tmp)
    tmp[0:3, :] = (dirs < 0).astype(jnp.float32)
    tmp[3:6, :] = mirror_ref[...].astype(jnp.float32)
    cols = nt_dot(eye, tmp[...])
    lane_f = lanes(DIRS).astype(jnp.float32)
    rep = eye
    for axis in range(3):
        image = (cols[:, 3 + axis : 4 + axis] == lane_f).astype(jnp.float32)
        rep = jnp.where(cols[:, axis : axis + 1] > 0.5, nn_dot(rep, image), rep)
    negs = cols[:, 0:1] + cols[:, 1:2] + cols[:, 2:3]
    positive = jnp.broadcast_to((negs < 0.5).astype(jnp.float32), (DIRS, DIRS))
    below = (lax.broadcasted_iota(jnp.int32, (DIRS, DIRS), 0) > lanes(DIRS)).astype(jnp.float32)
    rank = nn_dot(rep, nn_dot(below, positive))
    place = 64.0 * cols[:, 0:1] + 32.0 * cols[:, 1:2] + 16.0 * cols[:, 2:3] + rank
    tmp2[...] = (place == lane_f).astype(jnp.float32)
    for own in range(OWN):
        spread_ref[own * SRC : (own + 1) * SRC, :] = tmp2[pl.ds(own, SRC, stride=OWN), :]
    tmp[0:3, :] = jnp.abs(dirs)
    tmp[3:4, :] = weight_ref[...]
    placed = nn_dot(tmp[...], tmp2[...])
    eye_b = (
        lax.broadcasted_iota(jnp.int32, (BANDS, BANDS), 0)
        == lax.broadcasted_iota(jnp.int32, (BANDS, BANDS), 1)
    ).astype(jnp.float32)
    per_band = nt_dot(eye_b, bands_ref[...])
    cols_ref[...] = per_band
    courant = per_band[:, 0:1]
    for axis in range(3):
        s = courant * placed[axis : axis + 1, :]
        at = axis * 3 * BANDS
        coef_ref[at : at + BANDS, :] = 1.0 - 1.5 * s + 0.5 * s * s
        coef_ref[at + BANDS : at + 2 * BANDS, :] = 2.0 * s - s * s
        coef_ref[at + 2 * BANDS : at + 3 * BANDS, :] = 0.5 * s * s - 0.5 * s
    srcw_ref[...] = per_band[:, 1:2] * placed[3:4, :]

    lane = lanes(8)
    place_in = (nn_dot(lane_k(8), spread_ref[...]) + 0.5).astype(jnp.int32)
    back_ref[...] = (nt_dot(lane_k(8), spread_ref[...]) + 0.5).astype(jnp.int32)
    own = own_ref[0]
    half = own // 16
    offset = (own % 16) * YC
    for block in range(16):
        slots[block] = -1
    for k in range(16):
        @pl.when(k < count_ref[0])
        def _():
            slots[blocks_ref[0, k]] = k
    for xz in range(XZ):
        slot = slots[(xz // 4) * 8 + (xz % 4) * 2 + half]
        for y in range(YC):
            found = facet_ref[0, jnp.maximum(slot, 0), offset + y]
            facet = jnp.where(slot >= 0, found, 0)
            axis = lax.shift_right_logical(jnp.maximum(facet - 1, 0), 1)
            bit = jnp.where(facet > 0, lax.shift_right_logical(64, axis), 0)
            want = jnp.where((facet & 1) == 1, 0, bit)
            image = jnp.where((lane & bit) == want, lane ^ bit, lane)
            at = y * TILE + xz * 8
            image_ref[at : at + 8, :] = image
            first_ref[at : at + 8, :] = taken(place_in, image)


def lane_k(rows):
    return lanes(rows).astype(jnp.float32)


def pack_kernel(x_hbm, s_hbm, x_ref, s_ref, sems):
    ins = [
        pltpu.make_async_copy(
            x_hbm.at[pl.ds(own * 640, 640)], x_ref.at[pl.ds(own * 640, 640)], sems.at[own]
        )
        for own in range(OWN)
    ]
    for copy in ins:
        copy.start()
    lane = lanes(128)
    low = lane < 64
    low4 = lanes(4) < 64
    side = lane // 64
    natural = (lane % 8) * 16 + (lane // 32) % 2 * 8 + (lane // 8) % 4
    even = natural + side * 4
    odd = natural + (1 - side) * 4
    for dest in range(SRC):
        s_ref[dest * MSG + 80 : dest * MSG + 81, :] = jnp.zeros((1, DIRS), jnp.float32)
    for own in range(OWN):
        ins[own].wait()
        turned = []
        for octet in range(OCTS):
            at = own * 640 + octet * 128
            turned.append(x_ref[at : at + 128, :].T)
        for pair in range(2):
            a = taken(turned[2 * pair], even)
            b = taken(turned[2 * pair + 1], odd)
            for half, t in enumerate((jnp.where(low, a, b), jnp.where(low, b, a))):
                for jj in range(16):
                    at = (half * 16 + jj) * MSG + pair * 32 + own * YC
                    s_ref[at : at + YC, :] = t[jj * YC : (jj + 1) * YC]
        a = taken(turned[4], even)
        b = taken(turned[4], odd)
        for half, (t, u) in enumerate(((a, b), (b, a))):
            for jj in range(16):
                at = (half * 16 + jj) * MSG + 64 + own * 4
                y = jj * YC
                s_ref[at : at + 4, :] = jnp.where(low4, t[y : y + 4], u[y + 4 : y + 8])
    out = pltpu.make_async_copy(s_ref, s_hbm, sems.at[OWN])
    out.start()
    out.wait()


def upper_half():
    return lax.axis_index("dir").astype(jnp.int32) // 16


def store_edges(e_ref, ya_ref, yb_ref):
    pos = (lanes(TILE) & 32) == 0
    for octet in range(OCTS):
        at = octet * TILE
        row = lambda y: e_ref[y * ROW + at : y * ROW + at + TILE, :]
        ya_ref[at : at + TILE, :] = jnp.where(pos, row(6), pltpu.roll(row(7), 32, 1))
        yb_ref[at : at + TILE, :] = jnp.where(pos, pltpu.roll(row(1), 96, 1), row(0))


def store_faces(at, ay, low, a_ref, b_ref):
    e0, r1 = ay[:32], pltpu.roll(ay[32:], 64, 1)
    a_ref[pl.ds(at, 32), :] = jnp.where(low, e0, r1)
    b_ref[pl.ds(at, 32), :] = jnp.where(low, r1, e0)


def spread_kernel(r_ref, first_ref, e_ref, ya_ref, yb_ref):
    swap = upper_half() * TILE
    for y in (6, 7, 0, 1, 2, 3, 4, 5):
        index = first_ref[y * TILE : (y + 1) * TILE, :]
        for pair in range(2):
            t = jnp.concatenate(
                [
                    r_ref[pl.ds(pair * 32 + own * YC + y, SRC, stride=MSG), :]
                    for own in range(OWN)
                ],
                axis=0,
            ).T
            at = y * ROW + pair * 128
            e_ref[pl.ds(pl.multiple_of(at + swap, TILE), TILE), :] = taken(t[:TILE], index)
            e_ref[pl.ds(pl.multiple_of(at + TILE - swap, TILE), TILE), :] = taken(t[TILE:], index)
    for y in range(4):
        t = jnp.concatenate(
            [r_ref[pl.ds(64 + own * 4 + y, SRC, stride=MSG), :] for own in range(OWN)], axis=0
        ).T
        for part in range(2):
            yy = y + 4 * part
            index = first_ref[yy * TILE : (yy + 1) * TILE, :]
            e_ref[yy * ROW + 256 : yy * ROW + 320, :] = taken(
                t[part * TILE : (part + 1) * TILE], index
            )
    store_edges(e_ref, ya_ref, yb_ref)


def y_coefs(coef_ref, octet):
    at = 3 * BANDS + octet * 8
    return [tiled(coef_ref[at + k * BANDS : at + k * BANDS + 8, :], XZ) for k in range(3)]


def inner_kernel(e_ref, coef_ref, ay_ref, a_ref, b_ref):
    low = lanes(32) < 64
    pos = (lanes(TILE) & 32) == 0
    for octet in range(OCTS):
        y0, y1, y2 = y_coefs(coef_ref, octet)
        for k in range(YC - 2):
            at = octet * TILE
            far, near, here = (
                e_ref[(k + j) * ROW + at : (k + j) * ROW + at + TILE, :] for j in range(3)
            )
            ay = y0 * jnp.where(pos, here, far) + y1 * near + y2 * jnp.where(pos, far, here)
            ay_ref[k * ROW + at : k * ROW + at + TILE, :] = ay
            store_faces(k * FACE + octet * 32, ay, low, a_ref, b_ref)


def outer_kernel(e_ref, ml_ref, mr_ref, coef_ref, ay_ref, a_ref, b_ref):
    low = lanes(32) < 64
    pos = (lanes(TILE) & 32) == 0
    for octet in range(OCTS):
        y0, y1, y2 = y_coefs(coef_ref, octet)
        at = octet * TILE
        row = lambda y: e_ref[y * ROW + at : y * ROW + at + TILE, :]
        ml = ml_ref[at : at + TILE, :]
        mr = mr_ref[at : at + TILE, :]
        h0 = jnp.where(pos, ml, mr)
        h1 = jnp.where(pos, pltpu.roll(ml, 96, 1), pltpu.roll(mr, 32, 1))
        e0, e7 = row(0), row(7)
        ay0 = y0 * jnp.where(pos, e0, row(6)) + y1 * jnp.where(pos, h1, e7) + y2 * h0
        ay1 = y0 * jnp.where(pos, row(1), e7) + y1 * jnp.where(pos, e0, h0) + y2 * h1
        for k, ay in enumerate((ay0, ay1)):
            ay_ref[k * ROW + at : k * ROW + at + TILE, :] = ay
            store_faces(k * FACE + octet * 32, ay, low, a_ref, b_ref)


def expm1(q):
    small = q * (1.0 + q * (1 / 2) * (1.0 + q * (1 / 3) * (1.0 + q * (1 / 4) * (
        1.0 + q * (1 / 5) * (1.0 + q * (1 / 6))))))
    return jnp.where(q < 0.25, small, jnp.exp(q) - 1.0)


def moved_and_heat(
    inner, outer, coef_ref, srcw_ref, cols_ref, mv_ref, acc_ref
):
    lane = lanes(8)
    low = lane < 64
    pos_z = (lane & 16) == 0
    acc_ref[...] = jnp.zeros_like(acc_ref)

    def one_octet(octet, carry):
        def at(pitch, offset):
            return pl.ds(pl.multiple_of(octet * pitch + offset, 8), 8)

        x0, x1, x2, z0, z1, z2 = (coef_ref[at(8, k * BANDS), :] for k in (0, 1, 2, 6, 7, 8))
        weight = srcw_ref[at(8, 0), :]
        for k in range(YC):
            (ay_ref, ml_ref, mr_ref), row = (outer, k) if k < 2 else (inner, k - 2)
            swept = [[], []]
            for z in range(4):
                e0 = ay_ref[at(TILE, row * ROW + z * 8), :]
                e1 = ay_ref[at(TILE, row * ROW + (4 + z) * 8), :]
                ml = ml_ref[at(32, row * FACE + z * 8), :]
                mr = mr_ref[at(32, row * FACE + z * 8), :]
                g0 = jnp.where(low, ml, mr)
                g1 = pltpu.roll(jnp.where(low, mr, ml), 64, 1)
                swept[0].append(x0 * e0 + x1 * jnp.where(low, g1, e1) + x2 * g0)
                swept[1].append(x0 * e1 + x1 * jnp.where(low, e0, g0) + x2 * g1)
            for x in range(2):
                ax = swept[x]
                for z in range(4):
                    near = jnp.where(pos_z, ax[(z + 3) % 4], ax[(z + 1) % 4])
                    mv = z0 * ax[z] + z1 * near + z2 * ax[(z + 2) % 4]
                    xz = x * 4 + z
                    mv_ref[at(TILE, k * ROW + xz * 8), :] = mv
                    cell = (xz * YC + k) * 8
                    acc_ref[cell : cell + 8, :] += weight * mv
        return carry

    lax.fori_loop(0, OCTS, one_octet, 0)
    skewed = acc_ref[...].reshape(64, 8, DIRS).sum(axis=1)
    turned = jnp.concatenate(
        [pltpu.roll(skewed[xz * YC : (xz + 1) * YC], 6, 0) for xz in range(XZ)], axis=0
    )
    per_cell = jnp.where((lanes(64) & 32) == 0, skewed, turned)
    source = nt_dot(jnp.ones((8, DIRS), jnp.float32), per_cell)[0:1, :]
    relax = cols_ref[:, 1:2]
    heat = cols_ref[:, 2:3]
    pulse = cols_ref[:, 3:4]
    speed = relax * heat
    temp = jnp.ones((1, 64), jnp.float32)
    for _ in range(NEWTON):
        q = pulse / temp
        surplus = expm1(q)
        mismatch = jnp.sum(speed / surplus, axis=0, keepdims=True) - source
        slope = jnp.sum(
            speed * q * jnp.exp(q) / (surplus * surplus), axis=0, keepdims=True
        ) / temp
        temp = jnp.clip(temp - mismatch / slope, 0.5 * temp, 2.0 * temp)
    return temp, relax * (heat / expm1(pulse / temp))


def relaxed(mv_ref, keeps, eq, y, octet, pos):
    here, turned = (
        mv_ref[k * ROW + octet * TILE : k * ROW + (octet + 1) * TILE, :] for k in (y, (y + 2) % YC)
    )
    heat = jnp.concatenate(
        [
            jnp.broadcast_to(
                eq[octet * 8 : (octet + 1) * 8, xz * YC + y : xz * YC + y + 1], (8, DIRS)
            )
            for xz in range(XZ)
        ],
        axis=0,
    )
    return tiled(keeps[octet], XZ) * jnp.where(pos, here, turned) + heat


def kept(cols_ref):
    keep = jnp.broadcast_to(1.0 - cols_ref[:, 1:2], (BANDS, DIRS))
    return [keep[octet * 8 : (octet + 1) * 8] for octet in range(OCTS)]


def step_kernel(
    ayi_ref, mli_ref, mri_ref, ayo_ref, mlo_ref, mro_ref, coef_ref, srcw_ref, cols_ref, image_ref,
    e_ref, ya_ref, yb_ref, mv_ref, acc_ref,
):
    _, eq = moved_and_heat(
        (ayi_ref, mli_ref, mri_ref), (ayo_ref, mlo_ref, mro_ref), coef_ref, srcw_ref, cols_ref,
        mv_ref, acc_ref,
    )
    keeps = kept(cols_ref)
    pos = (lanes(TILE) & 32) == 0
    for y in range(YC):
        index = image_ref[y * TILE : (y + 1) * TILE, :]
        for octet in range(OCTS):
            at = y * ROW + octet * TILE
            e_ref[at : at + TILE, :] = taken(relaxed(mv_ref, keeps, eq, y, octet, pos), index)
    store_edges(e_ref, ya_ref, yb_ref)


def last_kernel(
    ayi_ref, mli_ref, mri_ref, ayo_ref, mlo_ref, mro_ref, coef_ref, srcw_ref, cols_ref, back_ref,
    s_ref, mv_ref, acc_ref, e_ref,
):
    temp, eq = moved_and_heat(
        (ayi_ref, mli_ref, mri_ref), (ayo_ref, mlo_ref, mro_ref), coef_ref, srcw_ref, cols_ref,
        mv_ref, acc_ref,
    )
    wide = jnp.concatenate([temp, jnp.zeros((1, DIRS - 64), jnp.float32)], axis=1)
    s_ref[pl.ds(80, SRC, stride=MSG), :] = jnp.broadcast_to(wide, (SRC, DIRS))
    keeps = kept(cols_ref)
    pos = (lanes(TILE) & 32) == 0
    index = tiled(back_ref[...], XZ)
    for y in range(YC):
        for octet in range(OCTS):
            at = y * ROW + octet * TILE
            e_ref[at : at + TILE, :] = taken(relaxed(mv_ref, keeps, eq, y, octet, pos), index)
    swap = upper_half() * TILE
    for y in range(YC):
        for pair in range(2):
            at = y * ROW + pair * 128
            t = jnp.concatenate(
                [
                    e_ref[pl.ds(pl.multiple_of(at + swap, TILE), TILE), :],
                    e_ref[pl.ds(pl.multiple_of(at + TILE - swap, TILE), TILE), :],
                ],
                axis=0,
            ).T
            for own in range(OWN):
                s_ref[pl.ds(pair * 32 + own * YC + y, SRC, stride=MSG), :] = t[
                    own * SRC : (own + 1) * SRC
                ]
    for y in range(4):
        t = jnp.concatenate(
            [e_ref[k * ROW + 256 : k * ROW + 320, :] for k in (y, y + 4)], axis=0
        ).T
        for own in range(OWN):
            s_ref[pl.ds(64 + own * 4 + y, SRC, stride=MSG), :] = t[own * SRC : (own + 1) * SRC]


def unpack_kernel(r_ref, x_hbm, t_ref, x_ref, sems):
    lane = lanes(128)
    low = lane < 64
    half_of = (lane // 4) % 2
    cell = ((lane // 8) % 2 * 4 + lane % 4) * 8 + lane // 16
    even = cell + half_of * 64
    odd = cell + (1 - half_of) * 64
    upper = lax.broadcasted_iota(jnp.int32, (128, DIRS), 0) % 8 // 4
    rest = cell + upper * 64
    copies = []
    for own in range(OWN):

        def finish(octet, x):
            at = own * 640 + octet * 128
            x_ref[at : at + 128, :] = x.T

        for pair in range(2):
            b0, b1 = (
                jnp.concatenate(
                    [
                        r_ref[at : at + YC, :]
                        for jj in range(16)
                        for at in [(half * 16 + jj) * MSG + pair * 32 + own * YC]
                    ],
                    axis=0,
                )
                for half in range(2)
            )
            finish(2 * pair, taken(jnp.where(low, b0, b1), even))
            finish(2 * pair + 1, taken(jnp.where(low, b1, b0), odd))
        fours = []
        for half in range(2):
            rows = []
            for jj in range(16):
                at = (half * 16 + jj) * MSG + 64 + own * 4
                four = r_ref[at : at + 4, :]
                rows += [four, four]
            fours.append(taken(jnp.concatenate(rows, axis=0), rest))
        finish(4, jnp.where(half_of == 0, fours[0], fours[1]))
        part = pl.ds(own * 640, 640)
        copies.append(pltpu.make_async_copy(x_ref.at[part], x_hbm.at[part], sems.at[own]))
        copies[own].start()
    lane = lanes(16)
    here = lane // 8 == lax.broadcasted_iota(jnp.int32, (16, DIRS), 0)
    for half in range(2):
        temps = r_ref[pl.ds(half * 16 * MSG + 80, 16, stride=MSG), :]
        for xz in range(XZ):
            spread = jnp.where(here, taken(temps, lane % 8 + xz * YC), 0.0)
            t_ref[xz // 4, xz % 4 : xz % 4 + 1, half * 128 : (half + 1) * 128] = jnp.sum(
                spread, axis=0, keepdims=True
            )
    for copy in copies:
        copy.wait()


def f32(*shape):
    return pltpu.VMEM(shape, jnp.float32)


VMEM = pl.BlockSpec(memory_space=pltpu.VMEM)
SMEM = pl.BlockSpec(memory_space=pltpu.SMEM)
ANY = pl.BlockSpec(memory_space=pltpu.HBM)


def call(kernel, in_specs, out_shape, scratch=(), out_specs=None, name=None, cost=None):
    if out_specs is None:
        out_specs = tuple(VMEM for _ in out_shape) if isinstance(out_shape, tuple) else VMEM

    def run(*args):
        args = [
            a if s is SMEM else pltpu.with_memory_space_constraint(a, s.memory_space)
            for a, s in zip(args, in_specs)
        ]
        return pl.pallas_call(
            kernel,
            in_specs=in_specs,
            out_specs=out_specs,
            out_shape=out_shape,
            scratch_shapes=list(scratch),
            compiler_params=pltpu.CompilerParams(vmem_limit_bytes=24 << 20),
            cost_estimate=cost,
            name=name,
        )(*args)

    return run


OUTER_COST = pl.CostEstimate(flops=0, transcendentals=0, bytes_accessed=200_000_000)


def exchanged(messages):
    whole = messages.reshape(SRC, 1, MSG * DIRS)
    return lax.all_to_all(whole, "dir", 0, 0, tiled=True).reshape(SENT, DIRS)


def both_ways(up, down, axis):
    count = lax.axis_size(axis)
    right = [(i, (i + 1) % count) for i in range(count)]
    left = [(j, i) for i, j in right]
    return lax.ppermute(up, axis, right), lax.ppermute(down, axis, left)


def on_device(
    phonon_heat_density,
    directions,
    quad_weight,
    mirror,
    band_courant,
    relax_rate,
    mode_heat_magnitude,
    mode_pulsation,
    wall_blocks,
    wall_count,
    wall_facet,
):
    own = lax.axis_index("dir").astype(jnp.int32).reshape(1)
    bands = jnp.stack([band_courant, relax_rate, mode_heat_magnitude, mode_pulsation])
    bands = jnp.concatenate([bands, jnp.zeros_like(bands)])
    x2 = phonon_heat_density.reshape(OWN, BANDS, 2, 4, 2, 128)
    x2 = x2.transpose(0, 1, 2, 4, 3, 5).reshape(2560, 128)
    whole = pltpu.VMEM((2560, 128), jnp.float32)
    packed = call(
        pack_kernel, [ANY], jax.ShapeDtypeStruct((SENT, 128), jnp.float32),
        [whole, pltpu.VMEM((SENT, 128), jnp.float32), pltpu.SemaphoreType.DMA((OWN + 1,))], ANY,
        name="pack",
    )(x2)
    index = pltpu.VMEM((YC * TILE, 128), jnp.int32)
    coef, srcw, cols, first, image, place = call(
        tables_kernel,
        [VMEM] * 4 + [SMEM] * 4,
        (f32(360, 128), f32(40, 128), f32(40, 8), index, index, pltpu.VMEM((8, 128), jnp.int32)),
        [pltpu.VMEM((8, 128), jnp.float32), pltpu.VMEM((128, 128), jnp.float32),
         pltpu.VMEM((128, 128), jnp.float32), pltpu.SMEM((16,), jnp.int32)],
        name="tables",
    )(directions, quad_weight.reshape(1, 128), mirror, bands, own, wall_blocks, wall_count,
      wall_facet)
    met = exchanged(packed)
    field = f32(2560, 128)
    edge = f32(ROW, 128)
    e, ya, yb = call(spread_kernel, [VMEM, VMEM], (field, edge, edge), name="spread")(met, first)
    work = [whole, pltpu.VMEM((512, 128), jnp.float32)]
    for step in range(2):
        yl, yr = both_ways(ya, yb, "dir")
        ayi, a, b = call(
            inner_kernel, [VMEM] * 2, (f32(6 * ROW, 128), f32(6 * FACE, 128), f32(6 * FACE, 128)),
            name="inner",
        )(e, coef)
        mli, mri = both_ways(a, b, "space")
        ayo, a, b = call(
            outer_kernel, [VMEM] * 4, (f32(2 * ROW, 128), edge, edge), name="outer", cost=OUTER_COST
        )(e, yl, yr, coef)
        mlo, mro = both_ways(a, b, "space")
        swept = (ayi, mli, mri, ayo, mlo, mro, coef, srcw, cols)
        if step == 0:
            e, ya, yb = call(
                step_kernel, [VMEM] * 10, (field, edge, edge), work, name="step"
            )(*swept, image)
        else:
            out = call(
                last_kernel, [VMEM] * 10, f32(SENT, 128), work + [whole], name="last"
            )(*swept, place)
    x2, temp = call(
        unpack_kernel,
        [VMEM],
        (jax.ShapeDtypeStruct((2560, 128), jnp.float32),
         jax.ShapeDtypeStruct((2, 4, 256), jnp.float32)),
        [whole, pltpu.SemaphoreType.DMA((OWN,))],
        (ANY, VMEM),
        name="unpack",
    )(exchanged(out))
    energy = x2.reshape(OWN, BANDS, 2, 2, 4, 128).transpose(0, 1, 2, 4, 3, 5)
    return energy.reshape(phonon_heat_density.shape), temp


def solution(mesh):
    in_specs = (
        P("dir", None, "space", None, None),
        P(),
        P(),
        P(),
        P(),
        P(),
        P(),
        P(),
        P("space", None),
        P("space"),
        P("space", None, None),
    )
    out_specs = (P("dir", None, "space", None, None), P("space", None, None))
    return jax.shard_map(
        on_device, mesh=mesh, in_specs=in_specs, out_specs=out_specs, check_vma=False
    )
```

```python
import jax
import jax.numpy as jnp
from jax import lax
from jax.experimental import pallas as pl
from jax.experimental.pallas import tpu as pltpu
from jax.sharding import PartitionSpec as P

NEWTON = 4
BANDS = 40
OCTS = 5
DIRS = 128
SRC = 32
OWN = 4
YC = 8
XZ = 8
TILE = XZ * 8
ROW = OCTS * TILE
FACE = ROW // 2
MSG = 81
SENT = SRC * MSG
HI = lax.Precision.HIGHEST
NT = (((1,), (1,)), ((), ()))


def nt_dot(a, b):
    return lax.dot_general(a, b, NT, precision=HI, preferred_element_type=jnp.float32)


def nn_dot(a, b):
    return jnp.dot(a, b, precision=HI, preferred_element_type=jnp.float32)


SNAKE = [c // 4 * 4 + (c % 4 if c // 4 % 2 == 0 else 3 - c % 4) for c in range(SRC)]


def chunk_of(device):
    along, across = device // 4, device % 4
    return along * 4 + jnp.where(along % 2 == 0, across, 3 - across)


def lanes(rows):
    return lax.broadcasted_iota(jnp.int32, (rows, DIRS), 1)


def taken(x, index):
    return jnp.take_along_axis(x, index, axis=1)


def tiled(x, count):
    return jnp.concatenate([x] * count, axis=0)


def tables_kernel(
    dirs_ref, weight_ref, mirror_ref, bands_ref, own_ref, blocks_ref, count_ref, facet_ref,
    coef_ref, srcw_ref, cols_ref, first_ref, image_ref, back_ref, tmp, tmp2, spread_ref, slots,
):
    eye = (lax.broadcasted_iota(jnp.int32, (DIRS, DIRS), 0) == lanes(DIRS)).astype(jnp.float32)
    dirs = dirs_ref[...]
    tmp[...] = jnp.zeros_like(tmp)
    tmp[0:3, :] = (dirs < 0).astype(jnp.float32)
    tmp[3:6, :] = mirror_ref[...].astype(jnp.float32)
    cols = nt_dot(eye, tmp[...])
    lane_f = lanes(DIRS).astype(jnp.float32)
    rep = eye
    for axis in range(3):
        image = (cols[:, 3 + axis : 4 + axis] == lane_f).astype(jnp.float32)
        rep = jnp.where(cols[:, axis : axis + 1] > 0.5, nn_dot(rep, image), rep)
    negs = cols[:, 0:1] + cols[:, 1:2] + cols[:, 2:3]
    positive = jnp.broadcast_to((negs < 0.5).astype(jnp.float32), (DIRS, DIRS))
    below = (lax.broadcasted_iota(jnp.int32, (DIRS, DIRS), 0) > lanes(DIRS)).astype(jnp.float32)
    rank = nn_dot(rep, nn_dot(below, positive))
    place = 64.0 * cols[:, 0:1] + 32.0 * cols[:, 1:2] + 16.0 * cols[:, 2:3] + rank
    tmp2[...] = (place == lane_f).astype(jnp.float32)
    for own in range(OWN):
        spread_ref[own * SRC : (own + 1) * SRC, :] = tmp2[pl.ds(own, SRC, stride=OWN), :]
    tmp[0:3, :] = jnp.abs(dirs)
    tmp[3:4, :] = weight_ref[...]
    placed = nn_dot(tmp[...], tmp2[...])
    eye_b = (
        lax.broadcasted_iota(jnp.int32, (BANDS, BANDS), 0)
        == lax.broadcasted_iota(jnp.int32, (BANDS, BANDS), 1)
    ).astype(jnp.float32)
    per_band = nt_dot(eye_b, bands_ref[...])
    cols_ref[...] = per_band
    courant = per_band[:, 0:1]
    for axis in range(3):
        s = courant * placed[axis : axis + 1, :]
        at = axis * 3 * BANDS
        coef_ref[at : at + BANDS, :] = 1.0 - 1.5 * s + 0.5 * s * s
        coef_ref[at + BANDS : at + 2 * BANDS, :] = 2.0 * s - s * s
        coef_ref[at + 2 * BANDS : at + 3 * BANDS, :] = 0.5 * s * s - 0.5 * s
    srcw_ref[...] = per_band[:, 1:2] * placed[3:4, :]

    lane = lanes(8)
    place_in = (nn_dot(lane_k(8), spread_ref[...]) + 0.5).astype(jnp.int32)
    back_ref[...] = (nt_dot(lane_k(8), spread_ref[...]) + 0.5).astype(jnp.int32)
    own = chunk_of(own_ref[0])
    half = own // 16
    offset = (own % 16) * YC
    for block in range(16):
        slots[block] = -1
    for k in range(16):
        @pl.when(k < count_ref[0])
        def _():
            slots[blocks_ref[0, k]] = k
    for xz in range(XZ):
        slot = slots[(xz // 4) * 8 + (xz % 4) * 2 + half]
        for y in range(YC):
            found = facet_ref[0, jnp.maximum(slot, 0), offset + y]
            facet = jnp.where(slot >= 0, found, 0)
            axis = lax.shift_right_logical(jnp.maximum(facet - 1, 0), 1)
            bit = jnp.where(facet > 0, lax.shift_right_logical(64, axis), 0)
            want = jnp.where((facet & 1) == 1, 0, bit)
            image = jnp.where((lane & bit) == want, lane ^ bit, lane)
            at = y * TILE + xz * 8
            image_ref[at : at + 8, :] = image
            first_ref[at : at + 8, :] = taken(place_in, image)


def lane_k(rows):
    return lanes(rows).astype(jnp.float32)


def pack_kernel(x_hbm, s_hbm, x_ref, s_ref, sems):
    ins = [
        pltpu.make_async_copy(
            x_hbm.at[pl.ds(own * 640, 640)], x_ref.at[pl.ds(own * 640, 640)], sems.at[own]
        )
        for own in range(OWN)
    ]
    for copy in ins:
        copy.start()
    lane = lanes(128)
    low = lane < 64
    low4 = lanes(4) < 64
    side = lane // 64
    natural = (lane % 8) * 16 + (lane // 32) % 2 * 8 + (lane // 8) % 4
    even = natural + side * 4
    odd = natural + (1 - side) * 4
    for dest in range(SRC):
        s_ref[dest * MSG + 80 : dest * MSG + 81, :] = jnp.zeros((1, DIRS), jnp.float32)
    for own in range(OWN):
        ins[own].wait()
        turned = []
        for octet in range(OCTS):
            at = own * 640 + octet * 128
            turned.append(x_ref[at : at + 128, :].T)
        for pair in range(2):
            a = taken(turned[2 * pair], even)
            b = taken(turned[2 * pair + 1], odd)
            for half, t in enumerate((jnp.where(low, a, b), jnp.where(low, b, a))):
                for jj in range(16):
                    at = SNAKE[half * 16 + jj] * MSG + pair * 32 + own * YC
                    s_ref[at : at + YC, :] = t[jj * YC : (jj + 1) * YC]
        a = taken(turned[4], even)
        b = taken(turned[4], odd)
        for half, (t, u) in enumerate(((a, b), (b, a))):
            for jj in range(16):
                at = SNAKE[half * 16 + jj] * MSG + 64 + own * 4
                y = jj * YC
                s_ref[at : at + 4, :] = jnp.where(low4, t[y : y + 4], u[y + 4 : y + 8])
    out = pltpu.make_async_copy(s_ref, s_hbm, sems.at[OWN])
    out.start()
    out.wait()


def upper_half():
    return lax.axis_index("dir").astype(jnp.int32) // 16


def store_edges(e_ref, ya_ref, yb_ref):
    pos = (lanes(TILE) & 32) == 0
    for octet in range(OCTS):
        at = octet * TILE
        row = lambda y: e_ref[y * ROW + at : y * ROW + at + TILE, :]
        ya_ref[at : at + TILE, :] = jnp.where(pos, row(6), pltpu.roll(row(7), 32, 1))
        yb_ref[at : at + TILE, :] = jnp.where(pos, pltpu.roll(row(1), 96, 1), row(0))


def store_faces(at, ay, low, a_ref, b_ref):
    e0, r1 = ay[:32], pltpu.roll(ay[32:], 64, 1)
    a_ref[pl.ds(at, 32), :] = jnp.where(low, e0, r1)
    b_ref[pl.ds(at, 32), :] = jnp.where(low, r1, e0)


def spread_kernel(r_ref, first_ref, coef_ref, e_ref, ya_ref, yb_ref, ay_ref, a_ref, b_ref):
    swap = upper_half() * TILE
    for y in (6, 7, 0, 1, 2, 3, 4, 5):
        index = first_ref[y * TILE : (y + 1) * TILE, :]
        for pair in range(2):
            t = jnp.concatenate(
                [
                    r_ref[pl.ds(pair * 32 + own * YC + y, SRC, stride=MSG), :]
                    for own in range(OWN)
                ],
                axis=0,
            ).T
            at = y * ROW + pair * 128
            e_ref[pl.ds(pl.multiple_of(at + swap, TILE), TILE), :] = taken(t[:TILE], index)
            e_ref[pl.ds(pl.multiple_of(at + TILE - swap, TILE), TILE), :] = taken(t[TILE:], index)
    for y in range(4):
        t = jnp.concatenate(
            [r_ref[pl.ds(64 + own * 4 + y, SRC, stride=MSG), :] for own in range(OWN)], axis=0
        ).T
        for part in range(2):
            yy = y + 4 * part
            index = first_ref[yy * TILE : (yy + 1) * TILE, :]
            e_ref[yy * ROW + 256 : yy * ROW + 320, :] = taken(
                t[part * TILE : (part + 1) * TILE], index
            )
    store_edges(e_ref, ya_ref, yb_ref)
    sweep_inner(e_ref, coef_ref, ay_ref, a_ref, b_ref)


def y_coefs(coef_ref, octet):
    at = 3 * BANDS + octet * 8
    return [tiled(coef_ref[at + k * BANDS : at + k * BANDS + 8, :], XZ) for k in range(3)]


def sweep_inner(e_ref, coef_ref, ay_ref, a_ref, b_ref):
    low = lanes(32) < 64
    pos = (lanes(TILE) & 32) == 0
    for octet in range(OCTS):
        y0, y1, y2 = y_coefs(coef_ref, octet)
        for k in range(YC - 2):
            at = octet * TILE
            far, near, here = (
                e_ref[(k + j) * ROW + at : (k + j) * ROW + at + TILE, :] for j in range(3)
            )
            ay = y0 * jnp.where(pos, here, far) + y1 * near + y2 * jnp.where(pos, far, here)
            ay_ref[k * ROW + at : k * ROW + at + TILE, :] = ay
            store_faces(k * FACE + octet * 32, ay, low, a_ref, b_ref)


def outer_kernel(e_ref, ml_ref, mr_ref, coef_ref, ay_ref, a_ref, b_ref):
    low = lanes(32) < 64
    pos = (lanes(TILE) & 32) == 0
    for octet in range(OCTS):
        y0, y1, y2 = y_coefs(coef_ref, octet)
        at = octet * TILE
        row = lambda y: e_ref[y * ROW + at : y * ROW + at + TILE, :]
        ml = ml_ref[at : at + TILE, :]
        mr = mr_ref[at : at + TILE, :]
        h0 = jnp.where(pos, ml, mr)
        h1 = jnp.where(pos, pltpu.roll(ml, 96, 1), pltpu.roll(mr, 32, 1))
        e0, e7 = row(0), row(7)
        ay0 = y0 * jnp.where(pos, e0, row(6)) + y1 * jnp.where(pos, h1, e7) + y2 * h0
        ay1 = y0 * jnp.where(pos, row(1), e7) + y1 * jnp.where(pos, e0, h0) + y2 * h1
        for k, ay in enumerate((ay0, ay1)):
            ay_ref[k * ROW + at : k * ROW + at + TILE, :] = ay
            store_faces(k * FACE + octet * 32, ay, low, a_ref, b_ref)


def expm1(q):
    small = q * (1.0 + q * (1 / 2) * (1.0 + q * (1 / 3) * (1.0 + q * (1 / 4) * (
        1.0 + q * (1 / 5) * (1.0 + q * (1 / 6))))))
    return jnp.where(q < 0.25, small, jnp.exp(q) - 1.0)


def moved_and_heat(
    inner, outer, coef_ref, srcw_ref, cols_ref, mv_ref, acc_ref
):
    lane = lanes(8)
    low = lane < 64
    pos_z = (lane & 16) == 0
    acc_ref[...] = jnp.zeros_like(acc_ref)

    def one_octet(octet, carry):
        def at(pitch, offset):
            return pl.ds(pl.multiple_of(octet * pitch + offset, 8), 8)

        x0, x1, x2, z0, z1, z2 = (coef_ref[at(8, k * BANDS), :] for k in (0, 1, 2, 6, 7, 8))
        weight = srcw_ref[at(8, 0), :]
        for k in range(YC):
            (ay_ref, ml_ref, mr_ref), row = (outer, k) if k < 2 else (inner, k - 2)
            swept = [[], []]
            for z in range(4):
                e0 = ay_ref[at(TILE, row * ROW + z * 8), :]
                e1 = ay_ref[at(TILE, row * ROW + (4 + z) * 8), :]
                ml = ml_ref[at(32, row * FACE + z * 8), :]
                mr = mr_ref[at(32, row * FACE + z * 8), :]
                g0 = jnp.where(low, ml, mr)
                g1 = pltpu.roll(jnp.where(low, mr, ml), 64, 1)
                swept[0].append(x0 * e0 + x1 * jnp.where(low, g1, e1) + x2 * g0)
                swept[1].append(x0 * e1 + x1 * jnp.where(low, e0, g0) + x2 * g1)
            for x in range(2):
                ax = swept[x]
                for z in range(4):
                    near = jnp.where(pos_z, ax[(z + 3) % 4], ax[(z + 1) % 4])
                    mv = z0 * ax[z] + z1 * near + z2 * ax[(z + 2) % 4]
                    xz = x * 4 + z
                    mv_ref[at(TILE, k * ROW + xz * 8), :] = mv
                    cell = (xz * YC + k) * 8
                    acc_ref[cell : cell + 8, :] += weight * mv
        return carry

    lax.fori_loop(0, OCTS, one_octet, 0)
    skewed = acc_ref[...].reshape(64, 8, DIRS).sum(axis=1)
    turned = jnp.concatenate(
        [pltpu.roll(skewed[xz * YC : (xz + 1) * YC], 6, 0) for xz in range(XZ)], axis=0
    )
    per_cell = jnp.where((lanes(64) & 32) == 0, skewed, turned)
    source = nt_dot(jnp.ones((8, DIRS), jnp.float32), per_cell)[0:1, :]
    relax = cols_ref[:, 1:2]
    heat = cols_ref[:, 2:3]
    pulse = cols_ref[:, 3:4]
    speed = relax * heat
    temp = jnp.ones((1, 64), jnp.float32)
    for _ in range(NEWTON):
        q = pulse / temp
        surplus = expm1(q)
        mismatch = jnp.sum(speed / surplus, axis=0, keepdims=True) - source
        slope = jnp.sum(
            speed * q * jnp.exp(q) / (surplus * surplus), axis=0, keepdims=True
        ) / temp
        temp = jnp.clip(temp - mismatch / slope, 0.5 * temp, 2.0 * temp)
    return temp, relax * (heat / expm1(pulse / temp))


def relaxed(mv_ref, keeps, eq, y, octet, pos):
    here, turned = (
        mv_ref[k * ROW + octet * TILE : k * ROW + (octet + 1) * TILE, :] for k in (y, (y + 2) % YC)
    )
    heat = jnp.concatenate(
        [
            jnp.broadcast_to(
                eq[octet * 8 : (octet + 1) * 8, xz * YC + y : xz * YC + y + 1], (8, DIRS)
            )
            for xz in range(XZ)
        ],
        axis=0,
    )
    return tiled(keeps[octet], XZ) * jnp.where(pos, here, turned) + heat


def kept(cols_ref):
    keep = jnp.broadcast_to(1.0 - cols_ref[:, 1:2], (BANDS, DIRS))
    return [keep[octet * 8 : (octet + 1) * 8] for octet in range(OCTS)]


def step_kernel(
    ayi_ref, mli_ref, mri_ref, ayo_ref, mlo_ref, mro_ref, coef_ref, srcw_ref, cols_ref, image_ref,
    e_ref, ya_ref, yb_ref, ay_ref, a_ref, b_ref, mv_ref, acc_ref,
):
    _, eq = moved_and_heat(
        (ayi_ref, mli_ref, mri_ref), (ayo_ref, mlo_ref, mro_ref), coef_ref, srcw_ref, cols_ref,
        mv_ref, acc_ref,
    )
    keeps = kept(cols_ref)
    pos = (lanes(TILE) & 32) == 0
    for y in range(YC):
        index = image_ref[y * TILE : (y + 1) * TILE, :]
        for octet in range(OCTS):
            at = y * ROW + octet * TILE
            e_ref[at : at + TILE, :] = taken(relaxed(mv_ref, keeps, eq, y, octet, pos), index)
    store_edges(e_ref, ya_ref, yb_ref)
    sweep_inner(e_ref, coef_ref, ay_ref, a_ref, b_ref)


def last_kernel(
    ayi_ref, mli_ref, mri_ref, ayo_ref, mlo_ref, mro_ref, coef_ref, srcw_ref, cols_ref, back_ref,
    s_ref, mv_ref, acc_ref, e_ref,
):
    temp, eq = moved_and_heat(
        (ayi_ref, mli_ref, mri_ref), (ayo_ref, mlo_ref, mro_ref), coef_ref, srcw_ref, cols_ref,
        mv_ref, acc_ref,
    )
    wide = jnp.concatenate([temp, jnp.zeros((1, DIRS - 64), jnp.float32)], axis=1)
    s_ref[pl.ds(80, SRC, stride=MSG), :] = jnp.broadcast_to(wide, (SRC, DIRS))
    keeps = kept(cols_ref)
    pos = (lanes(TILE) & 32) == 0
    index = tiled(back_ref[...], XZ)
    for y in range(YC):
        for octet in range(OCTS):
            at = y * ROW + octet * TILE
            e_ref[at : at + TILE, :] = taken(relaxed(mv_ref, keeps, eq, y, octet, pos), index)
    swap = upper_half() * TILE
    for y in range(YC):
        for pair in range(2):
            at = y * ROW + pair * 128
            t = jnp.concatenate(
                [
                    e_ref[pl.ds(pl.multiple_of(at + swap, TILE), TILE), :],
                    e_ref[pl.ds(pl.multiple_of(at + TILE - swap, TILE), TILE), :],
                ],
                axis=0,
            ).T
            for own in range(OWN):
                s_ref[pl.ds(pair * 32 + own * YC + y, SRC, stride=MSG), :] = t[
                    own * SRC : (own + 1) * SRC
                ]
    for y in range(4):
        t = jnp.concatenate(
            [e_ref[k * ROW + 256 : k * ROW + 320, :] for k in (y, y + 4)], axis=0
        ).T
        for own in range(OWN):
            s_ref[pl.ds(64 + own * 4 + y, SRC, stride=MSG), :] = t[own * SRC : (own + 1) * SRC]


def unpack_kernel(r_ref, x_hbm, t_ref, x_ref, sems):
    lane = lanes(128)
    low = lane < 64
    half_of = (lane // 4) % 2
    cell = ((lane // 8) % 2 * 4 + lane % 4) * 8 + lane // 16
    even = cell + half_of * 64
    odd = cell + (1 - half_of) * 64
    upper = lax.broadcasted_iota(jnp.int32, (128, DIRS), 0) % 8 // 4
    rest = cell + upper * 64
    copies = []
    for own in range(OWN):

        def finish(octet, x):
            at = own * 640 + octet * 128
            x_ref[at : at + 128, :] = x.T

        for pair in range(2):
            b0, b1 = (
                jnp.concatenate(
                    [
                        r_ref[at : at + YC, :]
                        for jj in range(16)
                        for at in [SNAKE[half * 16 + jj] * MSG + pair * 32 + own * YC]
                    ],
                    axis=0,
                )
                for half in range(2)
            )
            finish(2 * pair, taken(jnp.where(low, b0, b1), even))
            finish(2 * pair + 1, taken(jnp.where(low, b1, b0), odd))
        fours = []
        for half in range(2):
            rows = []
            for jj in range(16):
                at = SNAKE[half * 16 + jj] * MSG + 64 + own * 4
                four = r_ref[at : at + 4, :]
                rows += [four, four]
            fours.append(taken(jnp.concatenate(rows, axis=0), rest))
        finish(4, jnp.where(half_of == 0, fours[0], fours[1]))
        part = pl.ds(own * 640, 640)
        copies.append(pltpu.make_async_copy(x_ref.at[part], x_hbm.at[part], sems.at[own]))
        copies[own].start()
    lane = lanes(16)
    here = lane // 8 == chunk_of(lax.broadcasted_iota(jnp.int32, (16, DIRS), 0))
    for half in range(2):
        temps = r_ref[pl.ds(half * 16 * MSG + 80, 16, stride=MSG), :]
        for xz in range(XZ):
            spread = jnp.where(here, taken(temps, lane % 8 + xz * YC), 0.0)
            t_ref[xz // 4, xz % 4 : xz % 4 + 1, half * 128 : (half + 1) * 128] = jnp.sum(
                spread, axis=0, keepdims=True
            )
    for copy in copies:
        copy.wait()


def f32(*shape):
    return pltpu.VMEM(shape, jnp.float32)


VMEM = pl.BlockSpec(memory_space=pltpu.VMEM)
SMEM = pl.BlockSpec(memory_space=pltpu.SMEM)
ANY = pl.BlockSpec(memory_space=pltpu.HBM)


def call(kernel, in_specs, out_shape, scratch=(), out_specs=None, name=None, cost=None):
    if out_specs is None:
        out_specs = tuple(VMEM for _ in out_shape) if isinstance(out_shape, tuple) else VMEM

    def run(*args):
        args = [
            a if s is SMEM else pltpu.with_memory_space_constraint(a, s.memory_space)
            for a, s in zip(args, in_specs)
        ]
        return pl.pallas_call(
            kernel,
            in_specs=in_specs,
            out_specs=out_specs,
            out_shape=out_shape,
            scratch_shapes=list(scratch),
            compiler_params=pltpu.CompilerParams(vmem_limit_bytes=24 << 20),
            cost_estimate=cost,
            name=name,
        )(*args)

    return run


OUTER_COST = pl.CostEstimate(flops=0, transcendentals=0, bytes_accessed=200_000_000)


def exchanged(messages):
    whole = messages.reshape(SRC, 1, MSG * DIRS)
    return lax.all_to_all(whole, "dir", 0, 0, tiled=True).reshape(SENT, DIRS)


def both_ways(up, down, axis):
    order = SNAKE if axis == "dir" else list(range(lax.axis_size(axis)))
    right = list(zip(order, order[1:] + order[:1]))
    left = [(j, i) for i, j in right]
    return lax.ppermute(up, axis, right), lax.ppermute(down, axis, left)


def on_device(
    phonon_heat_density,
    directions,
    quad_weight,
    mirror,
    band_courant,
    relax_rate,
    mode_heat_magnitude,
    mode_pulsation,
    wall_blocks,
    wall_count,
    wall_facet,
):
    own = lax.axis_index("dir").astype(jnp.int32).reshape(1)
    bands = jnp.stack([band_courant, relax_rate, mode_heat_magnitude, mode_pulsation])
    bands = jnp.concatenate([bands, jnp.zeros_like(bands)])
    x2 = phonon_heat_density.reshape(OWN, BANDS, 2, 4, 2, 128)
    x2 = x2.transpose(0, 1, 2, 4, 3, 5).reshape(2560, 128)
    whole = pltpu.VMEM((2560, 128), jnp.float32)
    packed = call(
        pack_kernel, [ANY], jax.ShapeDtypeStruct((SENT, 128), jnp.float32),
        [whole, pltpu.VMEM((SENT, 128), jnp.float32), pltpu.SemaphoreType.DMA((OWN + 1,))], ANY,
        name="pack",
    )(x2)
    index = pltpu.VMEM((YC * TILE, 128), jnp.int32)
    coef, srcw, cols, first, image, place = call(
        tables_kernel,
        [VMEM] * 4 + [SMEM] * 4,
        (f32(360, 128), f32(40, 128), f32(40, 8), index, index, pltpu.VMEM((8, 128), jnp.int32)),
        [pltpu.VMEM((8, 128), jnp.float32), pltpu.VMEM((128, 128), jnp.float32),
         pltpu.VMEM((128, 128), jnp.float32), pltpu.SMEM((16,), jnp.int32)],
        name="tables",
    )(directions, quad_weight.reshape(1, 128), mirror, bands, own, wall_blocks, wall_count,
      wall_facet)
    met = exchanged(packed)
    field = f32(2560, 128)
    edge = f32(ROW, 128)
    swept_inner = (f32(6 * ROW, 128), f32(6 * FACE, 128), f32(6 * FACE, 128))
    e, ya, yb, ayi, a, b = call(
        spread_kernel, [VMEM] * 3, (field, edge, edge, *swept_inner), name="spread"
    )(met, first, coef)
    work = [whole, pltpu.VMEM((512, 128), jnp.float32)]
    for step in range(2):
        yl, yr = both_ways(ya, yb, "dir")
        mli, mri = both_ways(a, b, "space")
        ayo, a, b = call(
            outer_kernel, [VMEM] * 4, (f32(2 * ROW, 128), edge, edge), name="outer", cost=OUTER_COST
        )(e, yl, yr, coef)
        mlo, mro = both_ways(a, b, "space")
        swept = (ayi, mli, mri, ayo, mlo, mro, coef, srcw, cols)
        if step == 0:
            e, ya, yb, ayi, a, b = call(
                step_kernel, [VMEM] * 10, (field, edge, edge, *swept_inner), work, name="step"
            )(*swept, image)
        else:
            out = call(
                last_kernel, [VMEM] * 10, f32(SENT, 128), work + [whole], name="last"
            )(*swept, place)
    x2, temp = call(
        unpack_kernel,
        [VMEM],
        (jax.ShapeDtypeStruct((2560, 128), jnp.float32),
         jax.ShapeDtypeStruct((2, 4, 256), jnp.float32)),
        [whole, pltpu.SemaphoreType.DMA((OWN,))],
        (ANY, VMEM),
        name="unpack",
    )(exchanged(out))
    energy = x2.reshape(OWN, BANDS, 2, 2, 4, 128).transpose(0, 1, 2, 4, 3, 5)
    return energy.reshape(phonon_heat_density.shape), temp


def solution(mesh):
    in_specs = (
        P("dir", None, "space", None, None),
        P(),
        P(),
        P(),
        P(),
        P(),
        P(),
        P(),
        P("space", None),
        P("space"),
        P("space", None, None),
    )
    out_specs = (P("dir", None, "space", None, None), P("space", None, None))
    return jax.shard_map(
        on_device, mesh=mesh, in_specs=in_specs, out_specs=out_specs, check_vma=False
    )
```

```python
import jax
import jax.numpy as jnp
from jax import lax
from jax.experimental import pallas as pl
from jax.experimental.pallas import tpu as pltpu
from jax.sharding import PartitionSpec as P

NEWTON = 4
BANDS = 40
OCTS = 5
DIRS = 128
SRC = 32
OWN = 4
YC = 8
XZ = 8
TILE = XZ * 8
ROW = OCTS * TILE
FACE = ROW // 2
MSG = 81
SENT = SRC * MSG
HI = lax.Precision.HIGHEST
NT = (((1,), (1,)), ((), ()))


def nt_dot(a, b):
    return lax.dot_general(a, b, NT, precision=HI, preferred_element_type=jnp.float32)


def nn_dot(a, b):
    return jnp.dot(a, b, precision=HI, preferred_element_type=jnp.float32)


SNAKE = [c // 4 * 4 + (c % 4 if c // 4 % 2 == 0 else 3 - c % 4) for c in range(SRC)]


def chunk_of(device):
    along, across = device // 4, device % 4
    return along * 4 + jnp.where(along % 2 == 0, across, 3 - across)


def lanes(rows):
    return lax.broadcasted_iota(jnp.int32, (rows, DIRS), 1)


def taken(x, index):
    return jnp.take_along_axis(x, index, axis=1)


def tiled(x, count):
    return jnp.concatenate([x] * count, axis=0)


def tables_kernel(
    dirs_ref, weight_ref, mirror_ref, bands_ref, own_ref, blocks_ref, count_ref, facet_ref,
    coef_ref, srcw_ref, cols_ref, first_ref, image_ref, back_ref, tmp, tmp2, spread_ref, slots,
):
    eye = (lax.broadcasted_iota(jnp.int32, (DIRS, DIRS), 0) == lanes(DIRS)).astype(jnp.float32)
    dirs = dirs_ref[...]
    tmp[...] = jnp.zeros_like(tmp)
    tmp[0:3, :] = (dirs < 0).astype(jnp.float32)
    tmp[3:6, :] = mirror_ref[...].astype(jnp.float32)
    cols = nt_dot(eye, tmp[...])
    lane_f = lanes(DIRS).astype(jnp.float32)
    rep = eye
    for axis in range(3):
        image = (cols[:, 3 + axis : 4 + axis] == lane_f).astype(jnp.float32)
        rep = jnp.where(cols[:, axis : axis + 1] > 0.5, nn_dot(rep, image), rep)
    negs = cols[:, 0:1] + cols[:, 1:2] + cols[:, 2:3]
    positive = jnp.broadcast_to((negs < 0.5).astype(jnp.float32), (DIRS, DIRS))
    below = (lax.broadcasted_iota(jnp.int32, (DIRS, DIRS), 0) > lanes(DIRS)).astype(jnp.float32)
    rank = nn_dot(rep, nn_dot(below, positive))
    place = 64.0 * cols[:, 0:1] + 32.0 * cols[:, 1:2] + 16.0 * cols[:, 2:3] + rank
    tmp2[...] = (place == lane_f).astype(jnp.float32)
    for own in range(OWN):
        spread_ref[own * SRC : (own + 1) * SRC, :] = tmp2[pl.ds(own, SRC, stride=OWN), :]
    tmp[0:3, :] = jnp.abs(dirs)
    tmp[3:4, :] = weight_ref[...]
    placed = nn_dot(tmp[...], tmp2[...])
    eye_b = (
        lax.broadcasted_iota(jnp.int32, (BANDS, BANDS), 0)
        == lax.broadcasted_iota(jnp.int32, (BANDS, BANDS), 1)
    ).astype(jnp.float32)
    per_band = nt_dot(eye_b, bands_ref[...])
    cols_ref[...] = per_band
    courant = per_band[:, 0:1]
    for axis in range(3):
        s = courant * placed[axis : axis + 1, :]
        at = axis * 3 * BANDS
        coef_ref[at : at + BANDS, :] = 1.0 - 1.5 * s + 0.5 * s * s
        coef_ref[at + BANDS : at + 2 * BANDS, :] = 2.0 * s - s * s
        coef_ref[at + 2 * BANDS : at + 3 * BANDS, :] = 0.5 * s * s - 0.5 * s
    srcw_ref[...] = per_band[:, 1:2] * placed[3:4, :]

    lane = lanes(8)
    place_in = (nn_dot(lane_k(8), spread_ref[...]) + 0.5).astype(jnp.int32)
    back_ref[...] = (nt_dot(lane_k(8), spread_ref[...]) + 0.5).astype(jnp.int32)
    own = chunk_of(own_ref[0])
    half = own // 16
    offset = (own % 16) * YC
    for block in range(16):
        slots[block] = -1
    for k in range(16):
        @pl.when(k < count_ref[0])
        def _():
            slots[blocks_ref[0, k]] = k
    for xz in range(XZ):
        slot = slots[(xz // 4) * 8 + (xz % 4) * 2 + half]
        for y in range(YC):
            found = facet_ref[0, jnp.maximum(slot, 0), offset + y]
            facet = jnp.where(slot >= 0, found, 0)
            axis = lax.shift_right_logical(jnp.maximum(facet - 1, 0), 1)
            bit = jnp.where(facet > 0, lax.shift_right_logical(64, axis), 0)
            want = jnp.where((facet & 1) == 1, 0, bit)
            image = jnp.where((lane & bit) == want, lane ^ bit, lane)
            at = y * TILE + xz * 8
            image_ref[at : at + 8, :] = image
            first_ref[at : at + 8, :] = taken(place_in, image)


def lane_k(rows):
    return lanes(rows).astype(jnp.float32)


def pack_kernel(x_hbm, s_hbm, x_ref, s_ref, sems):
    ins = [
        pltpu.make_async_copy(
            x_hbm.at[pl.ds(own * 640, 640)], x_ref.at[pl.ds(own * 640, 640)], sems.at[own]
        )
        for own in range(OWN)
    ]
    for copy in ins:
        copy.start()
    lane = lanes(128)
    low = lane < 64
    low4 = lanes(4) < 64
    side = lane // 64
    natural = (lane % 8) * 16 + (lane // 32) % 2 * 8 + (lane // 8) % 4
    even = natural + side * 4
    odd = natural + (1 - side) * 4
    for dest in range(SRC):
        s_ref[dest * MSG + 80 : dest * MSG + 81, :] = jnp.zeros((1, DIRS), jnp.float32)
    for own in range(OWN):
        ins[own].wait()
        turned = []
        for octet in range(OCTS):
            at = own * 640 + octet * 128
            turned.append(x_ref[at : at + 128, :].T)
        for pair in range(2):
            a = taken(turned[2 * pair], even)
            b = taken(turned[2 * pair + 1], odd)
            for half, t in enumerate((jnp.where(low, a, b), jnp.where(low, b, a))):
                for jj in range(16):
                    at = SNAKE[half * 16 + jj] * MSG + pair * 32 + own * YC
                    s_ref[at : at + YC, :] = t[jj * YC : (jj + 1) * YC]
        a = taken(turned[4], even)
        b = taken(turned[4], odd)
        for half, (t, u) in enumerate(((a, b), (b, a))):
            for jj in range(16):
                at = SNAKE[half * 16 + jj] * MSG + 64 + own * 4
                y = jj * YC
                s_ref[at : at + 4, :] = jnp.where(low4, t[y : y + 4], u[y + 4 : y + 8])
    out = pltpu.make_async_copy(s_ref, s_hbm, sems.at[OWN])
    out.start()
    out.wait()


def upper_half():
    return lax.axis_index("dir").astype(jnp.int32) // 16


def store_edges(e_ref, ya_ref, yb_ref):
    pos = (lanes(TILE) & 32) == 0
    for octet in range(OCTS):
        at = octet * TILE
        row = lambda y: e_ref[y * ROW + at : y * ROW + at + TILE, :]
        ya_ref[at : at + TILE, :] = jnp.where(pos, row(6), pltpu.roll(row(7), 32, 1))
        yb_ref[at : at + TILE, :] = jnp.where(pos, pltpu.roll(row(1), 96, 1), row(0))


def store_faces(at, ay, low, a_ref, b_ref):
    e0, r1 = ay[:32], pltpu.roll(ay[32:], 64, 1)
    a_ref[pl.ds(at, 32), :] = jnp.where(low, e0, r1)
    b_ref[pl.ds(at, 32), :] = jnp.where(low, r1, e0)


def spread_kernel(r_ref, first_ref, coef_ref, e_ref, ya_ref, yb_ref, ay_ref, a_ref, b_ref, f_ref):
    swap = upper_half() * TILE
    for y in range(YC):
        for pair in range(2):
            t = jnp.concatenate(
                [
                    r_ref[pl.ds(pair * 32 + own * YC + y, SRC, stride=MSG), :]
                    for own in range(OWN)
                ],
                axis=0,
            ).T
            at = y * ROW + pair * 128
            f_ref[pl.ds(pl.multiple_of(at + swap, TILE), TILE), :] = t[:TILE]
            f_ref[pl.ds(pl.multiple_of(at + TILE - swap, TILE), TILE), :] = t[TILE:]
    for y in range(4):
        t = jnp.concatenate(
            [r_ref[pl.ds(64 + own * 4 + y, SRC, stride=MSG), :] for own in range(OWN)], axis=0
        ).T
        f_ref[y * ROW + 256 : y * ROW + 320, :] = t[:TILE]
        f_ref[(y + 4) * ROW + 256 : (y + 4) * ROW + 320, :] = t[TILE:]
    for y in range(YC):
        for xz in range(XZ):
            index = first_ref[y * TILE + xz * 8 : y * TILE + xz * 8 + 8, :]
            for octet in range(OCTS):
                at = y * ROW + octet * TILE + xz * 8
                e_ref[at : at + 8, :] = taken(f_ref[at : at + 8, :], index)
    store_edges(e_ref, ya_ref, yb_ref)
    sweep_inner(e_ref, coef_ref, ay_ref, a_ref, b_ref)


def y_coefs(coef_ref, octet):
    at = 3 * BANDS + octet * 8
    return [tiled(coef_ref[at + k * BANDS : at + k * BANDS + 8, :], XZ) for k in range(3)]


def sweep_inner(e_ref, coef_ref, ay_ref, a_ref, b_ref):
    low = lanes(32) < 64
    pos = (lanes(TILE) & 32) == 0
    for octet in range(OCTS):
        y0, y1, y2 = y_coefs(coef_ref, octet)
        for k in range(YC - 2):
            at = octet * TILE
            far, near, here = (
                e_ref[(k + j) * ROW + at : (k + j) * ROW + at + TILE, :] for j in range(3)
            )
            ay = y0 * jnp.where(pos, here, far) + y1 * near + y2 * jnp.where(pos, far, here)
            ay_ref[k * ROW + at : k * ROW + at + TILE, :] = ay
            store_faces(k * FACE + octet * 32, ay, low, a_ref, b_ref)


def outer_kernel(e_ref, ml_ref, mr_ref, coef_ref, ay_ref, a_ref, b_ref):
    low = lanes(32) < 64
    pos = (lanes(TILE) & 32) == 0
    for octet in range(OCTS):
        y0, y1, y2 = y_coefs(coef_ref, octet)
        at = octet * TILE
        row = lambda y: e_ref[y * ROW + at : y * ROW + at + TILE, :]
        ml = ml_ref[at : at + TILE, :]
        mr = mr_ref[at : at + TILE, :]
        h0 = jnp.where(pos, ml, mr)
        h1 = jnp.where(pos, pltpu.roll(ml, 96, 1), pltpu.roll(mr, 32, 1))
        e0, e7 = row(0), row(7)
        ay0 = y0 * jnp.where(pos, e0, row(6)) + y1 * jnp.where(pos, h1, e7) + y2 * h0
        ay1 = y0 * jnp.where(pos, row(1), e7) + y1 * jnp.where(pos, e0, h0) + y2 * h1
        for k, ay in enumerate((ay0, ay1)):
            ay_ref[k * ROW + at : k * ROW + at + TILE, :] = ay
            store_faces(k * FACE + octet * 32, ay, low, a_ref, b_ref)


def expm1(q):
    small = q * (1.0 + q * (1 / 2) * (1.0 + q * (1 / 3) * (1.0 + q * (1 / 4) * (
        1.0 + q * (1 / 5) * (1.0 + q * (1 / 6))))))
    return jnp.where(q < 0.25, small, jnp.exp(q) - 1.0)


def sweep_xz(count, ay_ref, ml_ref, mr_ref, coef_ref, srcw_ref, mv_ref, acc_ref):
    lane = lanes(8)
    low = lane < 64
    pos_z = (lane & 16) == 0
    acc_ref[...] = jnp.zeros_like(acc_ref)

    def one_octet(octet, carry):
        def at(pitch, offset):
            return pl.ds(pl.multiple_of(octet * pitch + offset, 8), 8)

        x0, x1, x2, z0, z1, z2 = (coef_ref[at(8, k * BANDS), :] for k in (0, 1, 2, 6, 7, 8))
        weight = srcw_ref[at(8, 0), :]
        for row in range(count):
            swept = [[], []]
            for z in range(4):
                e0 = ay_ref[at(TILE, row * ROW + z * 8), :]
                e1 = ay_ref[at(TILE, row * ROW + (4 + z) * 8), :]
                ml = ml_ref[at(32, row * FACE + z * 8), :]
                mr = mr_ref[at(32, row * FACE + z * 8), :]
                g0 = jnp.where(low, ml, mr)
                g1 = pltpu.roll(jnp.where(low, mr, ml), 64, 1)
                swept[0].append(x0 * e0 + x1 * jnp.where(low, g1, e1) + x2 * g0)
                swept[1].append(x0 * e1 + x1 * jnp.where(low, e0, g0) + x2 * g1)
            for x in range(2):
                ax = swept[x]
                for z in range(4):
                    near = jnp.where(pos_z, ax[(z + 3) % 4], ax[(z + 1) % 4])
                    mv = z0 * ax[z] + z1 * near + z2 * ax[(z + 2) % 4]
                    xz = x * 4 + z
                    mv_ref[at(TILE, row * ROW + xz * 8), :] = mv
                    cell = (row * XZ + xz) * 8
                    acc_ref[cell : cell + 8, :] += weight * mv
        return carry

    lax.fori_loop(0, OCTS, one_octet, 0)
    return acc_ref[...].reshape(count * XZ, 8, DIRS).sum(axis=1)


def mid_kernel(ay_ref, ml_ref, mr_ref, coef_ref, srcw_ref, mv_ref, sums_ref, acc_ref):
    sums_ref[...] = sweep_xz(YC - 2, ay_ref, ml_ref, mr_ref, coef_ref, srcw_ref, mv_ref, acc_ref)


def heat_of(inner_sums, outer_sums, cols_ref):
    here = jnp.concatenate([outer_sums, inner_sums], axis=0)
    turned = jnp.concatenate([inner_sums, outer_sums], axis=0)
    per_cell = jnp.where((lanes(64) & 32) == 0, here, turned)
    source = nt_dot(jnp.ones((8, DIRS), jnp.float32), per_cell)[0:1, :]
    relax = cols_ref[:, 1:2]
    heat = cols_ref[:, 2:3]
    pulse = cols_ref[:, 3:4]
    speed = relax * heat
    temp = jnp.ones((1, 64), jnp.float32)
    for _ in range(NEWTON):
        q = pulse / temp
        surplus = expm1(q)
        mismatch = jnp.sum(speed / surplus, axis=0, keepdims=True) - source
        slope = jnp.sum(
            speed * q * jnp.exp(q) / (surplus * surplus), axis=0, keepdims=True
        ) / temp
        temp = jnp.clip(temp - mismatch / slope, 0.5 * temp, 2.0 * temp)
    return temp, relax * (heat / expm1(pulse / temp))


def keep_moved(inner_ref, outer_ref, cols_ref, index_of, e_ref):
    keep = jnp.broadcast_to(1.0 - cols_ref[:, 1:2], (BANDS, DIRS))
    pos = (lanes(8) & 32) == 0

    def row(k, at):
        return outer_ref[k * ROW + at : k * ROW + at + 8, :] if k < 2 else inner_ref[
            (k - 2) * ROW + at : (k - 2) * ROW + at + 8, :
        ]

    for y in range(YC):
        for xz in range(XZ):
            index = index_of(y, xz)
            for octet in range(OCTS):
                at = octet * TILE + xz * 8
                moved = jnp.where(pos, row(y, at), row((y + 2) % YC, at))
                e_ref[y * ROW + at : y * ROW + at + 8, :] = taken(
                    keep[octet * 8 : (octet + 1) * 8] * moved, index
                )


def add_heat(eq, e_ref):
    for y in range(YC):
        for octet in range(OCTS):
            at = y * ROW + octet * TILE
            heat = jnp.concatenate(
                [
                    jnp.broadcast_to(
                        eq[octet * 8 : (octet + 1) * 8, y * XZ + xz : y * XZ + xz + 1], (8, DIRS)
                    )
                    for xz in range(XZ)
                ],
                axis=0,
            )
            e_ref[at : at + TILE, :] += heat


def step_kernel(
    mvi_ref, sums_ref, ayo_ref, mlo_ref, mro_ref, coef_ref, srcw_ref, cols_ref, image_ref,
    e_ref, ya_ref, yb_ref, ay_ref, a_ref, b_ref, mvo_ref, acc_ref,
):
    outer = sweep_xz(2, ayo_ref, mlo_ref, mro_ref, coef_ref, srcw_ref, mvo_ref, acc_ref)

    def index_of(y, xz):
        return image_ref[y * TILE + xz * 8 : y * TILE + xz * 8 + 8, :]

    keep_moved(mvi_ref, mvo_ref, cols_ref, index_of, e_ref)
    _, eq = heat_of(sums_ref[...], outer, cols_ref)
    add_heat(eq, e_ref)
    store_edges(e_ref, ya_ref, yb_ref)
    sweep_inner(e_ref, coef_ref, ay_ref, a_ref, b_ref)


def last_kernel(
    mvi_ref, sums_ref, ayo_ref, mlo_ref, mro_ref, coef_ref, srcw_ref, cols_ref, back_ref,
    s_ref, mvo_ref, acc_ref, e_ref,
):
    outer = sweep_xz(2, ayo_ref, mlo_ref, mro_ref, coef_ref, srcw_ref, mvo_ref, acc_ref)
    index = back_ref[...]
    keep_moved(mvi_ref, mvo_ref, cols_ref, lambda y, xz: index, e_ref)
    temp, eq = heat_of(sums_ref[...], outer, cols_ref)
    wide = jnp.concatenate([temp, jnp.zeros((1, DIRS - 64), jnp.float32)], axis=1)
    s_ref[pl.ds(80, SRC, stride=MSG), :] = jnp.broadcast_to(wide, (SRC, DIRS))
    add_heat(eq, e_ref)
    swap = upper_half() * TILE
    for y in range(YC):
        for pair in range(2):
            at = y * ROW + pair * 128
            t = jnp.concatenate(
                [
                    e_ref[pl.ds(pl.multiple_of(at + swap, TILE), TILE), :],
                    e_ref[pl.ds(pl.multiple_of(at + TILE - swap, TILE), TILE), :],
                ],
                axis=0,
            ).T
            for own in range(OWN):
                s_ref[pl.ds(pair * 32 + own * YC + y, SRC, stride=MSG), :] = t[
                    own * SRC : (own + 1) * SRC
                ]
    for y in range(4):
        t = jnp.concatenate(
            [e_ref[k * ROW + 256 : k * ROW + 320, :] for k in (y, y + 4)], axis=0
        ).T
        for own in range(OWN):
            s_ref[pl.ds(64 + own * 4 + y, SRC, stride=MSG), :] = t[own * SRC : (own + 1) * SRC]


def unpack_kernel(r_ref, x_hbm, t_ref, x_ref, sems):
    lane = lanes(128)
    low = lane < 64
    half_of = (lane // 4) % 2
    cell = ((lane // 8) % 2 * 4 + lane % 4) * 8 + lane // 16
    even = cell + half_of * 64
    odd = cell + (1 - half_of) * 64
    upper = lax.broadcasted_iota(jnp.int32, (128, DIRS), 0) % 8 // 4
    rest = cell + upper * 64
    copies = []
    for own in range(OWN):

        def finish(octet, x):
            at = own * 640 + octet * 128
            x_ref[at : at + 128, :] = x.T

        for pair in range(2):
            b0, b1 = (
                jnp.concatenate(
                    [
                        r_ref[at : at + YC, :]
                        for jj in range(16)
                        for at in [SNAKE[half * 16 + jj] * MSG + pair * 32 + own * YC]
                    ],
                    axis=0,
                )
                for half in range(2)
            )
            finish(2 * pair, taken(jnp.where(low, b0, b1), even))
            finish(2 * pair + 1, taken(jnp.where(low, b1, b0), odd))
        fours = []
        for half in range(2):
            rows = []
            for jj in range(16):
                at = SNAKE[half * 16 + jj] * MSG + 64 + own * 4
                four = r_ref[at : at + 4, :]
                rows += [four, four]
            fours.append(taken(jnp.concatenate(rows, axis=0), rest))
        finish(4, jnp.where(half_of == 0, fours[0], fours[1]))
        part = pl.ds(own * 640, 640)
        copies.append(pltpu.make_async_copy(x_ref.at[part], x_hbm.at[part], sems.at[own]))
        copies[own].start()
    lane = lanes(16)
    here = lane // 8 == chunk_of(lax.broadcasted_iota(jnp.int32, (16, DIRS), 0))
    for half in range(2):
        temps = r_ref[pl.ds(half * 16 * MSG + 80, 16, stride=MSG), :]
        for xz in range(XZ):
            spread = jnp.where(here, taken(temps, lane % 8 * XZ + xz), 0.0)
            t_ref[xz // 4, xz % 4 : xz % 4 + 1, half * 128 : (half + 1) * 128] = jnp.sum(
                spread, axis=0, keepdims=True
            )
    for copy in copies:
        copy.wait()


def f32(*shape):
    return pltpu.VMEM(shape, jnp.float32)


VMEM = pl.BlockSpec(memory_space=pltpu.VMEM)
SMEM = pl.BlockSpec(memory_space=pltpu.SMEM)
ANY = pl.BlockSpec(memory_space=pltpu.HBM)


def call(kernel, in_specs, out_shape, scratch=(), out_specs=None, name=None, cost=None):
    if out_specs is None:
        out_specs = tuple(VMEM for _ in out_shape) if isinstance(out_shape, tuple) else VMEM

    def run(*args):
        args = [
            a if s is SMEM else pltpu.with_memory_space_constraint(a, s.memory_space)
            for a, s in zip(args, in_specs)
        ]
        return pl.pallas_call(
            kernel,
            in_specs=in_specs,
            out_specs=out_specs,
            out_shape=out_shape,
            scratch_shapes=list(scratch),
            compiler_params=pltpu.CompilerParams(vmem_limit_bytes=24 << 20),
            cost_estimate=cost,
            name=name,
        )(*args)

    return run


MID_COST = pl.CostEstimate(flops=7_000_000, transcendentals=0, bytes_accessed=4_000_000)


def exchanged(messages):
    whole = messages.reshape(SRC, 1, MSG * DIRS)
    return lax.all_to_all(whole, "dir", 0, 0, tiled=True).reshape(SENT, DIRS)


def both_ways(up, down, axis):
    order = SNAKE if axis == "dir" else list(range(lax.axis_size(axis)))
    right = list(zip(order, order[1:] + order[:1]))
    left = [(j, i) for i, j in right]
    return lax.ppermute(up, axis, right), lax.ppermute(down, axis, left)


def on_device(
    phonon_heat_density,
    directions,
    quad_weight,
    mirror,
    band_courant,
    relax_rate,
    mode_heat_magnitude,
    mode_pulsation,
    wall_blocks,
    wall_count,
    wall_facet,
):
    own = lax.axis_index("dir").astype(jnp.int32).reshape(1)
    bands = jnp.stack([band_courant, relax_rate, mode_heat_magnitude, mode_pulsation])
    bands = jnp.concatenate([bands, jnp.zeros_like(bands)])
    x2 = phonon_heat_density.reshape(OWN, BANDS, 2, 4, 2, 128)
    x2 = x2.transpose(0, 1, 2, 4, 3, 5).reshape(2560, 128)
    whole = pltpu.VMEM((2560, 128), jnp.float32)
    packed = call(
        pack_kernel, [ANY], jax.ShapeDtypeStruct((SENT, 128), jnp.float32),
        [whole, pltpu.VMEM((SENT, 128), jnp.float32), pltpu.SemaphoreType.DMA((OWN + 1,))], ANY,
        name="pack",
    )(x2)
    index = pltpu.VMEM((YC * TILE, 128), jnp.int32)
    coef, srcw, cols, first, image, place = call(
        tables_kernel,
        [VMEM] * 4 + [SMEM] * 4,
        (f32(360, 128), f32(40, 128), f32(40, 8), index, index, pltpu.VMEM((8, 128), jnp.int32)),
        [pltpu.VMEM((8, 128), jnp.float32), pltpu.VMEM((128, 128), jnp.float32),
         pltpu.VMEM((128, 128), jnp.float32), pltpu.SMEM((16,), jnp.int32)],
        name="tables",
    )(directions, quad_weight.reshape(1, 128), mirror, bands, own, wall_blocks, wall_count,
      wall_facet)
    met = exchanged(packed)
    field = f32(2560, 128)
    edge = f32(ROW, 128)
    swept_inner = (f32(6 * ROW, 128), f32(6 * FACE, 128), f32(6 * FACE, 128))
    e, ya, yb, ayi, a, b = call(
        spread_kernel, [VMEM] * 3, (field, edge, edge, *swept_inner), [whole], name="spread"
    )(met, first, coef)
    work = [pltpu.VMEM((2 * ROW, 128), jnp.float32), pltpu.VMEM((128, 128), jnp.float32)]
    for step in range(2):
        yl, yr = both_ways(ya, yb, "dir")
        mli, mri = both_ways(a, b, "space")
        ayo, a, b = call(
            outer_kernel, [VMEM] * 4, (f32(2 * ROW, 128), edge, edge), name="outer"
        )(e, yl, yr, coef)
        mlo, mro = both_ways(a, b, "space")
        moved, sums = call(
            mid_kernel, [VMEM] * 5, (f32(6 * ROW, 128), f32(48, 128)),
            [pltpu.VMEM((384, 128), jnp.float32)], name="mid", cost=MID_COST,
        )(ayi, mli, mri, coef, srcw)
        swept = (moved, sums, ayo, mlo, mro, coef, srcw, cols)
        if step == 0:
            e, ya, yb, ayi, a, b = call(
                step_kernel, [VMEM] * 9, (field, edge, edge, *swept_inner), work, name="step"
            )(*swept, image)
        else:
            out = call(
                last_kernel, [VMEM] * 9, f32(SENT, 128), work + [whole], name="last"
            )(*swept, place)
    x2, temp = call(
        unpack_kernel,
        [VMEM],
        (jax.ShapeDtypeStruct((2560, 128), jnp.float32),
         jax.ShapeDtypeStruct((2, 4, 256), jnp.float32)),
        [whole, pltpu.SemaphoreType.DMA((OWN,))],
        (ANY, VMEM),
        name="unpack",
    )(exchanged(out))
    energy = x2.reshape(OWN, BANDS, 2, 2, 4, 128).transpose(0, 1, 2, 4, 3, 5)
    return energy.reshape(phonon_heat_density.shape), temp


def solution(mesh):
    in_specs = (
        P("dir", None, "space", None, None),
        P(),
        P(),
        P(),
        P(),
        P(),
        P(),
        P(),
        P("space", None),
        P("space"),
        P("space", None, None),
    )
    out_specs = (P("dir", None, "space", None, None), P("space", None, None))
    return jax.shard_map(
        on_device, mesh=mesh, in_specs=in_specs, out_specs=out_specs, check_vma=False
    )
```

```python
import jax
import jax.numpy as jnp
from jax import lax
from jax.experimental import pallas as pl
from jax.experimental.pallas import tpu as pltpu
from jax.sharding import PartitionSpec as P

NEWTON = 4
BANDS = 40
OCTS = 5
DIRS = 128
SRC = 32
OWN = 4
YC = 8
XZ = 8
TILE = XZ * 8
ROW = OCTS * TILE
FACE = ROW // 2
MSG = 81
SENT = SRC * MSG
HI = lax.Precision.HIGHEST
NT = (((1,), (1,)), ((), ()))


def nt_dot(a, b):
    return lax.dot_general(a, b, NT, precision=HI, preferred_element_type=jnp.float32)


def nn_dot(a, b):
    return jnp.dot(a, b, precision=HI, preferred_element_type=jnp.float32)


SNAKE = [c // 4 * 4 + (c % 4 if c // 4 % 2 == 0 else 3 - c % 4) for c in range(SRC)]


def chunk_of(device):
    along, across = device // 4, device % 4
    return along * 4 + jnp.where(along % 2 == 0, across, 3 - across)


def lanes(rows):
    return lax.broadcasted_iota(jnp.int32, (rows, DIRS), 1)


def taken(x, index):
    return jnp.take_along_axis(x, index, axis=1)


def tiled(x, count):
    return jnp.concatenate([x] * count, axis=0)


def tables_kernel(
    dirs_ref, weight_ref, mirror_ref, bands_ref, own_ref, blocks_ref, count_ref, facet_ref,
    coef_ref, srcw_ref, cols_ref, first_ref, image_ref, back_ref, tmp, tmp2, spread_ref, slots,
):
    eye = (lax.broadcasted_iota(jnp.int32, (DIRS, DIRS), 0) == lanes(DIRS)).astype(jnp.float32)
    dirs = dirs_ref[...]
    tmp[...] = jnp.zeros_like(tmp)
    tmp[0:3, :] = (dirs < 0).astype(jnp.float32)
    tmp[3:6, :] = mirror_ref[...].astype(jnp.float32)
    cols = nt_dot(eye, tmp[...])
    lane_f = lanes(DIRS).astype(jnp.float32)
    rep = eye
    for axis in range(3):
        image = (cols[:, 3 + axis : 4 + axis] == lane_f).astype(jnp.float32)
        rep = jnp.where(cols[:, axis : axis + 1] > 0.5, nn_dot(rep, image), rep)
    negs = cols[:, 0:1] + cols[:, 1:2] + cols[:, 2:3]
    positive = jnp.broadcast_to((negs < 0.5).astype(jnp.float32), (DIRS, DIRS))
    below = (lax.broadcasted_iota(jnp.int32, (DIRS, DIRS), 0) > lanes(DIRS)).astype(jnp.float32)
    rank = nn_dot(rep, nn_dot(below, positive))
    place = 64.0 * cols[:, 0:1] + 32.0 * cols[:, 1:2] + 16.0 * cols[:, 2:3] + rank
    tmp2[...] = (place == lane_f).astype(jnp.float32)
    for own in range(OWN):
        spread_ref[own * SRC : (own + 1) * SRC, :] = tmp2[pl.ds(own, SRC, stride=OWN), :]
    tmp[0:3, :] = jnp.abs(dirs)
    tmp[3:4, :] = weight_ref[...]
    placed = nn_dot(tmp[...], tmp2[...])
    eye_b = (
        lax.broadcasted_iota(jnp.int32, (BANDS, BANDS), 0)
        == lax.broadcasted_iota(jnp.int32, (BANDS, BANDS), 1)
    ).astype(jnp.float32)
    per_band = nt_dot(eye_b, bands_ref[...])
    cols_ref[...] = per_band
    courant = per_band[:, 0:1]
    for axis in range(3):
        s = courant * placed[axis : axis + 1, :]
        at = axis * 3 * BANDS
        coef_ref[at : at + BANDS, :] = 1.0 - 1.5 * s + 0.5 * s * s
        coef_ref[at + BANDS : at + 2 * BANDS, :] = 2.0 * s - s * s
        coef_ref[at + 2 * BANDS : at + 3 * BANDS, :] = 0.5 * s * s - 0.5 * s
    srcw_ref[...] = per_band[:, 1:2] * placed[3:4, :]

    lane = lanes(8)
    place_in = (nn_dot(lane_k(8), spread_ref[...]) + 0.5).astype(jnp.int32)
    back_ref[...] = (nt_dot(lane_k(8), spread_ref[...]) + 0.5).astype(jnp.int32)
    own = chunk_of(own_ref[0])
    half = own // 16
    offset = (own % 16) * YC
    for block in range(16):
        slots[block] = -1
    for k in range(16):
        @pl.when(k < count_ref[0])
        def _():
            slots[blocks_ref[0, k]] = k
    for xz in range(XZ):
        slot = slots[(xz // 4) * 8 + (xz % 4) * 2 + half]
        for y in range(YC):
            found = facet_ref[0, jnp.maximum(slot, 0), offset + y]
            facet = jnp.where(slot >= 0, found, 0)
            axis = lax.shift_right_logical(jnp.maximum(facet - 1, 0), 1)
            bit = jnp.where(facet > 0, lax.shift_right_logical(64, axis), 0)
            want = jnp.where((facet & 1) == 1, 0, bit)
            image = jnp.where((lane & bit) == want, lane ^ bit, lane)
            at = y * TILE + xz * 8
            image_ref[at : at + 8, :] = image
            first_ref[at : at + 8, :] = taken(place_in, image)


def lane_k(rows):
    return lanes(rows).astype(jnp.float32)


def pack_kernel(x_hbm, s_hbm, x_ref, s_ref, sems):
    ins = [
        pltpu.make_async_copy(
            x_hbm.at[pl.ds(own * 640, 640)], x_ref.at[pl.ds(own * 640, 640)], sems.at[own]
        )
        for own in range(OWN)
    ]
    for copy in ins:
        copy.start()
    lane = lanes(128)
    low = lane < 64
    low4 = lanes(4) < 64
    side = lane // 64
    natural = (lane % 8) * 16 + (lane // 32) % 2 * 8 + (lane // 8) % 4
    even = natural + side * 4
    odd = natural + (1 - side) * 4
    for dest in range(SRC):
        s_ref[dest * MSG + 80 : dest * MSG + 81, :] = jnp.zeros((1, DIRS), jnp.float32)
    for own in range(OWN):
        ins[own].wait()
        turned = []
        for octet in range(OCTS):
            at = own * 640 + octet * 128
            turned.append(x_ref[at : at + 128, :].T)
        for pair in range(2):
            a = taken(turned[2 * pair], even)
            b = taken(turned[2 * pair + 1], odd)
            for half, t in enumerate((jnp.where(low, a, b), jnp.where(low, b, a))):
                for jj in range(16):
                    at = SNAKE[half * 16 + jj] * MSG + pair * 32 + own * YC
                    s_ref[at : at + YC, :] = t[jj * YC : (jj + 1) * YC]
        a = taken(turned[4], even)
        b = taken(turned[4], odd)
        for half, (t, u) in enumerate(((a, b), (b, a))):
            for jj in range(16):
                at = SNAKE[half * 16 + jj] * MSG + 64 + own * 4
                y = jj * YC
                s_ref[at : at + 4, :] = jnp.where(low4, t[y : y + 4], u[y + 4 : y + 8])
    out = pltpu.make_async_copy(s_ref, s_hbm, sems.at[OWN])
    out.start()
    out.wait()


def upper_half():
    return lax.axis_index("dir").astype(jnp.int32) // 16


def store_edges(e_ref, ya_ref, yb_ref):
    pos = (lanes(TILE) & 32) == 0
    for octet in range(OCTS):
        at = octet * TILE
        row = lambda y: e_ref[y * ROW + at : y * ROW + at + TILE, :]
        ya_ref[at : at + TILE, :] = jnp.where(pos, row(6), pltpu.roll(row(7), 32, 1))
        yb_ref[at : at + TILE, :] = jnp.where(pos, pltpu.roll(row(1), 96, 1), row(0))


def store_faces(at, ay, low, a_ref, b_ref):
    e0, r1 = ay[:32], pltpu.roll(ay[32:], 64, 1)
    a_ref[pl.ds(at, 32), :] = jnp.where(low, e0, r1)
    b_ref[pl.ds(at, 32), :] = jnp.where(low, r1, e0)


def spread_kernel(r_ref, first_ref, coef_ref, e_ref, ya_ref, yb_ref, ay_ref, a_ref, b_ref, f_ref):
    swap = upper_half() * TILE
    for y in range(YC):
        for pair in range(2):
            t = jnp.concatenate(
                [
                    r_ref[pl.ds(pair * 32 + own * YC + y, SRC, stride=MSG), :]
                    for own in range(OWN)
                ],
                axis=0,
            ).T
            at = y * ROW + pair * 128
            f_ref[pl.ds(pl.multiple_of(at + swap, TILE), TILE), :] = t[:TILE]
            f_ref[pl.ds(pl.multiple_of(at + TILE - swap, TILE), TILE), :] = t[TILE:]
    for y in range(4):
        t = jnp.concatenate(
            [r_ref[pl.ds(64 + own * 4 + y, SRC, stride=MSG), :] for own in range(OWN)], axis=0
        ).T
        f_ref[y * ROW + 256 : y * ROW + 320, :] = t[:TILE]
        f_ref[(y + 4) * ROW + 256 : (y + 4) * ROW + 320, :] = t[TILE:]
    for y in range(YC):
        for xz in range(XZ):
            index = first_ref[y * TILE + xz * 8 : y * TILE + xz * 8 + 8, :]
            for octet in range(OCTS):
                at = y * ROW + octet * TILE + xz * 8
                e_ref[at : at + 8, :] = taken(f_ref[at : at + 8, :], index)
    store_edges(e_ref, ya_ref, yb_ref)
    sweep_inner(e_ref, coef_ref, ay_ref, a_ref, b_ref)


def y_coefs(coef_ref, octet):
    at = 3 * BANDS + octet * 8
    return [tiled(coef_ref[at + k * BANDS : at + k * BANDS + 8, :], XZ) for k in range(3)]


def sweep_inner(e_ref, coef_ref, ay_ref, a_ref, b_ref):
    low = lanes(32) < 64
    pos = (lanes(TILE) & 32) == 0
    for octet in range(OCTS):
        y0, y1, y2 = y_coefs(coef_ref, octet)
        for k in range(YC - 2):
            at = octet * TILE
            far, near, here = (
                e_ref[(k + j) * ROW + at : (k + j) * ROW + at + TILE, :] for j in range(3)
            )
            ay = y0 * jnp.where(pos, here, far) + y1 * near + y2 * jnp.where(pos, far, here)
            ay_ref[k * ROW + at : k * ROW + at + TILE, :] = ay
            store_faces(k * FACE + octet * 32, ay, low, a_ref, b_ref)


def outer_kernel(e_ref, ml_ref, mr_ref, coef_ref, ay_ref, a_ref, b_ref):
    low = lanes(32) < 64
    pos = (lanes(TILE) & 32) == 0
    for octet in range(OCTS):
        y0, y1, y2 = y_coefs(coef_ref, octet)
        at = octet * TILE
        row = lambda y: e_ref[y * ROW + at : y * ROW + at + TILE, :]
        ml = ml_ref[at : at + TILE, :]
        mr = mr_ref[at : at + TILE, :]
        h0 = jnp.where(pos, ml, mr)
        h1 = jnp.where(pos, pltpu.roll(ml, 96, 1), pltpu.roll(mr, 32, 1))
        e0, e7 = row(0), row(7)
        ay0 = y0 * jnp.where(pos, e0, row(6)) + y1 * jnp.where(pos, h1, e7) + y2 * h0
        ay1 = y0 * jnp.where(pos, row(1), e7) + y1 * jnp.where(pos, e0, h0) + y2 * h1
        for k, ay in enumerate((ay0, ay1)):
            ay_ref[k * ROW + at : k * ROW + at + TILE, :] = ay
            store_faces(k * FACE + octet * 32, ay, low, a_ref, b_ref)


def expm1(q):
    small = q * (1.0 + q * (1 / 2) * (1.0 + q * (1 / 3) * (1.0 + q * (1 / 4) * (
        1.0 + q * (1 / 5) * (1.0 + q * (1 / 6))))))
    return jnp.where(q < 0.25, small, jnp.exp(q) - 1.0)


def sweep_xz(count, ay_ref, ml_ref, mr_ref, coef_ref, srcw_ref, mv_ref, acc_ref):
    lane = lanes(8)
    low = lane < 64
    pos_z = (lane & 16) == 0
    acc_ref[...] = jnp.zeros_like(acc_ref)

    def one_octet(octet, carry):
        def at(pitch, offset):
            return pl.ds(pl.multiple_of(octet * pitch + offset, 8), 8)

        x0, x1, x2, z0, z1, z2 = (coef_ref[at(8, k * BANDS), :] for k in (0, 1, 2, 6, 7, 8))
        weight = srcw_ref[at(8, 0), :]
        for row in range(count):
            swept = [[], []]
            for z in range(4):
                e0 = ay_ref[at(TILE, row * ROW + z * 8), :]
                e1 = ay_ref[at(TILE, row * ROW + (4 + z) * 8), :]
                ml = ml_ref[at(32, row * FACE + z * 8), :]
                mr = mr_ref[at(32, row * FACE + z * 8), :]
                g0 = jnp.where(low, ml, mr)
                g1 = pltpu.roll(jnp.where(low, mr, ml), 64, 1)
                swept[0].append(x0 * e0 + x1 * jnp.where(low, g1, e1) + x2 * g0)
                swept[1].append(x0 * e1 + x1 * jnp.where(low, e0, g0) + x2 * g1)
            for x in range(2):
                ax = swept[x]
                for z in range(4):
                    near = jnp.where(pos_z, ax[(z + 3) % 4], ax[(z + 1) % 4])
                    mv = z0 * ax[z] + z1 * near + z2 * ax[(z + 2) % 4]
                    xz = x * 4 + z
                    mv_ref[at(TILE, row * ROW + xz * 8), :] = mv
                    cell = (row * XZ + xz) * 8
                    acc_ref[cell : cell + 8, :] += weight * mv
        return carry

    lax.fori_loop(0, OCTS, one_octet, 0)
    return acc_ref[...].reshape(count * XZ, 8, DIRS).sum(axis=1)


def keep_moved(ys, first, row, cols_ref, index_of, e_ref):
    keep = jnp.broadcast_to(1.0 - cols_ref[:, 1:2], (BANDS, DIRS))
    pos = (lanes(8) & 32) == 0
    for y in ys:
        for xz in range(XZ):
            index = index_of(y, xz)
            for octet in range(OCTS):
                at = octet * TILE + xz * 8
                moved = jnp.where(pos, row(y, at), row((y + 2) % YC, at))
                out = (y - first) * ROW + at
                e_ref[out : out + 8, :] = taken(keep[octet * 8 : (octet + 1) * 8] * moved, index)


def index_from(index_ref):
    if index_ref.shape[0] == 8:
        index = index_ref[...]
        return lambda y, xz: index
    return lambda y, xz: index_ref[y * TILE + xz * 8 : y * TILE + xz * 8 + 8, :]


def mid_kernel(
    ay_ref, ml_ref, mr_ref, coef_ref, srcw_ref, cols_ref, index_ref,
    mv_ref, sums_ref, e_ref, acc_ref,
):
    sums_ref[...] = sweep_xz(YC - 2, ay_ref, ml_ref, mr_ref, coef_ref, srcw_ref, mv_ref, acc_ref)
    row = lambda k, at: mv_ref[(k - 2) * ROW + at : (k - 2) * ROW + at + 8, :]
    keep_moved(range(2, 6), 2, row, cols_ref, index_from(index_ref), e_ref)


def heat_of(inner_sums, outer_sums, cols_ref):
    here = jnp.concatenate([outer_sums, inner_sums], axis=0)
    turned = jnp.concatenate([inner_sums, outer_sums], axis=0)
    per_cell = jnp.where((lanes(64) & 32) == 0, here, turned)
    source = nt_dot(jnp.ones((8, DIRS), jnp.float32), per_cell)[0:1, :]
    relax = cols_ref[:, 1:2]
    heat = cols_ref[:, 2:3]
    pulse = cols_ref[:, 3:4]
    speed = relax * heat
    temp = jnp.ones((1, 64), jnp.float32)
    for _ in range(NEWTON):
        q = pulse / temp
        surplus = expm1(q)
        mismatch = jnp.sum(speed / surplus, axis=0, keepdims=True) - source
        slope = jnp.sum(
            speed * q * jnp.exp(q) / (surplus * surplus), axis=0, keepdims=True
        ) / temp
        temp = jnp.clip(temp - mismatch / slope, 0.5 * temp, 2.0 * temp)
    return temp, relax * (heat / expm1(pulse / temp))


def keep_moved_rest(inner_ref, outer_ref, cols_ref, index_ref, e_ref):
    def row(k, at):
        return outer_ref[k * ROW + at : k * ROW + at + 8, :] if k < 2 else inner_ref[
            (k - 2) * ROW + at : (k - 2) * ROW + at + 8, :
        ]

    keep_moved((0, 1, 6, 7), 0, row, cols_ref, index_from(index_ref), e_ref)


def add_heat(eq, mid_ref, e_ref):
    for y in range(YC):
        for octet in range(OCTS):
            at = y * ROW + octet * TILE
            heat = jnp.concatenate(
                [
                    jnp.broadcast_to(
                        eq[octet * 8 : (octet + 1) * 8, y * XZ + xz : y * XZ + xz + 1], (8, DIRS)
                    )
                    for xz in range(XZ)
                ],
                axis=0,
            )
            kept = mid_ref[at - 2 * ROW : at - 2 * ROW + TILE, :] if 2 <= y < 6 else e_ref[
                at : at + TILE, :
            ]
            e_ref[at : at + TILE, :] = kept + heat


def step_kernel(
    mvi_ref, sums_ref, mid_ref, ayo_ref, mlo_ref, mro_ref, coef_ref, srcw_ref, cols_ref, image_ref,
    e_ref, ya_ref, yb_ref, ay_ref, a_ref, b_ref, mvo_ref, acc_ref,
):
    outer = sweep_xz(2, ayo_ref, mlo_ref, mro_ref, coef_ref, srcw_ref, mvo_ref, acc_ref)
    keep_moved_rest(mvi_ref, mvo_ref, cols_ref, image_ref, e_ref)
    _, eq = heat_of(sums_ref[...], outer, cols_ref)
    add_heat(eq, mid_ref, e_ref)
    store_edges(e_ref, ya_ref, yb_ref)
    sweep_inner(e_ref, coef_ref, ay_ref, a_ref, b_ref)


def last_kernel(
    mvi_ref, sums_ref, mid_ref, ayo_ref, mlo_ref, mro_ref, coef_ref, srcw_ref, cols_ref, back_ref,
    s_ref, mvo_ref, acc_ref, e_ref,
):
    outer = sweep_xz(2, ayo_ref, mlo_ref, mro_ref, coef_ref, srcw_ref, mvo_ref, acc_ref)
    keep_moved_rest(mvi_ref, mvo_ref, cols_ref, back_ref, e_ref)
    temp, eq = heat_of(sums_ref[...], outer, cols_ref)
    wide = jnp.concatenate([temp, jnp.zeros((1, DIRS - 64), jnp.float32)], axis=1)
    s_ref[pl.ds(80, SRC, stride=MSG), :] = jnp.broadcast_to(wide, (SRC, DIRS))
    add_heat(eq, mid_ref, e_ref)
    swap = upper_half() * TILE
    for y in range(YC):
        for pair in range(2):
            at = y * ROW + pair * 128
            t = jnp.concatenate(
                [
                    e_ref[pl.ds(pl.multiple_of(at + swap, TILE), TILE), :],
                    e_ref[pl.ds(pl.multiple_of(at + TILE - swap, TILE), TILE), :],
                ],
                axis=0,
            ).T
            for own in range(OWN):
                s_ref[pl.ds(pair * 32 + own * YC + y, SRC, stride=MSG), :] = t[
                    own * SRC : (own + 1) * SRC
                ]
    for y in range(4):
        t = jnp.concatenate(
            [e_ref[k * ROW + 256 : k * ROW + 320, :] for k in (y, y + 4)], axis=0
        ).T
        for own in range(OWN):
            s_ref[pl.ds(64 + own * 4 + y, SRC, stride=MSG), :] = t[own * SRC : (own + 1) * SRC]


def unpack_kernel(r_ref, x_hbm, t_ref, x_ref, sems):
    lane = lanes(128)
    low = lane < 64
    half_of = (lane // 4) % 2
    cell = ((lane // 8) % 2 * 4 + lane % 4) * 8 + lane // 16
    even = cell + half_of * 64
    odd = cell + (1 - half_of) * 64
    upper = lax.broadcasted_iota(jnp.int32, (128, DIRS), 0) % 8 // 4
    rest = cell + upper * 64
    copies = []
    for own in range(OWN):

        def finish(octet, x):
            at = own * 640 + octet * 128
            x_ref[at : at + 128, :] = x.T

        for pair in range(2):
            b0, b1 = (
                jnp.concatenate(
                    [
                        r_ref[at : at + YC, :]
                        for jj in range(16)
                        for at in [SNAKE[half * 16 + jj] * MSG + pair * 32 + own * YC]
                    ],
                    axis=0,
                )
                for half in range(2)
            )
            finish(2 * pair, taken(jnp.where(low, b0, b1), even))
            finish(2 * pair + 1, taken(jnp.where(low, b1, b0), odd))
        fours = []
        for half in range(2):
            rows = []
            for jj in range(16):
                at = SNAKE[half * 16 + jj] * MSG + 64 + own * 4
                four = r_ref[at : at + 4, :]
                rows += [four, four]
            fours.append(taken(jnp.concatenate(rows, axis=0), rest))
        finish(4, jnp.where(half_of == 0, fours[0], fours[1]))
        part = pl.ds(own * 640, 640)
        copies.append(pltpu.make_async_copy(x_ref.at[part], x_hbm.at[part], sems.at[own]))
        copies[own].start()
    lane = lanes(16)
    here = lane // 8 == chunk_of(lax.broadcasted_iota(jnp.int32, (16, DIRS), 0))
    for half in range(2):
        temps = r_ref[pl.ds(half * 16 * MSG + 80, 16, stride=MSG), :]
        for xz in range(XZ):
            spread = jnp.where(here, taken(temps, lane % 8 * XZ + xz), 0.0)
            t_ref[xz // 4, xz % 4 : xz % 4 + 1, half * 128 : (half + 1) * 128] = jnp.sum(
                spread, axis=0, keepdims=True
            )
    for copy in copies:
        copy.wait()


def f32(*shape):
    return pltpu.VMEM(shape, jnp.float32)


VMEM = pl.BlockSpec(memory_space=pltpu.VMEM)
SMEM = pl.BlockSpec(memory_space=pltpu.SMEM)
ANY = pl.BlockSpec(memory_space=pltpu.HBM)


def call(kernel, in_specs, out_shape, scratch=(), out_specs=None, name=None, cost=None):
    if out_specs is None:
        out_specs = tuple(VMEM for _ in out_shape) if isinstance(out_shape, tuple) else VMEM

    def run(*args):
        args = [
            a if s is SMEM else pltpu.with_memory_space_constraint(a, s.memory_space)
            for a, s in zip(args, in_specs)
        ]
        return pl.pallas_call(
            kernel,
            in_specs=in_specs,
            out_specs=out_specs,
            out_shape=out_shape,
            scratch_shapes=list(scratch),
            compiler_params=pltpu.CompilerParams(vmem_limit_bytes=24 << 20),
            cost_estimate=cost,
            name=name,
        )(*args)

    return run


OUTER_COST = pl.CostEstimate(flops=2_000_000_000, transcendentals=0, bytes_accessed=0)
MID_COST = pl.CostEstimate(flops=7_000_000, transcendentals=0, bytes_accessed=4_000_000)


def exchanged(messages):
    whole = messages.reshape(SRC, 1, MSG * DIRS)
    return lax.all_to_all(whole, "dir", 0, 0, tiled=True).reshape(SENT, DIRS)


def both_ways(up, down, axis):
    order = SNAKE if axis == "dir" else list(range(lax.axis_size(axis)))
    right = list(zip(order, order[1:] + order[:1]))
    left = [(j, i) for i, j in right]
    return lax.ppermute(up, axis, right), lax.ppermute(down, axis, left)


def on_device(
    phonon_heat_density,
    directions,
    quad_weight,
    mirror,
    band_courant,
    relax_rate,
    mode_heat_magnitude,
    mode_pulsation,
    wall_blocks,
    wall_count,
    wall_facet,
):
    own = lax.axis_index("dir").astype(jnp.int32).reshape(1)
    bands = jnp.stack([band_courant, relax_rate, mode_heat_magnitude, mode_pulsation])
    bands = jnp.concatenate([bands, jnp.zeros_like(bands)])
    x2 = phonon_heat_density.reshape(OWN, BANDS, 2, 4, 2, 128)
    x2 = x2.transpose(0, 1, 2, 4, 3, 5).reshape(2560, 128)
    whole = pltpu.VMEM((2560, 128), jnp.float32)
    packed = call(
        pack_kernel, [ANY], jax.ShapeDtypeStruct((SENT, 128), jnp.float32),
        [whole, pltpu.VMEM((SENT, 128), jnp.float32), pltpu.SemaphoreType.DMA((OWN + 1,))], ANY,
        name="pack",
    )(x2)
    table = pltpu.VMEM((YC * TILE, 128), jnp.int32)
    coef, srcw, cols, first, image, place = call(
        tables_kernel,
        [VMEM] * 4 + [SMEM] * 4,
        (f32(360, 128), f32(40, 128), f32(40, 8), table, table, pltpu.VMEM((8, 128), jnp.int32)),
        [pltpu.VMEM((8, 128), jnp.float32), pltpu.VMEM((128, 128), jnp.float32),
         pltpu.VMEM((128, 128), jnp.float32), pltpu.SMEM((16,), jnp.int32)],
        name="tables",
    )(directions, quad_weight.reshape(1, 128), mirror, bands, own, wall_blocks, wall_count,
      wall_facet)
    met = exchanged(packed)
    field = f32(2560, 128)
    edge = f32(ROW, 128)
    swept_inner = (f32(6 * ROW, 128), f32(6 * FACE, 128), f32(6 * FACE, 128))
    e, ya, yb, ayi, a, b = call(
        spread_kernel, [VMEM] * 3, (field, edge, edge, *swept_inner), [whole], name="spread"
    )(met, first, coef)
    work = [pltpu.VMEM((2 * ROW, 128), jnp.float32), pltpu.VMEM((128, 128), jnp.float32)]
    for step in range(2):
        yl, yr = both_ways(ya, yb, "dir")
        mli, mri = both_ways(a, b, "space")
        ayo, a, b = call(
            outer_kernel, [VMEM] * 4, (f32(2 * ROW, 128), edge, edge), name="outer", cost=OUTER_COST
        )(e, yl, yr, coef)
        mlo, mro = both_ways(a, b, "space")
        index = place if step else image
        moved, sums, mid = call(
            mid_kernel, [VMEM] * 7, (f32(6 * ROW, 128), f32(48, 128), f32(4 * ROW, 128)),
            [pltpu.VMEM((384, 128), jnp.float32)], name="mid", cost=MID_COST,
        )(ayi, mli, mri, coef, srcw, cols, index)
        swept = (moved, sums, mid, ayo, mlo, mro, coef, srcw, cols, index)
        if step == 0:
            e, ya, yb, ayi, a, b = call(
                step_kernel, [VMEM] * 10, (field, edge, edge, *swept_inner), work, name="step"
            )(*swept)
        else:
            out = call(
                last_kernel, [VMEM] * 10, f32(SENT, 128), work + [whole], name="last"
            )(*swept)
    x2, temp = call(
        unpack_kernel,
        [VMEM],
        (jax.ShapeDtypeStruct((2560, 128), jnp.float32),
         jax.ShapeDtypeStruct((2, 4, 256), jnp.float32)),
        [whole, pltpu.SemaphoreType.DMA((OWN,))],
        (ANY, VMEM),
        name="unpack",
    )(exchanged(out))
    energy = x2.reshape(OWN, BANDS, 2, 2, 4, 128).transpose(0, 1, 2, 4, 3, 5)
    return energy.reshape(phonon_heat_density.shape), temp


def solution(mesh):
    in_specs = (
        P("dir", None, "space", None, None),
        P(),
        P(),
        P(),
        P(),
        P(),
        P(),
        P(),
        P("space", None),
        P("space"),
        P("space", None, None),
    )
    out_specs = (P("dir", None, "space", None, None), P("space", None, None))
    return jax.shard_map(
        on_device, mesh=mesh, in_specs=in_specs, out_specs=out_specs, check_vma=False
    )
```

```python
import jax
import jax.numpy as jnp
from jax import lax
from jax.experimental import pallas as pl
from jax.experimental.pallas import tpu as pltpu
from jax.sharding import PartitionSpec as P

NEWTON = 4
BANDS = 40
OCTS = 5
DIRS = 128
SRC = 32
OWN = 4
YC = 8
XZ = 8
TILE = XZ * 8
ROW = OCTS * TILE
FACE = ROW // 2
MSG = 81
SENT = SRC * MSG
HI = lax.Precision.HIGHEST
NT = (((1,), (1,)), ((), ()))


def nt_dot(a, b):
    return lax.dot_general(a, b, NT, precision=HI, preferred_element_type=jnp.float32)


def nn_dot(a, b):
    return jnp.dot(a, b, precision=HI, preferred_element_type=jnp.float32)


SNAKE = [c // 4 * 4 + (c % 4 if c // 4 % 2 == 0 else 3 - c % 4) for c in range(SRC)]


def chunk_of(device):
    along, across = device // 4, device % 4
    return along * 4 + jnp.where(along % 2 == 0, across, 3 - across)


def lanes(rows):
    return lax.broadcasted_iota(jnp.int32, (rows, DIRS), 1)


def taken(x, index):
    return jnp.take_along_axis(x, index, axis=1)


def tiled(x, count):
    return jnp.concatenate([x] * count, axis=0)


def tables_kernel(
    dirs_ref, weight_ref, mirror_ref, bands_ref, own_ref, blocks_ref, count_ref, facet_ref,
    coef_ref, srcw_ref, cols_ref, first_ref, image_ref, back_ref, tmp, tmp2, spread_ref, slots,
):
    eye = (lax.broadcasted_iota(jnp.int32, (DIRS, DIRS), 0) == lanes(DIRS)).astype(jnp.float32)
    dirs = dirs_ref[...]
    tmp[...] = jnp.zeros_like(tmp)
    tmp[0:3, :] = (dirs < 0).astype(jnp.float32)
    tmp[3:6, :] = mirror_ref[...].astype(jnp.float32)
    cols = nt_dot(eye, tmp[...])
    lane_f = lanes(DIRS).astype(jnp.float32)
    rep = eye
    for axis in range(3):
        image = (cols[:, 3 + axis : 4 + axis] == lane_f).astype(jnp.float32)
        rep = jnp.where(cols[:, axis : axis + 1] > 0.5, nn_dot(rep, image), rep)
    negs = cols[:, 0:1] + cols[:, 1:2] + cols[:, 2:3]
    positive = jnp.broadcast_to((negs < 0.5).astype(jnp.float32), (DIRS, DIRS))
    below = (lax.broadcasted_iota(jnp.int32, (DIRS, DIRS), 0) > lanes(DIRS)).astype(jnp.float32)
    rank = nn_dot(rep, nn_dot(below, positive))
    place = 64.0 * cols[:, 0:1] + 32.0 * cols[:, 1:2] + 16.0 * cols[:, 2:3] + rank
    tmp2[...] = (place == lane_f).astype(jnp.float32)
    for own in range(OWN):
        spread_ref[own * SRC : (own + 1) * SRC, :] = tmp2[pl.ds(own, SRC, stride=OWN), :]
    tmp[0:3, :] = jnp.abs(dirs)
    tmp[3:4, :] = weight_ref[...]
    placed = nn_dot(tmp[...], tmp2[...])
    eye_b = (
        lax.broadcasted_iota(jnp.int32, (BANDS, BANDS), 0)
        == lax.broadcasted_iota(jnp.int32, (BANDS, BANDS), 1)
    ).astype(jnp.float32)
    per_band = nt_dot(eye_b, bands_ref[...])
    cols_ref[...] = per_band
    courant = per_band[:, 0:1]
    for axis in range(3):
        s = courant * placed[axis : axis + 1, :]
        at = axis * 3 * BANDS
        coef_ref[at : at + BANDS, :] = 1.0 - 1.5 * s + 0.5 * s * s
        coef_ref[at + BANDS : at + 2 * BANDS, :] = 2.0 * s - s * s
        coef_ref[at + 2 * BANDS : at + 3 * BANDS, :] = 0.5 * s * s - 0.5 * s
    srcw_ref[...] = per_band[:, 1:2] * placed[3:4, :]

    lane = lanes(8)
    place_in = (nn_dot(lane_k(8), spread_ref[...]) + 0.5).astype(jnp.int32)
    back_ref[...] = (nt_dot(lane_k(8), spread_ref[...]) + 0.5).astype(jnp.int32)
    own = chunk_of(own_ref[0])
    half = own // 16
    offset = (own % 16) * YC
    for block in range(16):
        slots[block] = -1
    for k in range(16):
        @pl.when(k < count_ref[0])
        def _():
            slots[blocks_ref[0, k]] = k
    for xz in range(XZ):
        slot = slots[(xz // 4) * 8 + (xz % 4) * 2 + half]
        for y in range(YC):
            found = facet_ref[0, jnp.maximum(slot, 0), offset + y]
            facet = jnp.where(slot >= 0, found, 0)
            axis = lax.shift_right_logical(jnp.maximum(facet - 1, 0), 1)
            bit = jnp.where(facet > 0, lax.shift_right_logical(64, axis), 0)
            want = jnp.where((facet & 1) == 1, 0, bit)
            image = jnp.where((lane & bit) == want, lane ^ bit, lane)
            at = y * TILE + xz * 8
            image_ref[at : at + 8, :] = image
            first_ref[at : at + 8, :] = taken(place_in, image)


def lane_k(rows):
    return lanes(rows).astype(jnp.float32)


def natural(own, octet, xz, half):
    start = own * 640 + octet * 128 + xz // 4 * 8 + half * 4 + xz % 4
    return pl.ds(start, 8, stride=16)


def pack_kernel(x_hbm, s_hbm, x_ref, s_ref, sems):
    ins = [
        pltpu.make_async_copy(
            x_hbm.at[pl.ds(own * 640, 640)], x_ref.at[pl.ds(own * 640, 640)], sems.at[own]
        )
        for own in range(OWN)
    ]
    outs = [
        pltpu.make_async_copy(
            s_ref.at[pl.ds(half * SENT // 2, SENT // 2)],
            s_hbm.at[pl.ds(half * SENT // 2, SENT // 2)],
            sems.at[OWN + half],
        )
        for half in range(2)
    ]
    for copy in ins:
        copy.start()
    for dest in range(SRC):
        s_ref[dest * MSG + 80 : dest * MSG + 81, :] = jnp.zeros((1, DIRS), jnp.float32)
    for half in range(2):
        for own in range(OWN):
            if half == 0:
                ins[own].wait()
            rows = [
                x_ref[natural(own, octet, xz, half), :] for octet in range(OCTS) for xz in range(XZ)
            ]
            for pair in range(2):
                t = jnp.concatenate(rows[pair * 16 : (pair + 1) * 16], axis=0).T
                for jj in range(16):
                    at = SNAKE[half * 16 + jj] * MSG + pair * 32 + own * YC
                    s_ref[at : at + YC, :] = t[jj * YC : (jj + 1) * YC]
            rest = jnp.concatenate(rows[32:], axis=0)
            t = jnp.concatenate([rest, pltpu.roll(rest, 124, 1)], axis=0).T
            for jj in range(16):
                at = SNAKE[half * 16 + jj] * MSG + 64 + own * 4
                s_ref[at : at + 4, :] = t[jj * YC : jj * YC + 4]
        outs[half].start()
    for copy in outs:
        copy.wait()


def store_edges(e_ref, ya_ref, yb_ref):
    pos = (lanes(TILE) & 32) == 0
    for octet in range(OCTS):
        at = octet * TILE
        row = lambda y: e_ref[y * ROW + at : y * ROW + at + TILE, :]
        ya_ref[at : at + TILE, :] = jnp.where(pos, row(6), pltpu.roll(row(7), 32, 1))
        yb_ref[at : at + TILE, :] = jnp.where(pos, pltpu.roll(row(1), 96, 1), row(0))


def store_faces(at, ay, low, a_ref, b_ref):
    e0, r1 = ay[:32], pltpu.roll(ay[32:], 64, 1)
    a_ref[pl.ds(at, 32), :] = jnp.where(low, e0, r1)
    b_ref[pl.ds(at, 32), :] = jnp.where(low, r1, e0)


def spread_kernel(r_ref, first_ref, coef_ref, e_ref, ya_ref, yb_ref, ay_ref, a_ref, b_ref, f_ref):
    for y in range(YC):
        for pair in range(2):
            t = jnp.concatenate(
                [
                    r_ref[pl.ds(pair * 32 + own * YC + y, SRC, stride=MSG), :]
                    for own in range(OWN)
                ],
                axis=0,
            ).T
            at = y * ROW + pair * 128
            f_ref[at : at + 128, :] = t
    for y in range(4):
        t = jnp.concatenate(
            [r_ref[pl.ds(64 + own * 4 + y, SRC, stride=MSG), :] for own in range(OWN)], axis=0
        ).T
        f_ref[y * ROW + 256 : y * ROW + 320, :] = t[:TILE]
        f_ref[(y + 4) * ROW + 256 : (y + 4) * ROW + 320, :] = t[TILE:]
    for y in range(YC):
        for xz in range(XZ):
            index = first_ref[y * TILE + xz * 8 : y * TILE + xz * 8 + 8, :]
            for octet in range(OCTS):
                at = y * ROW + octet * TILE + xz * 8
                e_ref[at : at + 8, :] = taken(f_ref[at : at + 8, :], index)
    store_edges(e_ref, ya_ref, yb_ref)
    sweep_inner(e_ref, coef_ref, ay_ref, a_ref, b_ref)


def y_coefs(coef_ref, octet):
    at = 3 * BANDS + octet * 8
    return [tiled(coef_ref[at + k * BANDS : at + k * BANDS + 8, :], XZ) for k in range(3)]


def sweep_inner(e_ref, coef_ref, ay_ref, a_ref, b_ref):
    low = lanes(32) < 64
    pos = (lanes(TILE) & 32) == 0
    for octet in range(OCTS):
        y0, y1, y2 = y_coefs(coef_ref, octet)
        for k in range(YC - 2):
            at = octet * TILE
            far, near, here = (
                e_ref[(k + j) * ROW + at : (k + j) * ROW + at + TILE, :] for j in range(3)
            )
            ay = y0 * jnp.where(pos, here, far) + y1 * near + y2 * jnp.where(pos, far, here)
            ay_ref[k * ROW + at : k * ROW + at + TILE, :] = ay
            store_faces(k * FACE + octet * 32, ay, low, a_ref, b_ref)


def outer_kernel(e_ref, ml_ref, mr_ref, coef_ref, ay_ref, a_ref, b_ref):
    low = lanes(32) < 64
    pos = (lanes(TILE) & 32) == 0
    for octet in range(OCTS):
        y0, y1, y2 = y_coefs(coef_ref, octet)
        at = octet * TILE
        row = lambda y: e_ref[y * ROW + at : y * ROW + at + TILE, :]
        ml = ml_ref[at : at + TILE, :]
        mr = mr_ref[at : at + TILE, :]
        h0 = jnp.where(pos, ml, mr)
        h1 = jnp.where(pos, pltpu.roll(ml, 96, 1), pltpu.roll(mr, 32, 1))
        e0, e7 = row(0), row(7)
        ay0 = y0 * jnp.where(pos, e0, row(6)) + y1 * jnp.where(pos, h1, e7) + y2 * h0
        ay1 = y0 * jnp.where(pos, row(1), e7) + y1 * jnp.where(pos, e0, h0) + y2 * h1
        for k, ay in enumerate((ay0, ay1)):
            ay_ref[k * ROW + at : k * ROW + at + TILE, :] = ay
            store_faces(k * FACE + octet * 32, ay, low, a_ref, b_ref)


def expm1(q):
    small = q * (1.0 + q * (1 / 2) * (1.0 + q * (1 / 3) * (1.0 + q * (1 / 4) * (
        1.0 + q * (1 / 5) * (1.0 + q * (1 / 6))))))
    return jnp.where(q < 0.25, small, jnp.exp(q) - 1.0)


def sweep_xz(count, ay_ref, ml_ref, mr_ref, coef_ref, srcw_ref, mv_ref, acc_ref):
    lane = lanes(8)
    low = lane < 64
    pos_z = (lane & 16) == 0
    acc_ref[...] = jnp.zeros_like(acc_ref)

    def one_octet(octet, carry):
        def at(pitch, offset):
            return pl.ds(pl.multiple_of(octet * pitch + offset, 8), 8)

        x0, x1, x2, z0, z1, z2 = (coef_ref[at(8, k * BANDS), :] for k in (0, 1, 2, 6, 7, 8))
        weight = srcw_ref[at(8, 0), :]
        for row in range(count):
            swept = [[], []]
            for z in range(4):
                e0 = ay_ref[at(TILE, row * ROW + z * 8), :]
                e1 = ay_ref[at(TILE, row * ROW + (4 + z) * 8), :]
                ml = ml_ref[at(32, row * FACE + z * 8), :]
                mr = mr_ref[at(32, row * FACE + z * 8), :]
                g0 = jnp.where(low, ml, mr)
                g1 = pltpu.roll(jnp.where(low, mr, ml), 64, 1)
                swept[0].append(x0 * e0 + x1 * jnp.where(low, g1, e1) + x2 * g0)
                swept[1].append(x0 * e1 + x1 * jnp.where(low, e0, g0) + x2 * g1)
            for x in range(2):
                ax = swept[x]
                for z in range(4):
                    near = jnp.where(pos_z, ax[(z + 3) % 4], ax[(z + 1) % 4])
                    mv = z0 * ax[z] + z1 * near + z2 * ax[(z + 2) % 4]
                    xz = x * 4 + z
                    mv_ref[at(TILE, row * ROW + xz * 8), :] = mv
                    cell = (row * XZ + xz) * 8
                    acc_ref[cell : cell + 8, :] += weight * mv
        return carry

    lax.fori_loop(0, OCTS, one_octet, 0)
    return acc_ref[...].reshape(count * XZ, 8, DIRS).sum(axis=1)


def keep_moved(ys, first, row, cols_ref, index_of, e_ref):
    keep = jnp.broadcast_to(1.0 - cols_ref[:, 1:2], (BANDS, DIRS))
    pos = (lanes(8) & 32) == 0
    for y in ys:
        for xz in range(XZ):
            index = index_of(y, xz)
            for octet in range(OCTS):
                at = octet * TILE + xz * 8
                moved = jnp.where(pos, row(y, at), row((y + 2) % YC, at))
                out = (y - first) * ROW + at
                e_ref[out : out + 8, :] = taken(keep[octet * 8 : (octet + 1) * 8] * moved, index)


def index_from(index_ref):
    if index_ref.shape[0] == 8:
        index = index_ref[...]
        return lambda y, xz: index
    return lambda y, xz: index_ref[y * TILE + xz * 8 : y * TILE + xz * 8 + 8, :]


def mid_kernel(
    ay_ref, ml_ref, mr_ref, coef_ref, srcw_ref, cols_ref, index_ref,
    mv_ref, sums_ref, e_ref, acc_ref,
):
    sums_ref[...] = sweep_xz(YC - 2, ay_ref, ml_ref, mr_ref, coef_ref, srcw_ref, mv_ref, acc_ref)
    row = lambda k, at: mv_ref[(k - 2) * ROW + at : (k - 2) * ROW + at + 8, :]
    keep_moved(range(2, 6), 2, row, cols_ref, index_from(index_ref), e_ref)


def heat_of(inner_sums, outer_sums, cols_ref):
    here = jnp.concatenate([outer_sums, inner_sums], axis=0)
    turned = jnp.concatenate([inner_sums, outer_sums], axis=0)
    per_cell = jnp.where((lanes(64) & 32) == 0, here, turned)
    source = nt_dot(jnp.ones((8, DIRS), jnp.float32), per_cell)[0:1, :]
    relax = cols_ref[:, 1:2]
    heat = cols_ref[:, 2:3]
    pulse = cols_ref[:, 3:4]
    speed = relax * heat
    temp = jnp.ones((1, 64), jnp.float32)
    for _ in range(NEWTON):
        q = pulse / temp
        surplus = expm1(q)
        mismatch = jnp.sum(speed / surplus, axis=0, keepdims=True) - source
        slope = jnp.sum(
            speed * q * jnp.exp(q) / (surplus * surplus), axis=0, keepdims=True
        ) / temp
        temp = jnp.clip(temp - mismatch / slope, 0.5 * temp, 2.0 * temp)
    return temp, relax * (heat / expm1(pulse / temp))


def keep_moved_rest(inner_ref, outer_ref, cols_ref, index_ref, e_ref):
    def row(k, at):
        return outer_ref[k * ROW + at : k * ROW + at + 8, :] if k < 2 else inner_ref[
            (k - 2) * ROW + at : (k - 2) * ROW + at + 8, :
        ]

    keep_moved((0, 1, 6, 7), 0, row, cols_ref, index_from(index_ref), e_ref)


def add_heat(eq, mid_ref, e_ref):
    for y in range(YC):
        for octet in range(OCTS):
            at = y * ROW + octet * TILE
            heat = jnp.concatenate(
                [
                    jnp.broadcast_to(
                        eq[octet * 8 : (octet + 1) * 8, y * XZ + xz : y * XZ + xz + 1], (8, DIRS)
                    )
                    for xz in range(XZ)
                ],
                axis=0,
            )
            kept = mid_ref[at - 2 * ROW : at - 2 * ROW + TILE, :] if 2 <= y < 6 else e_ref[
                at : at + TILE, :
            ]
            e_ref[at : at + TILE, :] = kept + heat


def step_kernel(
    mvi_ref, sums_ref, mid_ref, ayo_ref, mlo_ref, mro_ref, coef_ref, srcw_ref, cols_ref, image_ref,
    e_ref, ya_ref, yb_ref, ay_ref, a_ref, b_ref, mvo_ref, acc_ref,
):
    outer = sweep_xz(2, ayo_ref, mlo_ref, mro_ref, coef_ref, srcw_ref, mvo_ref, acc_ref)
    keep_moved_rest(mvi_ref, mvo_ref, cols_ref, image_ref, e_ref)
    _, eq = heat_of(sums_ref[...], outer, cols_ref)
    add_heat(eq, mid_ref, e_ref)
    store_edges(e_ref, ya_ref, yb_ref)
    sweep_inner(e_ref, coef_ref, ay_ref, a_ref, b_ref)


def last_kernel(
    mvi_ref, sums_ref, mid_ref, ayo_ref, mlo_ref, mro_ref, coef_ref, srcw_ref, cols_ref, back_ref,
    s_ref, mvo_ref, acc_ref, e_ref,
):
    outer = sweep_xz(2, ayo_ref, mlo_ref, mro_ref, coef_ref, srcw_ref, mvo_ref, acc_ref)
    keep_moved_rest(mvi_ref, mvo_ref, cols_ref, back_ref, e_ref)
    temp, eq = heat_of(sums_ref[...], outer, cols_ref)
    wide = jnp.concatenate([temp, jnp.zeros((1, DIRS - 64), jnp.float32)], axis=1)
    s_ref[pl.ds(80, SRC, stride=MSG), :] = jnp.broadcast_to(wide, (SRC, DIRS))
    add_heat(eq, mid_ref, e_ref)
    for y in range(YC):
        for pair in range(2):
            at = y * ROW + pair * 128
            t = e_ref[at : at + 128, :].T
            for own in range(OWN):
                s_ref[pl.ds(pair * 32 + own * YC + y, SRC, stride=MSG), :] = t[
                    own * SRC : (own + 1) * SRC
                ]
    for y in range(4):
        t = jnp.concatenate(
            [e_ref[k * ROW + 256 : k * ROW + 320, :] for k in (y, y + 4)], axis=0
        ).T
        for own in range(OWN):
            s_ref[pl.ds(64 + own * 4 + y, SRC, stride=MSG), :] = t[own * SRC : (own + 1) * SRC]


def unpack_kernel(r_ref, x_hbm, t_ref, x_ref, sems):
    lower = (lanes(TILE) & 4) == 0
    copies = []
    for own in range(OWN):
        for half in range(2):
            rows = []
            for pair in range(2):
                tiles = []
                for jj in range(16):
                    at = SNAKE[half * 16 + jj] * MSG + pair * 32 + own * YC
                    tiles.append(r_ref[at : at + YC, :])
                rows.append(jnp.concatenate(tiles, axis=0).T)
            tiles = []
            for jj in range(16):
                at = SNAKE[half * 16 + jj] * MSG + 64 + own * 4
                four = r_ref[at : at + 4, :]
                tiles += [four, four]
            t = jnp.concatenate(tiles, axis=0).T
            rows.append(jnp.where(lower, t[:TILE], t[TILE:]))
            for octet in range(OCTS):
                for xz in range(XZ):
                    at = octet % 2 * TILE + xz * 8
                    x_ref[natural(own, octet, xz, half), :] = rows[octet // 2][at : at + 8]
        part = pl.ds(own * 640, 640)
        copies.append(pltpu.make_async_copy(x_ref.at[part], x_hbm.at[part], sems.at[own]))
        copies[own].start()
    lane = lanes(16)
    here = lane // 8 == chunk_of(lax.broadcasted_iota(jnp.int32, (16, DIRS), 0))
    for half in range(2):
        temps = r_ref[pl.ds(half * 16 * MSG + 80, 16, stride=MSG), :]
        for xz in range(XZ):
            spread = jnp.where(here, taken(temps, lane % 8 * XZ + xz), 0.0)
            t_ref[xz // 4, xz % 4 : xz % 4 + 1, half * 128 : (half + 1) * 128] = jnp.sum(
                spread, axis=0, keepdims=True
            )
    for copy in copies:
        copy.wait()


def f32(*shape):
    return pltpu.VMEM(shape, jnp.float32)


VMEM = pl.BlockSpec(memory_space=pltpu.VMEM)
SMEM = pl.BlockSpec(memory_space=pltpu.SMEM)
ANY = pl.BlockSpec(memory_space=pltpu.HBM)


def call(kernel, in_specs, out_shape, scratch=(), out_specs=None, name=None, cost=None):
    if out_specs is None:
        out_specs = tuple(VMEM for _ in out_shape) if isinstance(out_shape, tuple) else VMEM

    def run(*args):
        args = [
            a if s is SMEM else pltpu.with_memory_space_constraint(a, s.memory_space)
            for a, s in zip(args, in_specs)
        ]
        return pl.pallas_call(
            kernel,
            in_specs=in_specs,
            out_specs=out_specs,
            out_shape=out_shape,
            scratch_shapes=list(scratch),
            compiler_params=pltpu.CompilerParams(vmem_limit_bytes=24 << 20),
            cost_estimate=cost,
            name=name,
        )(*args)

    return run


OUTER_COST = pl.CostEstimate(flops=2_000_000_000, transcendentals=0, bytes_accessed=0)
MID_COST = pl.CostEstimate(flops=7_000_000, transcendentals=0, bytes_accessed=4_000_000)


def exchanged(messages):
    whole = messages.reshape(SRC, 1, MSG * DIRS)
    return lax.all_to_all(whole, "dir", 0, 0, tiled=True).reshape(SENT, DIRS)


def both_ways(up, down, axis):
    order = SNAKE if axis == "dir" else list(range(lax.axis_size(axis)))
    right = list(zip(order, order[1:] + order[:1]))
    left = [(j, i) for i, j in right]
    return lax.ppermute(up, axis, right), lax.ppermute(down, axis, left)


def on_device(
    phonon_heat_density,
    directions,
    quad_weight,
    mirror,
    band_courant,
    relax_rate,
    mode_heat_magnitude,
    mode_pulsation,
    wall_blocks,
    wall_count,
    wall_facet,
):
    own = lax.axis_index("dir").astype(jnp.int32).reshape(1)
    bands = jnp.stack([band_courant, relax_rate, mode_heat_magnitude, mode_pulsation])
    bands = jnp.concatenate([bands, jnp.zeros_like(bands)])
    x2 = phonon_heat_density.reshape(OWN, BANDS, 2, 4, 2, 128)
    x2 = x2.transpose(0, 1, 2, 4, 3, 5).reshape(2560, 128)
    whole = pltpu.VMEM((2560, 128), jnp.float32)
    packed = call(
        pack_kernel, [ANY], jax.ShapeDtypeStruct((SENT, 128), jnp.float32),
        [whole, pltpu.VMEM((SENT, 128), jnp.float32), pltpu.SemaphoreType.DMA((OWN + 2,))], ANY,
        name="pack",
    )(x2)
    table = pltpu.VMEM((YC * TILE, 128), jnp.int32)
    coef, srcw, cols, first, image, place = call(
        tables_kernel,
        [VMEM] * 4 + [SMEM] * 4,
        (f32(360, 128), f32(40, 128), f32(40, 8), table, table, pltpu.VMEM((8, 128), jnp.int32)),
        [pltpu.VMEM((8, 128), jnp.float32), pltpu.VMEM((128, 128), jnp.float32),
         pltpu.VMEM((128, 128), jnp.float32), pltpu.SMEM((16,), jnp.int32)],
        name="tables",
    )(directions, quad_weight.reshape(1, 128), mirror, bands, own, wall_blocks, wall_count,
      wall_facet)
    met = exchanged(packed)
    field = f32(2560, 128)
    edge = f32(ROW, 128)
    swept_inner = (f32(6 * ROW, 128), f32(6 * FACE, 128), f32(6 * FACE, 128))
    e, ya, yb, ayi, a, b = call(
        spread_kernel, [VMEM] * 3, (field, edge, edge, *swept_inner), [whole], name="spread"
    )(met, first, coef)
    work = [pltpu.VMEM((2 * ROW, 128), jnp.float32), pltpu.VMEM((128, 128), jnp.float32)]
    for step in range(2):
        yl, yr = both_ways(ya, yb, "dir")
        mli, mri = both_ways(a, b, "space")
        ayo, a, b = call(
            outer_kernel, [VMEM] * 4, (f32(2 * ROW, 128), edge, edge), name="outer", cost=OUTER_COST
        )(e, yl, yr, coef)
        mlo, mro = both_ways(a, b, "space")
        index = place if step else image
        moved, sums, mid = call(
            mid_kernel, [VMEM] * 7, (f32(6 * ROW, 128), f32(48, 128), f32(4 * ROW, 128)),
            [pltpu.VMEM((384, 128), jnp.float32)], name="mid", cost=MID_COST,
        )(ayi, mli, mri, coef, srcw, cols, index)
        swept = (moved, sums, mid, ayo, mlo, mro, coef, srcw, cols, index)
        if step == 0:
            e, ya, yb, ayi, a, b = call(
                step_kernel, [VMEM] * 10, (field, edge, edge, *swept_inner), work, name="step"
            )(*swept)
        else:
            out = call(
                last_kernel, [VMEM] * 10, f32(SENT, 128), work + [whole], name="last"
            )(*swept)
    x2, temp = call(
        unpack_kernel,
        [VMEM],
        (jax.ShapeDtypeStruct((2560, 128), jnp.float32),
         jax.ShapeDtypeStruct((2, 4, 256), jnp.float32)),
        [whole, pltpu.SemaphoreType.DMA((OWN,))],
        (ANY, VMEM),
        name="unpack",
    )(exchanged(out))
    energy = x2.reshape(OWN, BANDS, 2, 2, 4, 128).transpose(0, 1, 2, 4, 3, 5)
    return energy.reshape(phonon_heat_density.shape), temp


def solution(mesh):
    in_specs = (
        P("dir", None, "space", None, None),
        P(),
        P(),
        P(),
        P(),
        P(),
        P(),
        P(),
        P("space", None),
        P("space"),
        P("space", None, None),
    )
    out_specs = (P("dir", None, "space", None, None), P("space", None, None))
    return jax.shard_map(
        on_device, mesh=mesh, in_specs=in_specs, out_specs=out_specs, check_vma=False
    )
```

```python
import jax
import jax.numpy as jnp
from jax import lax
from jax.experimental import pallas as pl
from jax.experimental.pallas import tpu as pltpu
from jax.sharding import PartitionSpec as P

NEWTON = 4
BANDS = 40
OCTS = 5
DIRS = 128
SRC = 32
OWN = 4
YC = 8
XZ = 8
TILE = XZ * 8
ROW = OCTS * TILE
FACE = ROW // 2
MSG = 81
SENT = SRC * MSG
HI = lax.Precision.HIGHEST
NT = (((1,), (1,)), ((), ()))


def nt_dot(a, b):
    return lax.dot_general(a, b, NT, precision=HI, preferred_element_type=jnp.float32)


def nn_dot(a, b):
    return jnp.dot(a, b, precision=HI, preferred_element_type=jnp.float32)


SNAKE = [c // 4 * 4 + (c % 4 if c // 4 % 2 == 0 else 3 - c % 4) for c in range(SRC)]


def chunk_of(device):
    along, across = device // 4, device % 4
    return along * 4 + jnp.where(along % 2 == 0, across, 3 - across)


def lanes(rows):
    return lax.broadcasted_iota(jnp.int32, (rows, DIRS), 1)


def taken(x, index):
    return jnp.take_along_axis(x, index, axis=1)


def tiled(x, count):
    return jnp.concatenate([x] * count, axis=0)


def tables_kernel(
    dirs_ref, weight_ref, mirror_ref, bands_ref, own_ref, blocks_ref, count_ref, facet_ref,
    coef_ref, srcw_ref, cols_ref, first_ref, image_ref, back_ref, tmp, tmp2, spread_ref, slots,
):
    eye = (lax.broadcasted_iota(jnp.int32, (DIRS, DIRS), 0) == lanes(DIRS)).astype(jnp.float32)
    dirs = dirs_ref[...]
    tmp[...] = jnp.zeros_like(tmp)
    tmp[0:3, :] = (dirs < 0).astype(jnp.float32)
    tmp[3:6, :] = mirror_ref[...].astype(jnp.float32)
    cols = nt_dot(eye, tmp[...])
    lane_f = lanes(DIRS).astype(jnp.float32)
    rep = eye
    for axis in range(3):
        image = (cols[:, 3 + axis : 4 + axis] == lane_f).astype(jnp.float32)
        rep = jnp.where(cols[:, axis : axis + 1] > 0.5, nn_dot(rep, image), rep)
    negs = cols[:, 0:1] + cols[:, 1:2] + cols[:, 2:3]
    positive = jnp.broadcast_to((negs < 0.5).astype(jnp.float32), (DIRS, DIRS))
    below = (lax.broadcasted_iota(jnp.int32, (DIRS, DIRS), 0) > lanes(DIRS)).astype(jnp.float32)
    rank = nn_dot(rep, nn_dot(below, positive))
    place = 64.0 * cols[:, 0:1] + 32.0 * cols[:, 1:2] + 16.0 * cols[:, 2:3] + rank
    tmp2[...] = (place == lane_f).astype(jnp.float32)
    for own in range(OWN):
        spread_ref[own * SRC : (own + 1) * SRC, :] = tmp2[pl.ds(own, SRC, stride=OWN), :]
    tmp[0:3, :] = jnp.abs(dirs)
    tmp[3:4, :] = weight_ref[...]
    placed = nn_dot(tmp[...], tmp2[...])
    eye_b = (
        lax.broadcasted_iota(jnp.int32, (BANDS, BANDS), 0)
        == lax.broadcasted_iota(jnp.int32, (BANDS, BANDS), 1)
    ).astype(jnp.float32)
    per_band = nt_dot(eye_b, bands_ref[...])
    cols_ref[...] = per_band
    courant = per_band[:, 0:1]
    for axis in range(3):
        s = courant * placed[axis : axis + 1, :]
        at = axis * 3 * BANDS
        coef_ref[at : at + BANDS, :] = 1.0 - 1.5 * s + 0.5 * s * s
        coef_ref[at + BANDS : at + 2 * BANDS, :] = 2.0 * s - s * s
        coef_ref[at + 2 * BANDS : at + 3 * BANDS, :] = 0.5 * s * s - 0.5 * s
    srcw_ref[...] = per_band[:, 1:2] * placed[3:4, :]

    lane = lanes(8)
    place_in = (nn_dot(lane_k(8), spread_ref[...]) + 0.5).astype(jnp.int32)
    back_ref[...] = (nt_dot(lane_k(8), spread_ref[...]) + 0.5).astype(jnp.int32)
    own = chunk_of(own_ref[0])
    half = own // 16
    offset = (own % 16) * YC
    for block in range(16):
        slots[block] = -1
    for k in range(16):
        @pl.when(k < count_ref[0])
        def _():
            slots[blocks_ref[0, k]] = k
    for xz in range(XZ):
        slot = slots[(xz // 4) * 8 + (xz % 4) * 2 + half]
        for y in range(YC):
            found = facet_ref[0, jnp.maximum(slot, 0), offset + y]
            facet = jnp.where(slot >= 0, found, 0)
            axis = lax.shift_right_logical(jnp.maximum(facet - 1, 0), 1)
            bit = jnp.where(facet > 0, lax.shift_right_logical(64, axis), 0)
            want = jnp.where((facet & 1) == 1, 0, bit)
            image = jnp.where((lane & bit) == want, lane ^ bit, lane)
            at = y * TILE + xz * 8
            image_ref[at : at + 8, :] = image
            first_ref[at : at + 8, :] = taken(place_in, image)


def lane_k(rows):
    return lanes(rows).astype(jnp.float32)


def natural(own, octet, xz, half):
    start = own * 640 + octet * 128 + xz // 4 * 8 + half * 4 + xz % 4
    return pl.ds(start, 8, stride=16)


def pack_kernel(x_hbm, s_hbm, x_ref, s_ref, sems):
    ins = [
        pltpu.make_async_copy(
            x_hbm.at[pl.ds(own * 640, 640)], x_ref.at[pl.ds(own * 640, 640)], sems.at[own]
        )
        for own in range(OWN)
    ]
    outs = [
        pltpu.make_async_copy(
            s_ref.at[pl.ds(half * SENT // 2, SENT // 2)],
            s_hbm.at[pl.ds(half * SENT // 2, SENT // 2)],
            sems.at[OWN + half],
        )
        for half in range(2)
    ]
    for copy in ins:
        copy.start()
    for dest in range(SRC):
        s_ref[dest * MSG + 80 : dest * MSG + 81, :] = jnp.zeros((1, DIRS), jnp.float32)
    for half in range(2):
        for own in range(OWN):
            if half == 0:
                ins[own].wait()
            rows = [
                x_ref[natural(own, octet, xz, half), :] for octet in range(OCTS) for xz in range(XZ)
            ]
            for pair in range(2):
                t = jnp.concatenate(rows[pair * 16 : (pair + 1) * 16], axis=0).T
                for jj in range(16):
                    at = SNAKE[half * 16 + jj] * MSG + pair * 32 + own * YC
                    s_ref[at : at + YC, :] = t[jj * YC : (jj + 1) * YC]
            rest = jnp.concatenate(rows[32:], axis=0)
            t = jnp.concatenate([rest, pltpu.roll(rest, 124, 1)], axis=0).T
            for jj in range(16):
                at = SNAKE[half * 16 + jj] * MSG + 64 + own * 4
                s_ref[at : at + 4, :] = t[jj * YC : jj * YC + 4]
        outs[half].start()
    for copy in outs:
        copy.wait()


def side(y):
    return y if y < 2 else y - 4


def store_edges(e_ref, ya_ref, yb_ref):
    pos = (lanes(TILE) & 32) == 0
    for octet in range(OCTS):
        at = octet * TILE
        row = lambda y: e_ref[side(y) * ROW + at : side(y) * ROW + at + TILE, :]
        ya_ref[at : at + TILE, :] = jnp.where(pos, row(6), pltpu.roll(row(7), 32, 1))
        yb_ref[at : at + TILE, :] = jnp.where(pos, pltpu.roll(row(1), 96, 1), row(0))


def store_faces(at, ay, low, a_ref, b_ref):
    e0, r1 = ay[:32], pltpu.roll(ay[32:], 64, 1)
    a_ref[pl.ds(at, 32), :] = jnp.where(low, e0, r1)
    b_ref[pl.ds(at, 32), :] = jnp.where(low, r1, e0)


def spread_kernel(r_ref, first_ref, coef_ref, e_ref, ya_ref, yb_ref, ay_ref, a_ref, b_ref, f_ref):
    for y in range(YC):
        for pair in range(2):
            t = jnp.concatenate(
                [
                    r_ref[pl.ds(pair * 32 + own * YC + y, SRC, stride=MSG), :]
                    for own in range(OWN)
                ],
                axis=0,
            ).T
            at = y * ROW + pair * 128
            f_ref[at : at + 128, :] = t
    for y in range(4):
        t = jnp.concatenate(
            [r_ref[pl.ds(64 + own * 4 + y, SRC, stride=MSG), :] for own in range(OWN)], axis=0
        ).T
        f_ref[y * ROW + 256 : y * ROW + 320, :] = t[:TILE]
        f_ref[(y + 4) * ROW + 256 : (y + 4) * ROW + 320, :] = t[TILE:]
    for y in range(YC):
        for xz in range(XZ):
            index = first_ref[y * TILE + xz * 8 : y * TILE + xz * 8 + 8, :]
            for octet in range(OCTS):
                at = octet * TILE + xz * 8
                e = taken(f_ref[y * ROW + at : y * ROW + at + 8, :], index)
                if 2 <= y < 6:
                    f_ref[y * ROW + at : y * ROW + at + 8, :] = e
                else:
                    e_ref[side(y) * ROW + at : side(y) * ROW + at + 8, :] = e
    store_edges(e_ref, ya_ref, yb_ref)
    sweep_inner(e_ref, f_ref, 0, coef_ref, ay_ref, a_ref, b_ref)


def y_coefs(coef_ref, octet):
    at = 3 * BANDS + octet * 8
    return [tiled(coef_ref[at + k * BANDS : at + k * BANDS + 8, :], XZ) for k in range(3)]


def row_of(y, e_ref, mid_ref, first, at):
    start = (y - first if 2 <= y < 6 else side(y)) * ROW + at
    return (mid_ref if 2 <= y < 6 else e_ref)[start : start + TILE, :]


def sweep_inner(e_ref, mid_ref, first, coef_ref, ay_ref, a_ref, b_ref):
    low = lanes(32) < 64
    pos = (lanes(TILE) & 32) == 0
    for octet in range(OCTS):
        y0, y1, y2 = y_coefs(coef_ref, octet)
        for k in range(YC - 2):
            at = octet * TILE
            far, near, here = (row_of(k + j, e_ref, mid_ref, first, at) for j in range(3))
            ay = y0 * jnp.where(pos, here, far) + y1 * near + y2 * jnp.where(pos, far, here)
            ay_ref[k * ROW + at : k * ROW + at + TILE, :] = ay
            store_faces(k * FACE + octet * 32, ay, low, a_ref, b_ref)


def outer_kernel(e_ref, ml_ref, mr_ref, coef_ref, ay_ref, a_ref, b_ref):
    low = lanes(32) < 64
    pos = (lanes(TILE) & 32) == 0
    for octet in range(OCTS):
        y0, y1, y2 = y_coefs(coef_ref, octet)
        at = octet * TILE
        row = lambda y: e_ref[side(y) * ROW + at : side(y) * ROW + at + TILE, :]
        ml = ml_ref[at : at + TILE, :]
        mr = mr_ref[at : at + TILE, :]
        h0 = jnp.where(pos, ml, mr)
        h1 = jnp.where(pos, pltpu.roll(ml, 96, 1), pltpu.roll(mr, 32, 1))
        e0, e7 = row(0), row(7)
        ay0 = y0 * jnp.where(pos, e0, row(6)) + y1 * jnp.where(pos, h1, e7) + y2 * h0
        ay1 = y0 * jnp.where(pos, row(1), e7) + y1 * jnp.where(pos, e0, h0) + y2 * h1
        for k, ay in enumerate((ay0, ay1)):
            ay_ref[k * ROW + at : k * ROW + at + TILE, :] = ay
            store_faces(k * FACE + octet * 32, ay, low, a_ref, b_ref)


def expm1(q):
    small = q * (1.0 + q * (1 / 2) * (1.0 + q * (1 / 3) * (1.0 + q * (1 / 4) * (
        1.0 + q * (1 / 5) * (1.0 + q * (1 / 6))))))
    return jnp.where(q < 0.25, small, jnp.exp(q) - 1.0)


def sweep_xz(count, ay_ref, ml_ref, mr_ref, coef_ref, srcw_ref, mv_ref, acc_ref):
    lane = lanes(8)
    low = lane < 64
    pos_z = (lane & 16) == 0
    acc_ref[...] = jnp.zeros_like(acc_ref)

    def one_octet(octet, carry):
        def at(pitch, offset):
            return pl.ds(pl.multiple_of(octet * pitch + offset, 8), 8)

        x0, x1, x2, z0, z1, z2 = (coef_ref[at(8, k * BANDS), :] for k in (0, 1, 2, 6, 7, 8))
        weight = srcw_ref[at(8, 0), :]
        for row in range(count):
            swept = [[], []]
            for z in range(4):
                e0 = ay_ref[at(TILE, row * ROW + z * 8), :]
                e1 = ay_ref[at(TILE, row * ROW + (4 + z) * 8), :]
                ml = ml_ref[at(32, row * FACE + z * 8), :]
                mr = mr_ref[at(32, row * FACE + z * 8), :]
                g0 = jnp.where(low, ml, mr)
                g1 = pltpu.roll(jnp.where(low, mr, ml), 64, 1)
                swept[0].append(x0 * e0 + x1 * jnp.where(low, g1, e1) + x2 * g0)
                swept[1].append(x0 * e1 + x1 * jnp.where(low, e0, g0) + x2 * g1)
            for x in range(2):
                ax = swept[x]
                for z in range(4):
                    near = jnp.where(pos_z, ax[(z + 3) % 4], ax[(z + 1) % 4])
                    mv = z0 * ax[z] + z1 * near + z2 * ax[(z + 2) % 4]
                    xz = x * 4 + z
                    mv_ref[at(TILE, row * ROW + xz * 8), :] = mv
                    cell = (row * XZ + xz) * 8
                    acc_ref[cell : cell + 8, :] += weight * mv
        return carry

    lax.fori_loop(0, OCTS, one_octet, 0)
    return acc_ref[...].reshape(count * XZ, 8, DIRS).sum(axis=1)


def keep_moved(ys, row, cols_ref, index_of, e_ref):
    keep = jnp.broadcast_to(1.0 - cols_ref[:, 1:2], (BANDS, DIRS))
    pos = (lanes(8) & 32) == 0
    for i, y in enumerate(ys):
        for xz in range(XZ):
            index = index_of(y, xz)
            for octet in range(OCTS):
                at = octet * TILE + xz * 8
                moved = jnp.where(pos, row(y, at), row((y + 2) % YC, at))
                out = i * ROW + at
                e_ref[out : out + 8, :] = taken(keep[octet * 8 : (octet + 1) * 8] * moved, index)


def index_from(index_ref):
    if index_ref.shape[0] == 8:
        index = index_ref[...]
        return lambda y, xz: index
    return lambda y, xz: index_ref[y * TILE + xz * 8 : y * TILE + xz * 8 + 8, :]


def mid_kernel(
    ay_ref, ml_ref, mr_ref, coef_ref, srcw_ref, cols_ref, index_ref,
    mv_ref, sums_ref, e_ref, t_ref, acc_ref,
):
    sums = sweep_xz(YC - 2, ay_ref, ml_ref, mr_ref, coef_ref, srcw_ref, mv_ref, acc_ref)
    sums_ref[...] = sums
    row = lambda k, at: mv_ref[(k - 2) * ROW + at : (k - 2) * ROW + at + 8, :]
    keep_moved((2, 3, 4, 5), row, cols_ref, index_from(index_ref), e_ref)
    temp, eq = heat_of(sums[:32], sums[16:], cols_ref)
    t_ref[...] = temp
    add_heat(eq, e_ref)


def heat_of(here, turned, cols_ref):
    per_cell = jnp.where((lanes(32) & 32) == 0, here, turned)
    source = nt_dot(jnp.ones((8, DIRS), jnp.float32), per_cell)[0:1, :]
    relax = cols_ref[:, 1:2]
    heat = cols_ref[:, 2:3]
    pulse = cols_ref[:, 3:4]
    speed = relax * heat
    temp = jnp.ones((1, 32), jnp.float32)
    for _ in range(NEWTON):
        q = pulse / temp
        surplus = expm1(q)
        inverse = 1.0 / surplus
        part = speed * inverse
        mismatch = jnp.sum(part, axis=0, keepdims=True) - source
        slope = jnp.sum(part * q * ((surplus + 1.0) * inverse), axis=0, keepdims=True) / temp
        temp = jnp.clip(temp - mismatch / slope, 0.5 * temp, 2.0 * temp)
    return temp, relax * (heat / expm1(pulse / temp))


def add_heat(eq, e_ref):
    for i in range(4):
        for octet in range(OCTS):
            at = i * ROW + octet * TILE
            e_ref[at : at + TILE, :] += jnp.concatenate(
                [
                    jnp.broadcast_to(
                        eq[octet * 8 : (octet + 1) * 8, i * XZ + xz : i * XZ + xz + 1], (8, DIRS)
                    )
                    for xz in range(XZ)
                ],
                axis=0,
            )


def finish_sides(
    mvi_ref, sums_ref, ayo_ref, mlo_ref, mro_ref, coef_ref, srcw_ref, cols_ref, index_ref,
    e_ref, mvo_ref, acc_ref,
):
    outer = sweep_xz(2, ayo_ref, mlo_ref, mro_ref, coef_ref, srcw_ref, mvo_ref, acc_ref)

    def row(k, at):
        return mvo_ref[k * ROW + at : k * ROW + at + 8, :] if k < 2 else mvi_ref[
            (k - 2) * ROW + at : (k - 2) * ROW + at + 8, :
        ]

    keep_moved((0, 1, 6, 7), row, cols_ref, index_from(index_ref), e_ref)
    temp, eq = heat_of(
        jnp.concatenate([outer, sums_ref[32:, :]], axis=0),
        jnp.concatenate([sums_ref[:16, :], outer], axis=0),
        cols_ref,
    )
    add_heat(eq, e_ref)
    return temp


def step_kernel(
    mvi_ref, sums_ref, mid_ref, tmid_ref, ayo_ref, mlo_ref, mro_ref, coef_ref, srcw_ref, cols_ref,
    image_ref, e_ref, ya_ref, yb_ref, ay_ref, a_ref, b_ref, mvo_ref, acc_ref,
):
    finish_sides(
        mvi_ref, sums_ref, ayo_ref, mlo_ref, mro_ref, coef_ref, srcw_ref, cols_ref, image_ref,
        e_ref, mvo_ref, acc_ref,
    )
    store_edges(e_ref, ya_ref, yb_ref)
    sweep_inner(e_ref, mid_ref, 2, coef_ref, ay_ref, a_ref, b_ref)


def last_kernel(
    mvi_ref, sums_ref, mid_ref, tmid_ref, ayo_ref, mlo_ref, mro_ref, coef_ref, srcw_ref, cols_ref,
    back_ref, s_ref, mvo_ref, acc_ref, e_ref,
):
    temp = finish_sides(
        mvi_ref, sums_ref, ayo_ref, mlo_ref, mro_ref, coef_ref, srcw_ref, cols_ref, back_ref,
        e_ref, mvo_ref, acc_ref,
    )
    temp = jnp.concatenate([temp, tmid_ref[...]], axis=1)
    wide = jnp.concatenate([temp, jnp.zeros((1, DIRS - 64), jnp.float32)], axis=1)
    s_ref[pl.ds(80, SRC, stride=MSG), :] = jnp.broadcast_to(wide, (SRC, DIRS))
    for y in range(YC):
        for pair in range(2):
            t = jnp.concatenate(
                [row_of(y, e_ref, mid_ref, 2, pair * 128 + part * TILE) for part in range(2)],
                axis=0,
            ).T
            for own in range(OWN):
                s_ref[pl.ds(pair * 32 + own * YC + y, SRC, stride=MSG), :] = t[
                    own * SRC : (own + 1) * SRC
                ]
    for y in range(4):
        t = jnp.concatenate(
            [row_of(k, e_ref, mid_ref, 2, 256) for k in (y, y + 4)], axis=0
        ).T
        for own in range(OWN):
            s_ref[pl.ds(64 + own * 4 + y, SRC, stride=MSG), :] = t[own * SRC : (own + 1) * SRC]


def unpack_kernel(r_ref, x_hbm, t_ref, x_ref, sems):
    lower = (lanes(TILE) & 4) == 0
    copies = []
    for own in range(OWN):
        for half in range(2):
            rows = []
            for pair in range(2):
                tiles = []
                for jj in range(16):
                    at = SNAKE[half * 16 + jj] * MSG + pair * 32 + own * YC
                    tiles.append(r_ref[at : at + YC, :])
                rows.append(jnp.concatenate(tiles, axis=0).T)
            tiles = []
            for jj in range(16):
                at = SNAKE[half * 16 + jj] * MSG + 64 + own * 4
                four = r_ref[at : at + 4, :]
                tiles += [four, four]
            t = jnp.concatenate(tiles, axis=0).T
            rows.append(jnp.where(lower, t[:TILE], t[TILE:]))
            for octet in range(OCTS):
                for xz in range(XZ):
                    at = octet % 2 * TILE + xz * 8
                    x_ref[natural(own, octet, xz, half), :] = rows[octet // 2][at : at + 8]
        part = pl.ds(own * 640, 640)
        copies.append(pltpu.make_async_copy(x_ref.at[part], x_hbm.at[part], sems.at[own]))
        copies[own].start()
    lane = lanes(16)
    here = lane // 8 == chunk_of(lax.broadcasted_iota(jnp.int32, (16, DIRS), 0))
    y = lane % 8
    place = jnp.where(y < 2, y, jnp.where(y < 6, y + 2, y - 4))
    for half in range(2):
        temps = r_ref[pl.ds(half * 16 * MSG + 80, 16, stride=MSG), :]
        for xz in range(XZ):
            spread = jnp.where(here, taken(temps, place * XZ + xz), 0.0)
            t_ref[xz // 4, xz % 4 : xz % 4 + 1, half * 128 : (half + 1) * 128] = jnp.sum(
                spread, axis=0, keepdims=True
            )
    for copy in copies:
        copy.wait()


def f32(*shape):
    return pltpu.VMEM(shape, jnp.float32)


VMEM = pl.BlockSpec(memory_space=pltpu.VMEM)
SMEM = pl.BlockSpec(memory_space=pltpu.SMEM)
ANY = pl.BlockSpec(memory_space=pltpu.HBM)


def call(kernel, in_specs, out_shape, scratch=(), out_specs=None, name=None, cost=None):
    if out_specs is None:
        out_specs = tuple(VMEM for _ in out_shape) if isinstance(out_shape, tuple) else VMEM

    def run(*args):
        args = [
            a if s is SMEM else pltpu.with_memory_space_constraint(a, s.memory_space)
            for a, s in zip(args, in_specs)
        ]
        return pl.pallas_call(
            kernel,
            in_specs=in_specs,
            out_specs=out_specs,
            out_shape=out_shape,
            scratch_shapes=list(scratch),
            compiler_params=pltpu.CompilerParams(vmem_limit_bytes=24 << 20),
            cost_estimate=cost,
            name=name,
        )(*args)

    return run


OUTER_COST = pl.CostEstimate(flops=2_000_000_000, transcendentals=0, bytes_accessed=0)
MID_COST = pl.CostEstimate(flops=7_000_000, transcendentals=0, bytes_accessed=4_000_000)


def exchanged(messages):
    whole = messages.reshape(SRC, 1, MSG * DIRS)
    return lax.all_to_all(whole, "dir", 0, 0, tiled=True).reshape(SENT, DIRS)


def both_ways(up, down, axis):
    order = SNAKE if axis == "dir" else list(range(lax.axis_size(axis)))
    right = list(zip(order, order[1:] + order[:1]))
    left = [(j, i) for i, j in right]
    return lax.ppermute(up, axis, right), lax.ppermute(down, axis, left)


def on_device(
    phonon_heat_density,
    directions,
    quad_weight,
    mirror,
    band_courant,
    relax_rate,
    mode_heat_magnitude,
    mode_pulsation,
    wall_blocks,
    wall_count,
    wall_facet,
):
    own = lax.axis_index("dir").astype(jnp.int32).reshape(1)
    bands = jnp.stack([band_courant, relax_rate, mode_heat_magnitude, mode_pulsation])
    bands = jnp.concatenate([bands, jnp.zeros_like(bands)])
    x2 = phonon_heat_density.reshape(OWN, BANDS, 2, 4, 2, 128)
    x2 = x2.transpose(0, 1, 2, 4, 3, 5).reshape(2560, 128)
    whole = pltpu.VMEM((2560, 128), jnp.float32)
    packed = call(
        pack_kernel, [ANY], jax.ShapeDtypeStruct((SENT, 128), jnp.float32),
        [whole, pltpu.VMEM((SENT, 128), jnp.float32), pltpu.SemaphoreType.DMA((OWN + 2,))], ANY,
        name="pack",
    )(x2)
    table = pltpu.VMEM((YC * TILE, 128), jnp.int32)
    coef, srcw, cols, first, image, place = call(
        tables_kernel,
        [VMEM] * 4 + [SMEM] * 4,
        (f32(360, 128), f32(40, 128), f32(40, 8), table, table, pltpu.VMEM((8, 128), jnp.int32)),
        [pltpu.VMEM((8, 128), jnp.float32), pltpu.VMEM((128, 128), jnp.float32),
         pltpu.VMEM((128, 128), jnp.float32), pltpu.SMEM((16,), jnp.int32)],
        name="tables",
    )(directions, quad_weight.reshape(1, 128), mirror, bands, own, wall_blocks, wall_count,
      wall_facet)
    met = exchanged(packed)
    sides = f32(4 * ROW, 128)
    edge = f32(ROW, 128)
    swept_inner = (f32(6 * ROW, 128), f32(6 * FACE, 128), f32(6 * FACE, 128))
    e, ya, yb, ayi, a, b = call(
        spread_kernel, [VMEM] * 3, (sides, edge, edge, *swept_inner), [whole], name="spread"
    )(met, first, coef)
    work = [pltpu.VMEM((2 * ROW, 128), jnp.float32), pltpu.VMEM((128, 128), jnp.float32)]
    for step in range(2):
        yl, yr = both_ways(ya, yb, "dir")
        mli, mri = both_ways(a, b, "space")
        ayo, a, b = call(
            outer_kernel, [VMEM] * 4, (f32(2 * ROW, 128), edge, edge), name="outer", cost=OUTER_COST
        )(e, yl, yr, coef)
        mlo, mro = both_ways(a, b, "space")
        index = place if step else image
        moved, sums, mid, tmid = call(
            mid_kernel, [VMEM] * 7, (f32(6 * ROW, 128), f32(48, 128), sides, f32(1, 32)),
            [pltpu.VMEM((384, 128), jnp.float32)], name="mid", cost=MID_COST,
        )(ayi, mli, mri, coef, srcw, cols, index)
        swept = (moved, sums, mid, tmid, ayo, mlo, mro, coef, srcw, cols, index)
        if step == 0:
            e, ya, yb, ayi, a, b = call(
                step_kernel, [VMEM] * 11, (sides, edge, edge, *swept_inner), work, name="step"
            )(*swept)
        else:
            out = call(
                last_kernel, [VMEM] * 11, f32(SENT, 128),
                work + [pltpu.VMEM((4 * ROW, 128), jnp.float32)], name="last"
            )(*swept)
    x2, temp = call(
        unpack_kernel,
        [VMEM],
        (jax.ShapeDtypeStruct((2560, 128), jnp.float32),
         jax.ShapeDtypeStruct((2, 4, 256), jnp.float32)),
        [whole, pltpu.SemaphoreType.DMA((OWN,))],
        (ANY, VMEM),
        name="unpack",
    )(exchanged(out))
    energy = x2.reshape(OWN, BANDS, 2, 2, 4, 128).transpose(0, 1, 2, 4, 3, 5)
    return energy.reshape(phonon_heat_density.shape), temp


def solution(mesh):
    in_specs = (
        P("dir", None, "space", None, None),
        P(),
        P(),
        P(),
        P(),
        P(),
        P(),
        P(),
        P("space", None),
        P("space"),
        P("space", None, None),
    )
    out_specs = (P("dir", None, "space", None, None), P("space", None, None))
    return jax.shard_map(
        on_device, mesh=mesh, in_specs=in_specs, out_specs=out_specs, check_vma=False
    )
```

```python
import jax
import jax.numpy as jnp
from jax import lax
from jax.experimental import pallas as pl
from jax.experimental.pallas import tpu as pltpu
from jax.sharding import PartitionSpec as P

NEWTON = 4
BANDS = 40
OCTS = 5
DIRS = 128
SRC = 32
OWN = 4
YC = 8
XZ = 8
TILE = XZ * 8
ROW = OCTS * TILE
FACE = ROW // 2
MSG_IN = 80
MSG = MSG_IN + 1
SENT = SRC * MSG
SENT_IN = SRC * MSG_IN
HI = lax.Precision.HIGHEST
NT = (((1,), (1,)), ((), ()))


def nt_dot(a, b):
    return lax.dot_general(a, b, NT, precision=HI, preferred_element_type=jnp.float32)


def nn_dot(a, b):
    return jnp.dot(a, b, precision=HI, preferred_element_type=jnp.float32)


SNAKE = [c // 4 * 4 + (c % 4 if c // 4 % 2 == 0 else 3 - c % 4) for c in range(SRC)]


def chunk_of(device):
    along, across = device // 4, device % 4
    return along * 4 + jnp.where(along % 2 == 0, across, 3 - across)


def lanes(rows):
    return lax.broadcasted_iota(jnp.int32, (rows, DIRS), 1)


def taken(x, index):
    return jnp.take_along_axis(x, index, axis=1)


def tiled(x, count):
    return jnp.concatenate([x] * count, axis=0)


def tables_kernel(
    dirs_ref, weight_ref, mirror_ref, bands_ref, own_ref, blocks_ref, count_ref, facet_ref,
    coef_ref, srcw_ref, cols_ref, first_ref, image_ref, back_ref, tmp, tmp2, spread_ref, slots,
):
    eye = (lax.broadcasted_iota(jnp.int32, (DIRS, DIRS), 0) == lanes(DIRS)).astype(jnp.float32)
    dirs = dirs_ref[...]
    tmp[...] = jnp.zeros_like(tmp)
    tmp[0:3, :] = (dirs < 0).astype(jnp.float32)
    tmp[3:6, :] = mirror_ref[...].astype(jnp.float32)
    cols = nt_dot(eye, tmp[...])
    lane_f = lanes(DIRS).astype(jnp.float32)
    rep = eye
    for axis in range(3):
        image = (cols[:, 3 + axis : 4 + axis] == lane_f).astype(jnp.float32)
        rep = jnp.where(cols[:, axis : axis + 1] > 0.5, nn_dot(rep, image), rep)
    negs = cols[:, 0:1] + cols[:, 1:2] + cols[:, 2:3]
    positive = jnp.broadcast_to((negs < 0.5).astype(jnp.float32), (DIRS, DIRS))
    below = (lax.broadcasted_iota(jnp.int32, (DIRS, DIRS), 0) > lanes(DIRS)).astype(jnp.float32)
    rank = nn_dot(rep, nn_dot(below, positive))
    place = 64.0 * cols[:, 0:1] + 32.0 * cols[:, 1:2] + 16.0 * cols[:, 2:3] + rank
    tmp2[...] = (place == lane_f).astype(jnp.float32)
    for own in range(OWN):
        spread_ref[own * SRC : (own + 1) * SRC, :] = tmp2[pl.ds(own, SRC, stride=OWN), :]
    tmp[0:3, :] = jnp.abs(dirs)
    tmp[3:4, :] = weight_ref[...]
    placed = nn_dot(tmp[...], tmp2[...])
    eye_b = (
        lax.broadcasted_iota(jnp.int32, (BANDS, BANDS), 0)
        == lax.broadcasted_iota(jnp.int32, (BANDS, BANDS), 1)
    ).astype(jnp.float32)
    per_band = nt_dot(eye_b, bands_ref[...])
    cols_ref[...] = per_band
    courant = per_band[:, 0:1]
    for axis in range(3):
        s = courant * placed[axis : axis + 1, :]
        at = axis * 3 * BANDS
        coef_ref[at : at + BANDS, :] = 1.0 - 1.5 * s + 0.5 * s * s
        coef_ref[at + BANDS : at + 2 * BANDS, :] = 2.0 * s - s * s
        coef_ref[at + 2 * BANDS : at + 3 * BANDS, :] = 0.5 * s * s - 0.5 * s
    srcw_ref[...] = per_band[:, 1:2] * placed[3:4, :]

    lane = lanes(8)
    place_in = (nn_dot(lane_k(8), spread_ref[...]) + 0.5).astype(jnp.int32)
    back_ref[...] = (nt_dot(lane_k(8), spread_ref[...]) + 0.5).astype(jnp.int32)
    own = chunk_of(own_ref[0])
    half = own // 16
    offset = (own % 16) * YC
    for block in range(16):
        slots[block] = -1
    for k in range(16):
        @pl.when(k < count_ref[0])
        def _():
            slots[blocks_ref[0, k]] = k
    for xz in range(XZ):
        slot = slots[(xz // 4) * 8 + (xz % 4) * 2 + half]
        for y in range(YC):
            found = facet_ref[0, jnp.maximum(slot, 0), offset + y]
            facet = jnp.where(slot >= 0, found, 0)
            axis = lax.shift_right_logical(jnp.maximum(facet - 1, 0), 1)
            bit = jnp.where(facet > 0, lax.shift_right_logical(64, axis), 0)
            want = jnp.where((facet & 1) == 1, 0, bit)
            image = jnp.where((lane & bit) == want, lane ^ bit, lane)
            at = y * TILE + xz * 8
            image_ref[at : at + 8, :] = image
            first_ref[at : at + 8, :] = taken(place_in, image)


def lane_k(rows):
    return lanes(rows).astype(jnp.float32)


def natural(own, octet, xz, half):
    start = own * 640 + octet * 128 + xz // 4 * 8 + half * 4 + xz % 4
    return pl.ds(start, 8, stride=16)


def pack_kernel(x_hbm, s_hbm, x_ref, s_ref, sems):
    ins = [
        pltpu.make_async_copy(
            x_hbm.at[pl.ds(own * 640, 640)], x_ref.at[pl.ds(own * 640, 640)], sems.at[own]
        )
        for own in range(OWN)
    ]
    outs = [
        pltpu.make_async_copy(
            s_ref.at[pl.ds(half * SENT_IN // 2, SENT_IN // 2)],
            s_hbm.at[pl.ds(half * SENT_IN // 2, SENT_IN // 2)],
            sems.at[OWN + half],
        )
        for half in range(2)
    ]
    for copy in ins:
        copy.start()
    for half in range(2):
        for own in range(OWN):
            if half == 0:
                ins[own].wait()
            rows = [
                x_ref[natural(own, octet, xz, half), :] for octet in range(OCTS) for xz in range(XZ)
            ]
            for pair in range(2):
                t = jnp.concatenate(rows[pair * 16 : (pair + 1) * 16], axis=0).T
                for jj in range(16):
                    at = SNAKE[half * 16 + jj] * MSG_IN + pair * 32 + own * YC
                    s_ref[at : at + YC, :] = t[jj * YC : (jj + 1) * YC]
            rest = jnp.concatenate(rows[32:], axis=0)
            t = jnp.concatenate([rest, pltpu.roll(rest, 124, 1)], axis=0).T
            for jj in range(16):
                at = SNAKE[half * 16 + jj] * MSG_IN + 64 + own * 4
                s_ref[at : at + 4, :] = t[jj * YC : jj * YC + 4]
        outs[half].start()
    for copy in outs:
        copy.wait()


def side(y):
    return y if y < 2 else y - 4


def store_edges(e_ref, ya_ref, yb_ref):
    pos = (lanes(TILE) & 32) == 0
    for octet in range(OCTS):
        at = octet * TILE
        row = lambda y: e_ref[side(y) * ROW + at : side(y) * ROW + at + TILE, :]
        ya_ref[at : at + TILE, :] = jnp.where(pos, row(6), pltpu.roll(row(7), 32, 1))
        yb_ref[at : at + TILE, :] = jnp.where(pos, pltpu.roll(row(1), 96, 1), row(0))


def store_faces(at, ay, low, a_ref, b_ref):
    e0, r1 = ay[:32], pltpu.roll(ay[32:], 64, 1)
    a_ref[pl.ds(at, 32), :] = jnp.where(low, e0, r1)
    b_ref[pl.ds(at, 32), :] = jnp.where(low, r1, e0)


def spread_kernel(r_ref, first_ref, coef_ref, e_ref, ya_ref, yb_ref, ay_ref, a_ref, b_ref, f_ref):
    for y in range(YC):
        for pair in range(2):
            t = jnp.concatenate(
                [
                    r_ref[pl.ds(pair * 32 + own * YC + y, SRC, stride=MSG_IN), :]
                    for own in range(OWN)
                ],
                axis=0,
            ).T
            at = y * ROW + pair * 128
            f_ref[at : at + 128, :] = t
    for y in range(4):
        t = jnp.concatenate(
            [r_ref[pl.ds(64 + own * 4 + y, SRC, stride=MSG_IN), :] for own in range(OWN)], axis=0
        ).T
        f_ref[y * ROW + 256 : y * ROW + 320, :] = t[:TILE]
        f_ref[(y + 4) * ROW + 256 : (y + 4) * ROW + 320, :] = t[TILE:]
    for y in range(YC):
        for xz in range(XZ):
            index = first_ref[y * TILE + xz * 8 : y * TILE + xz * 8 + 8, :]
            for octet in range(OCTS):
                at = octet * TILE + xz * 8
                e = taken(f_ref[y * ROW + at : y * ROW + at + 8, :], index)
                if 2 <= y < 6:
                    f_ref[y * ROW + at : y * ROW + at + 8, :] = e
                else:
                    e_ref[side(y) * ROW + at : side(y) * ROW + at + 8, :] = e
    store_edges(e_ref, ya_ref, yb_ref)
    sweep_inner(e_ref, f_ref, 0, coef_ref, ay_ref, a_ref, b_ref)


def y_coefs(coef_ref, octet):
    at = 3 * BANDS + octet * 8
    return [tiled(coef_ref[at + k * BANDS : at + k * BANDS + 8, :], XZ) for k in range(3)]


def row_of(y, e_ref, mid_ref, first, at):
    start = (y - first if 2 <= y < 6 else side(y)) * ROW + at
    return (mid_ref if 2 <= y < 6 else e_ref)[start : start + TILE, :]


def sweep_inner(e_ref, mid_ref, first, coef_ref, ay_ref, a_ref, b_ref):
    low = lanes(32) < 64
    pos = (lanes(TILE) & 32) == 0
    for octet in range(OCTS):
        y0, y1, y2 = y_coefs(coef_ref, octet)
        for k in range(YC - 2):
            at = octet * TILE
            far, near, here = (row_of(k + j, e_ref, mid_ref, first, at) for j in range(3))
            ay = y0 * jnp.where(pos, here, far) + y1 * near + y2 * jnp.where(pos, far, here)
            ay_ref[k * ROW + at : k * ROW + at + TILE, :] = ay
            store_faces(k * FACE + octet * 32, ay, low, a_ref, b_ref)


def outer_kernel(e_ref, ml_ref, mr_ref, coef_ref, ay_ref, a_ref, b_ref):
    low = lanes(32) < 64
    pos = (lanes(TILE) & 32) == 0
    for octet in range(OCTS):
        y0, y1, y2 = y_coefs(coef_ref, octet)
        at = octet * TILE
        row = lambda y: e_ref[side(y) * ROW + at : side(y) * ROW + at + TILE, :]
        ml = ml_ref[at : at + TILE, :]
        mr = mr_ref[at : at + TILE, :]
        h0 = jnp.where(pos, ml, mr)
        h1 = jnp.where(pos, pltpu.roll(ml, 96, 1), pltpu.roll(mr, 32, 1))
        e0, e7 = row(0), row(7)
        ay0 = y0 * jnp.where(pos, e0, row(6)) + y1 * jnp.where(pos, h1, e7) + y2 * h0
        ay1 = y0 * jnp.where(pos, row(1), e7) + y1 * jnp.where(pos, e0, h0) + y2 * h1
        for k, ay in enumerate((ay0, ay1)):
            ay_ref[k * ROW + at : k * ROW + at + TILE, :] = ay
            store_faces(k * FACE + octet * 32, ay, low, a_ref, b_ref)


def expm1(q):
    small = q * (1.0 + q * (1 / 2) * (1.0 + q * (1 / 3) * (1.0 + q * (1 / 4) * (
        1.0 + q * (1 / 5) * (1.0 + q * (1 / 6))))))
    return jnp.where(q < 0.25, small, jnp.exp(q) - 1.0)


def sweep_xz(count, ay_ref, ml_ref, mr_ref, coef_ref, srcw_ref, mv_ref, acc_ref):
    lane = lanes(8)
    low = lane < 64
    pos_z = (lane & 16) == 0
    acc_ref[...] = jnp.zeros_like(acc_ref)

    for octet in range(OCTS):

        def at(pitch, offset):
            return pl.ds(octet * pitch + offset, 8)

        x0, x1, x2, z0, z1, z2 = (coef_ref[at(8, k * BANDS), :] for k in (0, 1, 2, 6, 7, 8))
        weight = srcw_ref[at(8, 0), :]
        for row in range(count):
            swept = [[], []]
            for z in range(4):
                e0 = ay_ref[at(TILE, row * ROW + z * 8), :]
                e1 = ay_ref[at(TILE, row * ROW + (4 + z) * 8), :]
                ml = ml_ref[at(32, row * FACE + z * 8), :]
                mr = mr_ref[at(32, row * FACE + z * 8), :]
                g0 = jnp.where(low, ml, mr)
                g1 = pltpu.roll(jnp.where(low, mr, ml), 64, 1)
                swept[0].append(x0 * e0 + x1 * jnp.where(low, g1, e1) + x2 * g0)
                swept[1].append(x0 * e1 + x1 * jnp.where(low, e0, g0) + x2 * g1)
            for x in range(2):
                ax = swept[x]
                for z in range(4):
                    near = jnp.where(pos_z, ax[(z + 3) % 4], ax[(z + 1) % 4])
                    mv = z0 * ax[z] + z1 * near + z2 * ax[(z + 2) % 4]
                    xz = x * 4 + z
                    mv_ref[at(TILE, row * ROW + xz * 8), :] = mv
                    cell = (row * XZ + xz) * 8
                    acc_ref[cell : cell + 8, :] += weight * mv
    return acc_ref[...].reshape(count * XZ, 8, DIRS).sum(axis=1)


def keep_moved(ys, row, cols_ref, index_of, e_ref):
    keep = jnp.broadcast_to(1.0 - cols_ref[:, 1:2], (BANDS, DIRS))
    pos = (lanes(8) & 32) == 0
    for i, y in enumerate(ys):
        for xz in range(XZ):
            index = index_of(y, xz)
            for octet in range(OCTS):
                at = octet * TILE + xz * 8
                moved = jnp.where(pos, row(y, at), row((y + 2) % YC, at))
                out = i * ROW + at
                e_ref[out : out + 8, :] = taken(keep[octet * 8 : (octet + 1) * 8] * moved, index)


def index_from(index_ref):
    if index_ref.shape[0] == 8:
        index = index_ref[...]
        return lambda y, xz: index
    return lambda y, xz: index_ref[y * TILE + xz * 8 : y * TILE + xz * 8 + 8, :]


def mid_kernel(
    ay_ref, ml_ref, mr_ref, coef_ref, srcw_ref, cols_ref, index_ref,
    mv_ref, sums_ref, e_ref, t_ref, acc_ref,
):
    sums = sweep_xz(YC - 2, ay_ref, ml_ref, mr_ref, coef_ref, srcw_ref, mv_ref, acc_ref)
    sums_ref[...] = sums
    row = lambda k, at: mv_ref[(k - 2) * ROW + at : (k - 2) * ROW + at + 8, :]
    temp, eq = heat_of(sums[:32], sums[16:], cols_ref)
    t_ref[...] = temp
    keep_moved((2, 3, 4, 5), row, cols_ref, index_from(index_ref), e_ref)
    add_heat(eq, e_ref)


def heat_of(here, turned, cols_ref):
    per_cell = jnp.where((lanes(32) & 32) == 0, here, turned)
    source = nt_dot(jnp.ones((8, DIRS), jnp.float32), per_cell)[0:1, :]
    relax = cols_ref[:, 1:2]
    heat = cols_ref[:, 2:3]
    pulse = cols_ref[:, 3:4]
    speed = relax * heat
    temp = jnp.ones((1, 32), jnp.float32)
    for _ in range(NEWTON):
        per_temp = 1.0 / temp
        q = pulse * per_temp
        surplus = expm1(q)
        inverse = 1.0 / surplus
        part = speed * inverse
        mismatch = jnp.sum(part, axis=0, keepdims=True) - source
        slope = jnp.sum(part * q * ((surplus + 1.0) * inverse), axis=0, keepdims=True) * per_temp
        temp = jnp.clip(temp - mismatch / slope, 0.5 * temp, 2.0 * temp)
    return temp, speed / expm1(pulse * (1.0 / temp))


def add_heat(eq, e_ref):
    for i in range(4):
        for octet in range(OCTS):
            at = i * ROW + octet * TILE
            e_ref[at : at + TILE, :] += jnp.concatenate(
                [
                    jnp.broadcast_to(
                        eq[octet * 8 : (octet + 1) * 8, i * XZ + xz : i * XZ + xz + 1], (8, DIRS)
                    )
                    for xz in range(XZ)
                ],
                axis=0,
            )


def finish_sides(
    mvi_ref, sums_ref, ayo_ref, mlo_ref, mro_ref, coef_ref, srcw_ref, cols_ref, index_ref,
    e_ref, mvo_ref, acc_ref,
):
    outer = sweep_xz(2, ayo_ref, mlo_ref, mro_ref, coef_ref, srcw_ref, mvo_ref, acc_ref)

    def row(k, at):
        return mvo_ref[k * ROW + at : k * ROW + at + 8, :] if k < 2 else mvi_ref[
            (k - 2) * ROW + at : (k - 2) * ROW + at + 8, :
        ]

    temp, eq = heat_of(
        jnp.concatenate([outer, sums_ref[32:, :]], axis=0),
        jnp.concatenate([sums_ref[:16, :], outer], axis=0),
        cols_ref,
    )
    keep_moved((0, 1, 6, 7), row, cols_ref, index_from(index_ref), e_ref)
    add_heat(eq, e_ref)
    return temp


def step_kernel(
    mvi_ref, sums_ref, mid_ref, tmid_ref, ayo_ref, mlo_ref, mro_ref, coef_ref, srcw_ref, cols_ref,
    image_ref, e_ref, ya_ref, yb_ref, ay_ref, a_ref, b_ref, mvo_ref, acc_ref,
):
    finish_sides(
        mvi_ref, sums_ref, ayo_ref, mlo_ref, mro_ref, coef_ref, srcw_ref, cols_ref, image_ref,
        e_ref, mvo_ref, acc_ref,
    )
    store_edges(e_ref, ya_ref, yb_ref)
    sweep_inner(e_ref, mid_ref, 2, coef_ref, ay_ref, a_ref, b_ref)


def last_kernel(
    mvi_ref, sums_ref, mid_ref, tmid_ref, ayo_ref, mlo_ref, mro_ref, coef_ref, srcw_ref, cols_ref,
    back_ref, s_ref, mvo_ref, acc_ref, e_ref,
):
    temp = finish_sides(
        mvi_ref, sums_ref, ayo_ref, mlo_ref, mro_ref, coef_ref, srcw_ref, cols_ref, back_ref,
        e_ref, mvo_ref, acc_ref,
    )
    temp = jnp.concatenate([temp, tmid_ref[...]], axis=1)
    wide = jnp.concatenate([temp, jnp.zeros((1, DIRS - 64), jnp.float32)], axis=1)
    s_ref[pl.ds(80, SRC, stride=MSG), :] = jnp.broadcast_to(wide, (SRC, DIRS))
    for y in range(YC):
        for pair in range(2):
            t = jnp.concatenate(
                [row_of(y, e_ref, mid_ref, 2, pair * 128 + part * TILE) for part in range(2)],
                axis=0,
            ).T
            for own in range(OWN):
                s_ref[pl.ds(pair * 32 + own * YC + y, SRC, stride=MSG), :] = t[
                    own * SRC : (own + 1) * SRC
                ]
    for y in range(4):
        t = jnp.concatenate(
            [row_of(k, e_ref, mid_ref, 2, 256) for k in (y, y + 4)], axis=0
        ).T
        for own in range(OWN):
            s_ref[pl.ds(64 + own * 4 + y, SRC, stride=MSG), :] = t[own * SRC : (own + 1) * SRC]


def unpack_kernel(r_ref, x_hbm, t_ref, x_ref, sems):
    lower = (lanes(TILE) & 4) == 0
    copies = []
    for own in range(OWN):
        for half in range(2):
            rows = []
            for pair in range(2):
                tiles = []
                for jj in range(16):
                    at = SNAKE[half * 16 + jj] * MSG + pair * 32 + own * YC
                    tiles.append(r_ref[at : at + YC, :])
                rows.append(jnp.concatenate(tiles, axis=0).T)
            tiles = []
            for jj in range(16):
                at = SNAKE[half * 16 + jj] * MSG + 64 + own * 4
                four = r_ref[at : at + 4, :]
                tiles += [four, four]
            t = jnp.concatenate(tiles, axis=0).T
            rows.append(jnp.where(lower, t[:TILE], t[TILE:]))
            for octet in range(OCTS):
                for xz in range(XZ):
                    at = octet % 2 * TILE + xz * 8
                    x_ref[natural(own, octet, xz, half), :] = rows[octet // 2][at : at + 8]
        part = pl.ds(own * 640, 640)
        copies.append(pltpu.make_async_copy(x_ref.at[part], x_hbm.at[part], sems.at[own]))
        copies[own].start()
    lane = lanes(16)
    here = lane // 8 == chunk_of(lax.broadcasted_iota(jnp.int32, (16, DIRS), 0))
    y = lane % 8
    place = jnp.where(y < 2, y, jnp.where(y < 6, y + 2, y - 4))
    for half in range(2):
        temps = r_ref[pl.ds(half * 16 * MSG + 80, 16, stride=MSG), :]
        for xz in range(XZ):
            spread = jnp.where(here, taken(temps, place * XZ + xz), 0.0)
            t_ref[xz // 4, xz % 4 : xz % 4 + 1, half * 128 : (half + 1) * 128] = jnp.sum(
                spread, axis=0, keepdims=True
            )
    for copy in copies:
        copy.wait()


def f32(*shape):
    return pltpu.VMEM(shape, jnp.float32)


VMEM = pl.BlockSpec(memory_space=pltpu.VMEM)
SMEM = pl.BlockSpec(memory_space=pltpu.SMEM)
ANY = pl.BlockSpec(memory_space=pltpu.HBM)


def call(kernel, in_specs, out_shape, scratch=(), out_specs=None, name=None, cost=None):
    if out_specs is None:
        out_specs = tuple(VMEM for _ in out_shape) if isinstance(out_shape, tuple) else VMEM

    def run(*args):
        args = [
            a if s is SMEM else pltpu.with_memory_space_constraint(a, s.memory_space)
            for a, s in zip(args, in_specs)
        ]
        return pl.pallas_call(
            kernel,
            in_specs=in_specs,
            out_specs=out_specs,
            out_shape=out_shape,
            scratch_shapes=list(scratch),
            compiler_params=pltpu.CompilerParams(vmem_limit_bytes=24 << 20),
            cost_estimate=cost,
            name=name,
        )(*args)

    return run


OUTER_COST = pl.CostEstimate(flops=2_000_000_000, transcendentals=0, bytes_accessed=0)
MID_COST = pl.CostEstimate(flops=7_000_000, transcendentals=0, bytes_accessed=4_000_000)


def exchanged(messages):
    whole = messages.reshape(SRC, 1, -1)
    return lax.all_to_all(whole, "dir", 0, 0, tiled=True).reshape(messages.shape)


def both_ways(up, down, axis):
    order = SNAKE if axis == "dir" else list(range(lax.axis_size(axis)))
    right = list(zip(order, order[1:] + order[:1]))
    left = [(j, i) for i, j in right]
    return lax.ppermute(up, axis, right), lax.ppermute(down, axis, left)


def on_device(
    phonon_heat_density,
    directions,
    quad_weight,
    mirror,
    band_courant,
    relax_rate,
    mode_heat_magnitude,
    mode_pulsation,
    wall_blocks,
    wall_count,
    wall_facet,
):
    own = lax.axis_index("dir").astype(jnp.int32).reshape(1)
    bands = jnp.stack([band_courant, relax_rate, mode_heat_magnitude, mode_pulsation])
    bands = jnp.concatenate([bands, jnp.zeros_like(bands)])
    x2 = phonon_heat_density.reshape(OWN, BANDS, 2, 4, 2, 128)
    x2 = x2.transpose(0, 1, 2, 4, 3, 5).reshape(2560, 128)
    whole = pltpu.VMEM((2560, 128), jnp.float32)
    packed = call(
        pack_kernel, [ANY], jax.ShapeDtypeStruct((SENT_IN, 128), jnp.float32),
        [whole, whole, pltpu.SemaphoreType.DMA((OWN + 2,))], ANY,
        name="pack",
    )(x2)
    table = pltpu.VMEM((YC * TILE, 128), jnp.int32)
    coef, srcw, cols, first, image, place = call(
        tables_kernel,
        [VMEM] * 4 + [SMEM] * 4,
        (f32(360, 128), f32(40, 128), f32(40, 8), table, table, pltpu.VMEM((8, 128), jnp.int32)),
        [pltpu.VMEM((8, 128), jnp.float32), pltpu.VMEM((128, 128), jnp.float32),
         pltpu.VMEM((128, 128), jnp.float32), pltpu.SMEM((16,), jnp.int32)],
        name="tables",
    )(directions, quad_weight.reshape(1, 128), mirror, bands, own, wall_blocks, wall_count,
      wall_facet)
    met = exchanged(packed)
    sides = f32(4 * ROW, 128)
    edge = f32(ROW, 128)
    swept_inner = (f32(6 * ROW, 128), f32(6 * FACE, 128), f32(6 * FACE, 128))
    e, ya, yb, ayi, a, b = call(
        spread_kernel, [VMEM] * 3, (sides, edge, edge, *swept_inner), [whole], name="spread"
    )(met, first, coef)
    work = [pltpu.VMEM((2 * ROW, 128), jnp.float32), pltpu.VMEM((128, 128), jnp.float32)]
    for step in range(2):
        yl, yr = both_ways(ya, yb, "dir")
        mli, mri = both_ways(a, b, "space")
        ayo, a, b = call(
            outer_kernel, [VMEM] * 4, (f32(2 * ROW, 128), edge, edge), name="outer", cost=OUTER_COST
        )(e, yl, yr, coef)
        mlo, mro = both_ways(a, b, "space")
        index = place if step else image
        moved, sums, mid, tmid = call(
            mid_kernel, [VMEM] * 7, (f32(6 * ROW, 128), f32(48, 128), sides, f32(1, 32)),
            [pltpu.VMEM((384, 128), jnp.float32)], name="mid", cost=MID_COST,
        )(ayi, mli, mri, coef, srcw, cols, index)
        swept = (moved, sums, mid, tmid, ayo, mlo, mro, coef, srcw, cols, index)
        if step == 0:
            e, ya, yb, ayi, a, b = call(
                step_kernel, [VMEM] * 11, (sides, edge, edge, *swept_inner), work, name="step"
            )(*swept)
        else:
            out = call(
                last_kernel, [VMEM] * 11, f32(SENT, 128),
                work + [pltpu.VMEM((4 * ROW, 128), jnp.float32)], name="last"
            )(*swept)
    x2, temp = call(
        unpack_kernel,
        [VMEM],
        (jax.ShapeDtypeStruct((2560, 128), jnp.float32),
         jax.ShapeDtypeStruct((2, 4, 256), jnp.float32)),
        [whole, pltpu.SemaphoreType.DMA((OWN,))],
        (ANY, VMEM),
        name="unpack",
    )(exchanged(out))
    energy = x2.reshape(OWN, BANDS, 2, 2, 4, 128).transpose(0, 1, 2, 4, 3, 5)
    return energy.reshape(phonon_heat_density.shape), temp


def solution(mesh):
    in_specs = (
        P("dir", None, "space", None, None),
        P(),
        P(),
        P(),
        P(),
        P(),
        P(),
        P(),
        P("space", None),
        P("space"),
        P("space", None, None),
    )
    out_specs = (P("dir", None, "space", None, None), P("space", None, None))
    return jax.shard_map(
        on_device, mesh=mesh, in_specs=in_specs, out_specs=out_specs, check_vma=False
    )
```

```python
import jax
import jax.numpy as jnp
from jax import lax
from jax.experimental import pallas as pl
from jax.experimental.pallas import tpu as pltpu
from jax.sharding import PartitionSpec as P

NEWTON = 4
BANDS = 40
OCTS = 5
DIRS = 128
SRC = 32
OWN = 4
YC = 8
XZ = 8
TILE = XZ * 8
ROW = OCTS * TILE
FACE = ROW // 2
MSG_IN = 80
MSG = MSG_IN + 1
SENT = SRC * MSG
SENT_IN = SRC * MSG_IN
HI = lax.Precision.HIGHEST
NT = (((1,), (1,)), ((), ()))


def nt_dot(a, b):
    return lax.dot_general(a, b, NT, precision=HI, preferred_element_type=jnp.float32)


def nn_dot(a, b):
    return jnp.dot(a, b, precision=HI, preferred_element_type=jnp.float32)


SNAKE = [c // 4 * 4 + (c % 4 if c // 4 % 2 == 0 else 3 - c % 4) for c in range(SRC)]


def chunk_of(device):
    along, across = device // 4, device % 4
    return along * 4 + jnp.where(along % 2 == 0, across, 3 - across)


def lanes(rows):
    return lax.broadcasted_iota(jnp.int32, (rows, DIRS), 1)


def taken(x, index):
    return jnp.take_along_axis(x, index, axis=1)


def tiled(x, count):
    return jnp.concatenate([x] * count, axis=0)


def tables_kernel(
    dirs_ref, weight_ref, mirror_ref, bands_ref, own_ref, blocks_ref, count_ref, facet_ref,
    coef_ref, srcw_ref, cols_ref, first_ref, image_ref, back_ref, tmp, tmp2, spread_ref, slots,
):
    eye = (lax.broadcasted_iota(jnp.int32, (DIRS, DIRS), 0) == lanes(DIRS)).astype(jnp.float32)
    dirs = dirs_ref[...]
    tmp[...] = jnp.zeros_like(tmp)
    tmp[0:3, :] = (dirs < 0).astype(jnp.float32)
    tmp[3:6, :] = mirror_ref[...].astype(jnp.float32)
    cols = nt_dot(eye, tmp[...])
    lane_f = lanes(DIRS).astype(jnp.float32)
    rep = eye
    for axis in range(3):
        image = (cols[:, 3 + axis : 4 + axis] == lane_f).astype(jnp.float32)
        rep = jnp.where(cols[:, axis : axis + 1] > 0.5, nn_dot(rep, image), rep)
    negs = cols[:, 0:1] + cols[:, 1:2] + cols[:, 2:3]
    positive = jnp.broadcast_to((negs < 0.5).astype(jnp.float32), (DIRS, DIRS))
    below = (lax.broadcasted_iota(jnp.int32, (DIRS, DIRS), 0) > lanes(DIRS)).astype(jnp.float32)
    rank = nn_dot(rep, nn_dot(below, positive))
    place = 64.0 * cols[:, 0:1] + 32.0 * cols[:, 1:2] + 16.0 * cols[:, 2:3] + rank
    tmp2[...] = (place == lane_f).astype(jnp.float32)
    for own in range(OWN):
        spread_ref[own * SRC : (own + 1) * SRC, :] = tmp2[pl.ds(own, SRC, stride=OWN), :]
    tmp[0:3, :] = jnp.abs(dirs)
    tmp[3:4, :] = weight_ref[...]
    placed = nn_dot(tmp[...], tmp2[...])
    eye_b = (
        lax.broadcasted_iota(jnp.int32, (BANDS, BANDS), 0)
        == lax.broadcasted_iota(jnp.int32, (BANDS, BANDS), 1)
    ).astype(jnp.float32)
    per_band = nt_dot(eye_b, bands_ref[...])
    cols_ref[...] = per_band
    courant = per_band[:, 0:1]
    for axis in range(3):
        s = courant * placed[axis : axis + 1, :]
        at = axis * 3 * BANDS
        coef_ref[at : at + BANDS, :] = 1.0 - 1.5 * s + 0.5 * s * s
        coef_ref[at + BANDS : at + 2 * BANDS, :] = 2.0 * s - s * s
        coef_ref[at + 2 * BANDS : at + 3 * BANDS, :] = 0.5 * s * s - 0.5 * s
    srcw_ref[...] = per_band[:, 1:2] * placed[3:4, :]

    lane = lanes(8)
    place_in = (nn_dot(lane_k(8), spread_ref[...]) + 0.5).astype(jnp.int32)
    back_ref[...] = (nt_dot(lane_k(8), spread_ref[...]) + 0.5).astype(jnp.int32)
    own = chunk_of(own_ref[0])
    half = own // 16
    offset = (own % 16) * YC
    for block in range(16):
        slots[block] = -1
    for k in range(16):
        @pl.when(k < count_ref[0])
        def _():
            slots[blocks_ref[0, k]] = k
    for xz in range(XZ):
        slot = slots[(xz // 4) * 8 + (xz % 4) * 2 + half]
        for y in range(YC):
            found = facet_ref[0, jnp.maximum(slot, 0), offset + y]
            facet = jnp.where(slot >= 0, found, 0)
            axis = lax.shift_right_logical(jnp.maximum(facet - 1, 0), 1)
            bit = jnp.where(facet > 0, lax.shift_right_logical(64, axis), 0)
            want = jnp.where((facet & 1) == 1, 0, bit)
            image = jnp.where((lane & bit) == want, lane ^ bit, lane)
            at = y * TILE + xz * 8
            image_ref[at : at + 8, :] = image
            first_ref[at : at + 8, :] = taken(place_in, image)


def lane_k(rows):
    return lanes(rows).astype(jnp.float32)


def natural(own, octet, xz, half):
    start = own * 640 + octet * 128 + xz // 4 * 8 + half * 4 + xz % 4
    return pl.ds(start, 8, stride=16)


def pack_kernel(x_hbm, s_hbm, x_ref, s_ref, sems):
    ins = [
        pltpu.make_async_copy(
            x_hbm.at[pl.ds(own * 1280, 1280)], x_ref.at[pl.ds(own * 1280, 1280)], sems.at[own]
        )
        for own in range(2)
    ]
    outs = [
        pltpu.make_async_copy(
            s_ref.at[pl.ds(half * SENT_IN // 2, SENT_IN // 2)],
            s_hbm.at[pl.ds(half * SENT_IN // 2, SENT_IN // 2)],
            sems.at[OWN + half],
        )
        for half in range(2)
    ]
    for copy in ins:
        copy.start()
    for half in range(2):
        for own in range(OWN):
            if half == 0 and own % 2 == 0:
                ins[own // 2].wait()
            rows = [
                x_ref[natural(own, octet, xz, half), :] for octet in range(OCTS) for xz in range(XZ)
            ]
            for pair in range(2):
                t = jnp.concatenate(rows[pair * 16 : (pair + 1) * 16], axis=0).T
                for jj in range(16):
                    at = SNAKE[half * 16 + jj] * MSG_IN + pair * 32 + own * YC
                    s_ref[at : at + YC, :] = t[jj * YC : (jj + 1) * YC]
            rest = jnp.concatenate(rows[32:], axis=0)
            t = jnp.concatenate([rest, pltpu.roll(rest, 124, 1)], axis=0).T
            for jj in range(16):
                at = SNAKE[half * 16 + jj] * MSG_IN + 64 + own * 4
                s_ref[at : at + 4, :] = t[jj * YC : jj * YC + 4]
        outs[half].start()
    for copy in outs:
        copy.wait()


def side(y):
    return y if y < 2 else y - 4


def store_edges(e_ref, ya_ref, yb_ref):
    pos = (lanes(TILE) & 32) == 0
    for octet in range(OCTS):
        at = octet * TILE
        row = lambda y: e_ref[side(y) * ROW + at : side(y) * ROW + at + TILE, :]
        ya_ref[at : at + TILE, :] = jnp.where(pos, row(6), pltpu.roll(row(7), 32, 1))
        yb_ref[at : at + TILE, :] = jnp.where(pos, pltpu.roll(row(1), 96, 1), row(0))


def store_faces(at, ay, low, a_ref, b_ref):
    e0, r1 = ay[:32], pltpu.roll(ay[32:], 64, 1)
    a_ref[pl.ds(at, 32), :] = jnp.where(low, e0, r1)
    b_ref[pl.ds(at, 32), :] = jnp.where(low, r1, e0)


def spread_kernel(r_ref, first_ref, coef_ref, e_ref, ya_ref, yb_ref, ay_ref, a_ref, b_ref, f_ref):
    for y in range(YC):
        for pair in range(2):
            t = jnp.concatenate(
                [
                    r_ref[pl.ds(pair * 32 + own * YC + y, SRC, stride=MSG_IN), :]
                    for own in range(OWN)
                ],
                axis=0,
            ).T
            at = y * ROW + pair * 128
            f_ref[at : at + 128, :] = t
    for y in range(4):
        t = jnp.concatenate(
            [r_ref[pl.ds(64 + own * 4 + y, SRC, stride=MSG_IN), :] for own in range(OWN)], axis=0
        ).T
        f_ref[y * ROW + 256 : y * ROW + 320, :] = t[:TILE]
        f_ref[(y + 4) * ROW + 256 : (y + 4) * ROW + 320, :] = t[TILE:]
    for y in range(YC):
        for xz in range(XZ):
            index = first_ref[y * TILE + xz * 8 : y * TILE + xz * 8 + 8, :]
            for octet in range(OCTS):
                at = octet * TILE + xz * 8
                e = taken(f_ref[y * ROW + at : y * ROW + at + 8, :], index)
                if 2 <= y < 6:
                    f_ref[y * ROW + at : y * ROW + at + 8, :] = e
                else:
                    e_ref[side(y) * ROW + at : side(y) * ROW + at + 8, :] = e
    store_edges(e_ref, ya_ref, yb_ref)
    sweep_inner(e_ref, f_ref, 0, coef_ref, ay_ref, a_ref, b_ref)


def y_coefs(coef_ref, octet):
    at = 3 * BANDS + octet * 8
    return [tiled(coef_ref[at + k * BANDS : at + k * BANDS + 8, :], XZ) for k in range(3)]


def row_of(y, e_ref, mid_ref, first, at):
    start = (y - first if 2 <= y < 6 else side(y)) * ROW + at
    return (mid_ref if 2 <= y < 6 else e_ref)[start : start + TILE, :]


def sweep_inner(e_ref, mid_ref, first, coef_ref, ay_ref, a_ref, b_ref):
    low = lanes(32) < 64
    pos = (lanes(TILE) & 32) == 0
    for octet in range(OCTS):
        y0, y1, y2 = y_coefs(coef_ref, octet)
        for k in range(YC - 2):
            at = octet * TILE
            far, near, here = (row_of(k + j, e_ref, mid_ref, first, at) for j in range(3))
            ay = y0 * jnp.where(pos, here, far) + y1 * near + y2 * jnp.where(pos, far, here)
            ay_ref[k * ROW + at : k * ROW + at + TILE, :] = ay
            store_faces(k * FACE + octet * 32, ay, low, a_ref, b_ref)


def outer_kernel(e_ref, ml_ref, mr_ref, coef_ref, ay_ref, a_ref, b_ref):
    low = lanes(32) < 64
    pos = (lanes(TILE) & 32) == 0
    for octet in range(OCTS):
        y0, y1, y2 = y_coefs(coef_ref, octet)
        at = octet * TILE
        row = lambda y: e_ref[side(y) * ROW + at : side(y) * ROW + at + TILE, :]
        ml = ml_ref[at : at + TILE, :]
        mr = mr_ref[at : at + TILE, :]
        h0 = jnp.where(pos, ml, mr)
        h1 = jnp.where(pos, pltpu.roll(ml, 96, 1), pltpu.roll(mr, 32, 1))
        e0, e7 = row(0), row(7)
        ay0 = y0 * jnp.where(pos, e0, row(6)) + y1 * jnp.where(pos, h1, e7) + y2 * h0
        ay1 = y0 * jnp.where(pos, row(1), e7) + y1 * jnp.where(pos, e0, h0) + y2 * h1
        for k, ay in enumerate((ay0, ay1)):
            ay_ref[k * ROW + at : k * ROW + at + TILE, :] = ay
            store_faces(k * FACE + octet * 32, ay, low, a_ref, b_ref)


def expm1(q):
    small = q * (1.0 + q * (1 / 2) * (1.0 + q * (1 / 3) * (1.0 + q * (1 / 4) * (
        1.0 + q * (1 / 5) * (1.0 + q * (1 / 6))))))
    return jnp.where(q < 0.25, small, jnp.exp(q) - 1.0)


def sweep_xz(count, ay_ref, ml_ref, mr_ref, coef_ref, srcw_ref, mv_ref, acc_ref):
    lane = lanes(8)
    low = lane < 64
    pos_z = (lane & 16) == 0
    acc_ref[...] = jnp.zeros_like(acc_ref)

    for octet in range(OCTS):

        def at(pitch, offset):
            return pl.ds(octet * pitch + offset, 8)

        x0, x1, x2, z0, z1, z2 = (coef_ref[at(8, k * BANDS), :] for k in (0, 1, 2, 6, 7, 8))
        weight = srcw_ref[at(8, 0), :]
        for row in range(count):
            swept = [[], []]
            for z in range(4):
                e0 = ay_ref[at(TILE, row * ROW + z * 8), :]
                e1 = ay_ref[at(TILE, row * ROW + (4 + z) * 8), :]
                ml = ml_ref[at(32, row * FACE + z * 8), :]
                mr = mr_ref[at(32, row * FACE + z * 8), :]
                g0 = jnp.where(low, ml, mr)
                g1 = pltpu.roll(jnp.where(low, mr, ml), 64, 1)
                swept[0].append(x0 * e0 + x1 * jnp.where(low, g1, e1) + x2 * g0)
                swept[1].append(x0 * e1 + x1 * jnp.where(low, e0, g0) + x2 * g1)
            for x in range(2):
                ax = swept[x]
                for z in range(4):
                    near = jnp.where(pos_z, ax[(z + 3) % 4], ax[(z + 1) % 4])
                    mv = z0 * ax[z] + z1 * near + z2 * ax[(z + 2) % 4]
                    xz = x * 4 + z
                    mv_ref[at(TILE, row * ROW + xz * 8), :] = mv
                    cell = (row * XZ + xz) * 8
                    acc_ref[cell : cell + 8, :] += weight * mv
    return acc_ref[...].reshape(count * XZ, 8, DIRS).sum(axis=1)


def keep_moved(ys, row, cols_ref, index_of, e_ref):
    keep = jnp.broadcast_to(1.0 - cols_ref[:, 1:2], (BANDS, DIRS))
    pos = (lanes(8) & 32) == 0
    for i, y in enumerate(ys):
        for xz in range(XZ):
            index = index_of(y, xz)
            for octet in range(OCTS):
                at = octet * TILE + xz * 8
                moved = jnp.where(pos, row(y, at), row((y + 2) % YC, at))
                out = i * ROW + at
                e_ref[out : out + 8, :] = taken(keep[octet * 8 : (octet + 1) * 8] * moved, index)


def index_from(index_ref):
    if index_ref.shape[0] == 8:
        index = index_ref[...]
        return lambda y, xz: index
    return lambda y, xz: index_ref[y * TILE + xz * 8 : y * TILE + xz * 8 + 8, :]


def mid_kernel(
    ay_ref, ml_ref, mr_ref, coef_ref, srcw_ref, cols_ref, index_ref,
    mv_ref, sums_ref, e_ref, t_ref, acc_ref,
):
    sums = sweep_xz(YC - 2, ay_ref, ml_ref, mr_ref, coef_ref, srcw_ref, mv_ref, acc_ref)
    sums_ref[...] = sums
    row = lambda k, at: mv_ref[(k - 2) * ROW + at : (k - 2) * ROW + at + 8, :]
    temp, eq = heat_of(sums[:32], sums[16:], cols_ref)
    t_ref[...] = temp
    keep_moved((2, 3, 4, 5), row, cols_ref, index_from(index_ref), e_ref)
    add_heat(eq, e_ref)


def heat_of(here, turned, cols_ref):
    per_cell = jnp.where((lanes(32) & 32) == 0, here, turned)
    source = nt_dot(jnp.ones((8, DIRS), jnp.float32), per_cell)[0:1, :]
    relax = cols_ref[:, 1:2]
    heat = cols_ref[:, 2:3]
    pulse = cols_ref[:, 3:4]
    speed = relax * heat
    temp = jnp.ones((1, 32), jnp.float32)
    for _ in range(NEWTON):
        per_temp = 1.0 / temp
        q = pulse * per_temp
        surplus = expm1(q)
        inverse = 1.0 / surplus
        part = speed * inverse
        mismatch = jnp.sum(part, axis=0, keepdims=True) - source
        slope = jnp.sum(part * q * ((surplus + 1.0) * inverse), axis=0, keepdims=True) * per_temp
        temp = jnp.clip(temp - mismatch / slope, 0.5 * temp, 2.0 * temp)
    return temp, speed / expm1(pulse * (1.0 / temp))


def add_heat(eq, e_ref):
    for i in range(4):
        for octet in range(OCTS):
            at = i * ROW + octet * TILE
            e_ref[at : at + TILE, :] += jnp.concatenate(
                [
                    jnp.broadcast_to(
                        eq[octet * 8 : (octet + 1) * 8, i * XZ + xz : i * XZ + xz + 1], (8, DIRS)
                    )
                    for xz in range(XZ)
                ],
                axis=0,
            )


def finish_sides(
    mvi_ref, sums_ref, ayo_ref, mlo_ref, mro_ref, coef_ref, srcw_ref, cols_ref, index_ref,
    e_ref, mvo_ref, acc_ref,
):
    outer = sweep_xz(2, ayo_ref, mlo_ref, mro_ref, coef_ref, srcw_ref, mvo_ref, acc_ref)

    def row(k, at):
        return mvo_ref[k * ROW + at : k * ROW + at + 8, :] if k < 2 else mvi_ref[
            (k - 2) * ROW + at : (k - 2) * ROW + at + 8, :
        ]

    temp, eq = heat_of(
        jnp.concatenate([outer, sums_ref[32:, :]], axis=0),
        jnp.concatenate([sums_ref[:16, :], outer], axis=0),
        cols_ref,
    )
    keep_moved((0, 1, 6, 7), row, cols_ref, index_from(index_ref), e_ref)
    add_heat(eq, e_ref)
    return temp


def step_kernel(
    mvi_ref, sums_ref, mid_ref, tmid_ref, ayo_ref, mlo_ref, mro_ref, coef_ref, srcw_ref, cols_ref,
    image_ref, e_ref, ya_ref, yb_ref, ay_ref, a_ref, b_ref, mvo_ref, acc_ref,
):
    finish_sides(
        mvi_ref, sums_ref, ayo_ref, mlo_ref, mro_ref, coef_ref, srcw_ref, cols_ref, image_ref,
        e_ref, mvo_ref, acc_ref,
    )
    store_edges(e_ref, ya_ref, yb_ref)
    sweep_inner(e_ref, mid_ref, 2, coef_ref, ay_ref, a_ref, b_ref)


def last_kernel(
    mvi_ref, sums_ref, mid_ref, tmid_ref, ayo_ref, mlo_ref, mro_ref, coef_ref, srcw_ref, cols_ref,
    back_ref, s_ref, mvo_ref, acc_ref, e_ref,
):
    temp = finish_sides(
        mvi_ref, sums_ref, ayo_ref, mlo_ref, mro_ref, coef_ref, srcw_ref, cols_ref, back_ref,
        e_ref, mvo_ref, acc_ref,
    )
    temp = jnp.concatenate([temp, tmid_ref[...]], axis=1)
    wide = jnp.concatenate([temp, jnp.zeros((1, DIRS - 64), jnp.float32)], axis=1)
    s_ref[pl.ds(80, SRC, stride=MSG), :] = jnp.broadcast_to(wide, (SRC, DIRS))
    for y in range(YC):
        for pair in range(2):
            t = jnp.concatenate(
                [row_of(y, e_ref, mid_ref, 2, pair * 128 + part * TILE) for part in range(2)],
                axis=0,
            ).T
            for own in range(OWN):
                s_ref[pl.ds(pair * 32 + own * YC + y, SRC, stride=MSG), :] = t[
                    own * SRC : (own + 1) * SRC
                ]
    for y in range(4):
        t = jnp.concatenate(
            [row_of(k, e_ref, mid_ref, 2, 256) for k in (y, y + 4)], axis=0
        ).T
        for own in range(OWN):
            s_ref[pl.ds(64 + own * 4 + y, SRC, stride=MSG), :] = t[own * SRC : (own + 1) * SRC]


def unpack_kernel(r_ref, x_hbm, t_ref, x_ref, sems):
    lower = (lanes(TILE) & 4) == 0
    copies = []
    for own in range(OWN):
        for half in range(2):
            rows = []
            for pair in range(2):
                tiles = []
                for jj in range(16):
                    at = SNAKE[half * 16 + jj] * MSG + pair * 32 + own * YC
                    tiles.append(r_ref[at : at + YC, :])
                rows.append(jnp.concatenate(tiles, axis=0).T)
            tiles = []
            for jj in range(16):
                at = SNAKE[half * 16 + jj] * MSG + 64 + own * 4
                four = r_ref[at : at + 4, :]
                tiles += [four, four]
            t = jnp.concatenate(tiles, axis=0).T
            rows.append(jnp.where(lower, t[:TILE], t[TILE:]))
            for octet in range(OCTS):
                for xz in range(XZ):
                    at = octet % 2 * TILE + xz * 8
                    x_ref[natural(own, octet, xz, half), :] = rows[octet // 2][at : at + 8]
        part = pl.ds(own * 640, 640)
        copies.append(pltpu.make_async_copy(x_ref.at[part], x_hbm.at[part], sems.at[own]))
        copies[own].start()
    lane = lanes(16)
    here = lane // 8 == chunk_of(lax.broadcasted_iota(jnp.int32, (16, DIRS), 0))
    y = lane % 8
    place = jnp.where(y < 2, y, jnp.where(y < 6, y + 2, y - 4))
    for half in range(2):
        temps = r_ref[pl.ds(half * 16 * MSG + 80, 16, stride=MSG), :]
        for xz in range(XZ):
            spread = jnp.where(here, taken(temps, place * XZ + xz), 0.0)
            t_ref[xz // 4, xz % 4 : xz % 4 + 1, half * 128 : (half + 1) * 128] = jnp.sum(
                spread, axis=0, keepdims=True
            )
    for copy in copies:
        copy.wait()


def f32(*shape):
    return pltpu.VMEM(shape, jnp.float32)


VMEM = pl.BlockSpec(memory_space=pltpu.VMEM)
SMEM = pl.BlockSpec(memory_space=pltpu.SMEM)
ANY = pl.BlockSpec(memory_space=pltpu.HBM)


def call(kernel, in_specs, out_shape, scratch=(), out_specs=None, name=None, cost=None):
    if out_specs is None:
        out_specs = tuple(VMEM for _ in out_shape) if isinstance(out_shape, tuple) else VMEM

    def run(*args):
        args = [
            a if s is SMEM else pltpu.with_memory_space_constraint(a, s.memory_space)
            for a, s in zip(args, in_specs)
        ]
        return pl.pallas_call(
            kernel,
            in_specs=in_specs,
            out_specs=out_specs,
            out_shape=out_shape,
            scratch_shapes=list(scratch),
            compiler_params=pltpu.CompilerParams(vmem_limit_bytes=24 << 20),
            cost_estimate=cost,
            name=name,
        )(*args)

    return run


OUTER_COST = pl.CostEstimate(flops=2_000_000_000, transcendentals=0, bytes_accessed=0)
MID_COST = pl.CostEstimate(flops=7_000_000, transcendentals=0, bytes_accessed=4_000_000)


def exchanged(messages):
    whole = messages.reshape(SRC, 1, -1)
    return lax.all_to_all(whole, "dir", 0, 0, tiled=True).reshape(messages.shape)


def both_ways(up, down, axis):
    order = SNAKE if axis == "dir" else list(range(lax.axis_size(axis)))
    right = list(zip(order, order[1:] + order[:1]))
    left = [(j, i) for i, j in right]
    return lax.ppermute(up, axis, right), lax.ppermute(down, axis, left)


def on_device(
    phonon_heat_density,
    directions,
    quad_weight,
    mirror,
    band_courant,
    relax_rate,
    mode_heat_magnitude,
    mode_pulsation,
    wall_blocks,
    wall_count,
    wall_facet,
):
    own = lax.axis_index("dir").astype(jnp.int32).reshape(1)
    bands = jnp.stack([band_courant, relax_rate, mode_heat_magnitude, mode_pulsation])
    bands = jnp.concatenate([bands, jnp.zeros_like(bands)])
    x2 = phonon_heat_density.reshape(OWN, BANDS, 2, 4, 2, 128)
    x2 = x2.transpose(0, 1, 2, 4, 3, 5).reshape(2560, 128)
    whole = pltpu.VMEM((2560, 128), jnp.float32)
    packed = call(
        pack_kernel, [ANY], jax.ShapeDtypeStruct((SENT_IN, 128), jnp.float32),
        [whole, whole, pltpu.SemaphoreType.DMA((OWN + 2,))], ANY,
        name="pack",
    )(x2)
    table = pltpu.VMEM((YC * TILE, 128), jnp.int32)
    coef, srcw, cols, first, image, place = call(
        tables_kernel,
        [VMEM] * 4 + [SMEM] * 4,
        (f32(360, 128), f32(40, 128), f32(40, 8), table, table, pltpu.VMEM((8, 128), jnp.int32)),
        [pltpu.VMEM((8, 128), jnp.float32), pltpu.VMEM((128, 128), jnp.float32),
         pltpu.VMEM((128, 128), jnp.float32), pltpu.SMEM((16,), jnp.int32)],
        name="tables",
    )(directions, quad_weight.reshape(1, 128), mirror, bands, own, wall_blocks, wall_count,
      wall_facet)
    met = exchanged(packed)
    sides = f32(4 * ROW, 128)
    edge = f32(ROW, 128)
    swept_inner = (f32(6 * ROW, 128), f32(6 * FACE, 128), f32(6 * FACE, 128))
    e, ya, yb, ayi, a, b = call(
        spread_kernel, [VMEM] * 3, (sides, edge, edge, *swept_inner), [whole], name="spread"
    )(met, first, coef)
    work = [pltpu.VMEM((2 * ROW, 128), jnp.float32), pltpu.VMEM((128, 128), jnp.float32)]
    for step in range(2):
        yl, yr = both_ways(ya, yb, "dir")
        mli, mri = both_ways(a, b, "space")
        ayo, a, b = call(
            outer_kernel, [VMEM] * 4, (f32(2 * ROW, 128), edge, edge), name="outer", cost=OUTER_COST
        )(e, yl, yr, coef)
        mlo, mro = both_ways(a, b, "space")
        index = place if step else image
        moved, sums, mid, tmid = call(
            mid_kernel, [VMEM] * 7, (f32(6 * ROW, 128), f32(48, 128), sides, f32(1, 32)),
            [pltpu.VMEM((384, 128), jnp.float32)], name="mid", cost=MID_COST,
        )(ayi, mli, mri, coef, srcw, cols, index)
        swept = (moved, sums, mid, tmid, ayo, mlo, mro, coef, srcw, cols, index)
        if step == 0:
            e, ya, yb, ayi, a, b = call(
                step_kernel, [VMEM] * 11, (sides, edge, edge, *swept_inner), work, name="step"
            )(*swept)
        else:
            out = call(
                last_kernel, [VMEM] * 11, f32(SENT, 128),
                work + [pltpu.VMEM((4 * ROW, 128), jnp.float32)], name="last"
            )(*swept)
    x2, temp = call(
        unpack_kernel,
        [VMEM],
        (jax.ShapeDtypeStruct((2560, 128), jnp.float32),
         jax.ShapeDtypeStruct((2, 4, 256), jnp.float32)),
        [whole, pltpu.SemaphoreType.DMA((OWN,))],
        (ANY, VMEM),
        name="unpack",
    )(exchanged(out))
    energy = x2.reshape(OWN, BANDS, 2, 2, 4, 128).transpose(0, 1, 2, 4, 3, 5)
    return energy.reshape(phonon_heat_density.shape), temp


def solution(mesh):
    in_specs = (
        P("dir", None, "space", None, None),
        P(),
        P(),
        P(),
        P(),
        P(),
        P(),
        P(),
        P("space", None),
        P("space"),
        P("space", None, None),
    )
    out_specs = (P("dir", None, "space", None, None), P("space", None, None))
    return jax.shard_map(
        on_device, mesh=mesh, in_specs=in_specs, out_specs=out_specs, check_vma=False
    )
```
